32 devices in a mesh: tm: 8 (over z, core), space: 4 (over y, x).
Axes of the slice: x: 2, y: 2, z: 4, core: 2. Of those that a mesh axis runs over, the one named last changes fastest.
Arguments:
- spectrum: float32 [2048], P('space'), may hold values from 4 to 64
- coupling: float32 [64, 2048], P('tm', 'space'), may hold values from 0 to 1, as said below
- spatial_basis: bfloat16 [2048, 2048], P(None, 'space'), may hold values from -0.125 to 0.125
- noise_keys: int32 [64], replicated, may hold values from 0 to 16777215
- noise_counters: int32 [64], replicated, may hold values from 0 to 1048575
Outputs:
- samples: float32 [2048, 4096], P('space', 'tm')
The draws below stay inside these ranges and needn't reach their ends.
Inputs may be any that keep to these rules, and one draw needn't show every extreme that they name: `coupling`: every entry lies strictly between 0 and 1.
All inputs are finite; a program needn't handle non-finite values.
Results may differ from the reference program's by a relative error of at most 0.015.
Values may be sent and summed in bfloat16 or wider, within the bound.
No kernel may reach another device: no remote copies, remote signals or barrier semaphores. Data moves between devices by JAX's collectives and lax.ppermute only.
A program may use at most 64 MiB of HBM per device.

```python
import math
import jax
import jax.numpy as jnp
from jax import lax

NODES = 2048
VECS = 64
STEPS_DEV = 8
STEPS = 64


def draw_coupling(key, part):
    streams = jax.random.split(jax.random.fold_in(key, 7), 6)
    slow_share = 0.5
    chosen = jax.random.uniform(streams[0], (NODES,), jnp.float32) < slow_share
    slow_rate = jax.random.uniform(streams[1], (NODES,), jnp.float32, 0.03, 0.1) / STEPS
    fast_rate = jax.random.uniform(streams[2], (NODES,), jnp.float32, 0.045, 0.08)
    baseline_rate = jnp.where(chosen, slow_rate, fast_rate)
    block_cholesky_factor = jnp.exp(0.6931471805599453 * jax.random.uniform(streams[3], (STEPS // STEPS_DEV, 1), jnp.float32))
    block_cholesky_factor = jnp.repeat(block_cholesky_factor, STEPS_DEV, axis=0)
    diagonal_nudge = jax.random.uniform(streams[4], (STEPS, NODES), jnp.float32, 0.7, 1.3)
    places = jax.random.randint(streams[5], (3,), 1, STEPS)
    match_count = jnp.any(jnp.arange(STEPS)[:, None] == places[None, :], axis=1)
    noise_surge = jnp.where(match_count, 0.8, 1.0).astype(jnp.float32)[:, None]
    return (jnp.exp(-baseline_rate[None, :] * block_cholesky_factor * diagonal_nudge) * noise_surge).astype(jnp.float32)


def place_ends(drawn, stream_key, smallest, largest):
    extent = drawn.shape
    place = [jax.random.randint(jax.random.fold_in(stream_key, axis), (), 0, extent[axis]) for axis in range(len(extent))]
    drawn = drawn.at[tuple(place)].set(smallest)
    longest = extent.index(max(extent))
    place[longest] = (place[longest] + 1) % extent[longest]
    return drawn.at[tuple(place)].set(largest)


def steps_of(stream_key, shape, shards, smallest, high):
    def one(position, shards_of):
        draws = jax.random.uniform(jax.random.fold_in(jax.random.fold_in(stream_key, 6), position), (shards_of,), jnp.float32, smallest / len(shards), high / len(shards))
        return jnp.repeat(jnp.exp(draws), shape[position] // shards_of).reshape((-1,) + (1,) * (len(shape) - position - 1))

    factor_of = one(*shards[0])
    for cut in shards[1:]:
        factor_of = factor_of * one(*cut)
    return factor_of


def scatter_about(rng, shape, spread, most, cuts=(), kind=jnp.bfloat16):
    result = spread * jax.random.normal(rng, shape, jnp.float32)
    if cuts:
        result = result * steps_of(rng, shape, cuts, -0.22, 0.18)
    return jnp.clip(result, -most, most).astype(kind)


def setup_inputs(seed: int = 0) -> dict:
    arg_keys = jax.random.split(jax.random.key(seed), 6)
    spectrum = jnp.clip(jnp.exp(math.log(64.0) - 2.7725887 * jax.random.uniform(arg_keys[0], (NODES,), jnp.float32) ** steps_of(arg_keys[0], (NODES,), ((0, 4),), -0.2, 0.2)), 4.0, 64.0)
    coupling = draw_coupling(jax.random.fold_in(arg_keys[5], 71), 0)
    spatial_basis = scatter_about(arg_keys[2], (NODES, NODES), NODES ** -0.5, 0.125, ((1, 4),))
    noise_keys = place_ends(jax.random.randint(arg_keys[3], (VECS,), 0, 16777216), jax.random.fold_in(arg_keys[3], 1), 0, 16777215).astype(jnp.int32)
    noise_counters = place_ends(jax.random.randint(arg_keys[4], (VECS,), 0, 1048576), jax.random.fold_in(arg_keys[4], 1), 0, 1048575).astype(jnp.int32)
    return dict(spectrum=spectrum, coupling=coupling, spatial_basis=spatial_basis, noise_keys=noise_keys, noise_counters=noise_counters)


def mix_bits(state):
    state = state ^ lax.shift_right_logical(state, jnp.int32(16))
    state = state * jnp.int32(-2048144789)
    state = state ^ lax.shift_right_logical(state, jnp.int32(13))
    state = state * jnp.int32(-1028477387)
    state = state ^ lax.shift_right_logical(state, jnp.int32(16))
    return state

def unit_value(state):
    return (lax.shift_right_logical(state, jnp.int32(8)).astype(jnp.float32) + 0.5) * (1.0 / 16777216.0)

def noise_block(noise_keys, noise_counters, step_ids, mode_ids):
    seeded = noise_keys[None, :, None] * jnp.int32(668265261)
    seeded = seeded + (noise_counters[None, :, None] + step_ids[:, None, None]) * jnp.int32(374761393)
    seeded = seeded + mode_ids[None, None, :] * jnp.int32(-1640531535)
    first = mix_bits(seeded)
    second = mix_bits(first + jnp.int32(1013904223))
    radius = jnp.sqrt(-2.0 * jnp.log(unit_value(first)))
    return radius * jnp.cos(6.283185307179586 * unit_value(second))

def reference(spectrum, coupling, spatial_basis, noise_keys, noise_counters):
    step_ids = jnp.arange(STEPS, dtype=jnp.int32)
    mode_ids = jnp.arange(NODES, dtype=jnp.int32)
    noise = noise_block(noise_keys, noise_counters, step_ids, mode_ids)
    diag_part = spectrum[None, :] * (1.0 + coupling * coupling)
    product_part = spectrum[None, :] * coupling
    couple_square = product_part * product_part

    def forward(inverse_matrix, inputs):
        current_diagonal, couple_now = inputs
        pivot = current_diagonal - couple_now * inverse_matrix
        return (1.0 / pivot, pivot)
    _, pivots = lax.scan(forward, jnp.zeros((NODES,), jnp.float32), (diag_part, couple_square))
    scaled = noise / jnp.sqrt(pivots)[:, None, :]

    def backward(carry, inputs):
        scaled_now, pivot, coupling_now = inputs
        value = scaled_now + carry / pivot[None, :]
        return ((spectrum * coupling_now)[None, :] * value, value)
    _, mode_values = lax.scan(backward, jnp.zeros((VECS, NODES), jnp.float32), (scaled, pivots, coupling), reverse=True)
    rounded = mode_values.astype(jnp.bfloat16).reshape(STEPS * VECS, NODES)
    return jnp.dot(spatial_basis, rounded.T, preferred_element_type=jnp.float32)
```

```python
import functools

import jax
import jax.numpy as jnp
from jax import lax
from jax.experimental import pallas as pl
from jax.experimental.pallas import tpu as pltpu
from jax.sharding import PartitionSpec as P


F32 = jnp.float32
BF16 = jnp.bfloat16
VMEM = pl.BlockSpec(memory_space=pltpu.VMEM)
ANY = pl.BlockSpec(memory_space=pl.ANY)
LIMIT = pltpu.CompilerParams(vmem_limit_bytes=48 << 20)
SINE = (6.28318516, -41.34165503, 81.60100406, -76.54978208, 39.53670436)


def swap(x, axis, offset):
    count = lax.axis_size(axis)
    return lax.ppermute(x, axis, [(i, i ^ offset) for i in range(count)])


def split3(x):
    high = x.astype(BF16).astype(F32)
    rest = x - high
    middle = rest.astype(BF16).astype(F32)
    return high, middle, rest - middle


def mix_bits(state):
    state = state ^ lax.shift_right_logical(state, jnp.int32(16))
    state = state * jnp.int32(-2048144789)
    state = state ^ lax.shift_right_logical(state, jnp.int32(13))
    state = state * jnp.int32(-1028477387)
    return state ^ lax.shift_right_logical(state, jnp.int32(16))


def gaussian(seeded):
    first = mix_bits(seeded)
    second = mix_bits(first + jnp.int32(1013904223))
    unit = (lax.shift_right_logical(first, jnp.int32(8)).astype(F32) + 0.5) * (1.0 / 16777216.0)
    square = -2.0 * jnp.log(unit)
    radius = square * lax.rsqrt(jnp.maximum(square, 1e-30))
    turn = (lax.shift_right_arithmetic(second, jnp.int32(8)).astype(F32) + 0.5) * (1.0 / 16777216.0)
    w = 0.25 - jnp.abs(turn)
    z = w * w
    sine = SINE[4]
    for c in SINE[3::-1]:
        sine = sine * z + c
    return radius * (sine * w)


def pack_kernel(tm_axis, sp_axis, coup, other, spec, basis, *rest):
    *outs, zmsg, sems = rest
    me, sp = lax.axis_index(tm_axis), lax.axis_index(sp_axis)
    core = lax.rem(me, 2)
    rows = outs[0].shape[0] - 32
    copies = []
    for i, out in enumerate(outs):
        start = pl.multiple_of(((sp ^ (i + 1)) * 2 + core) * rows, rows)
        copies.append(
            pltpu.make_async_copy(basis.at[pl.ds(start, rows), :], out.at[pl.ds(0, rows), :], sems.at[i])
        )
        copies[-1].start()
    x = coup[...]
    parts = split3(x)
    tail = [jnp.concatenate(parts[:2], 0).astype(BF16)]
    row = lax.broadcasted_iota(jnp.int32, x.shape, 0)
    sparts = split3(spec[...])
    extra = jnp.zeros_like(x)
    for j in range(3):
        extra = jnp.where(row == j, sparts[j], extra)
    tail.append(jnp.concatenate([parts[2], extra], 0).astype(BF16))
    for out in outs:
        out[pl.ds(rows, 16), :] = tail[0]
        out[pl.ds(rows + 16, 16), :] = tail[1]

    def block(ref):
        product = square = total = None
        for t in range(ref.shape[0]):
            c = ref[pl.ds(t, 1), :]
            product = c if t == 0 else product * c
            square = c * c if t == 0 else square * (c * c)
            total = square if t == 0 else total + square
        return product, total

    mine, theirs = block(coup), block(other)
    first = core == 0
    table = jnp.zeros_like(x)
    for j in range(2):
        table = jnp.where(row == j, jnp.where(first, mine[j], theirs[j]), table)
        table = jnp.where(row == j + 2, jnp.where(first, theirs[j], mine[j]), table)
    zmsg[...] = table
    for copy in copies:
        copy.wait()


def noise_kernel(tm_axis, sp_axis, offsets, keys, counters, *rest):
    *outs, base = rest
    steps, vecs, modes = outs[0].shape
    first_step = lax.axis_index(tm_axis) * steps
    sp = lax.axis_index(sp_axis)
    diagonal = lax.broadcasted_iota(jnp.int32, (vecs, vecs), 0) == lax.broadcasted_iota(
        jnp.int32, (vecs, vecs), 1
    )

    def column(ref):
        row = jnp.broadcast_to(ref[...].astype(F32), (vecs, vecs))
        return jnp.sum(jnp.where(diagonal, row, 0.0), axis=1, keepdims=True).astype(jnp.int32)

    start = column(keys) * jnp.int32(668265261) + (column(counters) + first_step) * jnp.int32(374761393)
    base[...] = jnp.broadcast_to(start, base.shape)
    group = 8
    for out, offset in zip(outs, offsets):
        ids = (sp ^ offset) * modes + lax.broadcasted_iota(jnp.int32, (1, modes), 1)
        lane = ids * jnp.int32(-1640531535)

        def step(t, _):
            shifted = lane + t * jnp.int32(374761393)
            for v in range(vecs // group):
                seeded = jnp.tile(base[pl.ds(v * group, group), :], (1, modes // 128)) + shifted
                out[t, pl.ds(v * group, group), :] = gaussian(seeded)
            return 0

        lax.fori_loop(0, steps, step, 0)


def chain(coup, spec, d_start, f_start):
    before, after = [], []
    square, total = None, None
    d_now = d_start
    for t in range(coup.shape[0]):
        c = coup[t : t + 1, :]
        square = c * c if t == 0 else square * (c * c)
        total = square if t == 0 else total + square
        before.append(d_now)
        d_now = d_start + f_start * total
        after.append(d_now)
    ratio = jnp.concatenate(before, 0) / jnp.concatenate(after, 0)
    return jnp.sqrt(ratio / spec), ratio


def offset_kernel(tm_axis, noise, coup, spec, zown, *rest):
    zin = rest[: len(rest) - 7]
    o_ref, wts, df, table, alpha_ref, beta_ref, _ = rest[len(zin) :]
    steps, vecs, modes = noise.shape
    me = lax.axis_index(tm_axis)
    chip = me // 2
    chips = len(zin) + 1
    table[chip] = zown[...]
    for e, ref in enumerate(zin):
        table[chip ^ (e + 1)] = ref[...]
    d_now = jnp.ones((1, modes), F32)
    f_now = jnp.ones((1, modes), F32)
    d_start, f_start = d_now, f_now
    own = jnp.zeros((1, modes), F32)
    other = jnp.zeros((1, modes), F32)
    row = lax.broadcasted_iota(jnp.int32, (8, modes), 0)
    for b in range(2 * chips):
        wts[b] = jnp.where(row == 0, own, jnp.where(row == 1, other, 0.0))
        product = table[b // 2, pl.ds(2 * (b % 2), 1), :]
        total = table[b // 2, pl.ds(2 * (b % 2) + 1, 1), :]
        d_start = jnp.where(me == b, d_now, d_start)
        f_start = jnp.where(me == b, f_now, f_start)
        d_next = d_now + f_now * total
        gain = product * d_now / d_next
        own = jnp.where(me == b, 1.0, own * gain)
        other = jnp.where((me ^ 1) == b, 1.0, other * gain)
        d_now, f_now = d_next, f_now * (product * product)
    df[...] = jnp.where(row == 0, d_start, jnp.where(row == 1, f_start, 0.0))
    c = coup[...]
    a, ratio = chain(c, spec[...], d_start, f_start)
    alpha_ref[...] = c * a
    beta_ref[...] = c * ratio
    group = 8

    def tile(v, _):
        at = pl.ds(pl.multiple_of(v * 2 * group, 2 * group), 2 * group)
        carry = jnp.zeros((2 * group, modes), F32)
        for t in range(steps - 1, -1, -1):
            carry = alpha_ref[pl.ds(t, 1), :] * noise[t, at, :] + beta_ref[pl.ds(t, 1), :] * carry
        o_ref[at, :] = carry.astype(BF16)
        return 0

    lax.fori_loop(0, vecs // (2 * group), tile, 0)


def combine_kernel(tm_axis, own, wts, *rest):
    *others, u_own, u_other = rest
    me = lax.axis_index(tm_axis)
    last = wts.shape[0] - 1
    w = wts[me]
    mine = jnp.zeros(u_own.shape, F32)
    theirs = w[1:2, :] * own[...].astype(F32)
    for e, ref in enumerate(others):
        w = wts[jnp.minimum(me + 2 * (e + 1), last)]
        x = ref[...].astype(F32)
        mine = mine + w[0:1, :] * x
        theirs = theirs + w[1:2, :] * x
    u_own[...] = mine
    u_other[...] = theirs.astype(BF16)


def carry_kernel(u_own, u_in, df, out):
    vecs, modes = u_own.shape
    out[pl.ds(0, vecs), :] = (u_own[...] + u_in[...].astype(F32)).astype(BF16)
    row = lax.broadcasted_iota(jnp.int32, (16, modes), 0)
    block = jnp.zeros((16, modes), F32)
    parts = split3(df[pl.ds(0, 1), :]) + split3(df[pl.ds(1, 1), :])
    for j, part in enumerate(parts):
        block = jnp.where(row == j, part, block)
    out[pl.ds(vecs, 16), :] = block.astype(BF16)


def final_kernel(tm_axis, sp_axis, count, coup, spec, basis, *rest):
    direct, rest = rest[: count - 1], rest[count - 1 :]
    swapped, rest = rest[: count - 1], rest[count - 1 :]
    noise, rest = rest[:count], rest[count:]
    carries, rest = rest[:count], rest[count:]
    out, lhs, rhs, tails, a_ref, ratio_ref, c_ref, sems = rest
    steps, vecs, modes = noise[0].shape
    me, sp = lax.axis_index(tm_axis), lax.axis_index(sp_axis)
    core = lax.rem(me, 2)
    rows = lhs.shape[0] // 2
    here = pl.ds(pl.multiple_of(core * rows, rows), rows)
    there = pl.ds(pl.multiple_of((1 - core) * rows, rows), rows)
    start = pl.multiple_of(sp * (2 * rows), 2 * rows)
    copies = [
        pltpu.make_async_copy(basis.at[pl.ds(start, 2 * rows), :], lhs.at[:, pl.ds(0, modes)], sems.at[0])
    ]
    for d in range(1, count):
        at = pl.ds(d * modes, modes)
        copies.append(
            pltpu.make_async_copy(direct[d - 1].at[pl.ds(0, rows), :], lhs.at[here, at], sems.at[3 * d])
        )
        copies.append(
            pltpu.make_async_copy(swapped[d - 1].at[pl.ds(0, rows), :], lhs.at[there, at], sems.at[3 * d + 1])
        )
    heads = [
        pltpu.make_async_copy(direct[d - 1].at[pl.ds(rows, 32), :], tails.at[d], sems.at[3 * d + 2])
        for d in range(1, count)
    ]
    for copy in heads + copies:
        copy.start()
    for copy in heads:
        copy.wait()
    for d in range(count):
        if d == 0:
            c, lam = coup[...], spec[...]
        else:
            upper = tails[d, pl.ds(0, 16), :].astype(F32)
            lower = tails[d, pl.ds(16, 16), :].astype(F32)
            c = upper[0:8] + upper[8:16] + lower[0:8]
            lam = lower[8:9] + lower[9:10] + lower[10:11]
        df = carries[d][pl.ds(vecs, 16), :].astype(F32)
        a, ratio = chain(c, lam, df[0:1] + df[1:2] + df[2:3], df[3:4] + df[4:5] + df[5:6])
        a_ref[...] = a
        ratio_ref[...] = ratio
        c_ref[...] = c

        def tile(v, _):
            at = pl.ds(pl.multiple_of(v * 16, 16), 16)
            carry = carries[d][at, :].astype(F32)
            for t in range(steps - 1, -1, -1):
                value = a_ref[pl.ds(t, 1), :] * noise[d][t, at, :] + ratio_ref[pl.ds(t, 1), :] * carry
                if t:
                    carry = c_ref[pl.ds(t, 1), :] * value
                rhs[pl.ds(pl.multiple_of(t * vecs + v * 16, 16), 16), pl.ds(d * modes, modes)] = value.astype(BF16)
            return 0

        lax.fori_loop(0, vecs // 16, tile, 0)
    for copy in copies:
        copy.wait()
    out[...] = lax.dot_general(
        lhs[...], rhs[...], (((1,), (1,)), ((), ())), preferred_element_type=F32
    )


def local(spectrum, coupling, spatial_basis, noise_keys, noise_counters):
    steps, modes = coupling.shape
    vecs = noise_keys.shape[0]
    tm, space = lax.axis_size("tm"), lax.axis_size("space")
    chips = tm // 2
    nodes_here = spatial_basis.shape[0] // space
    half = nodes_here // 2
    spec = spectrum.reshape(1, modes)
    keys, counters = noise_keys.reshape(1, vecs), noise_counters.reshape(1, vecs)
    row_block = jax.ShapeDtypeStruct((8, modes), F32)

    other = swap(coupling, "tm", 1)
    *messages, zmsg = pl.pallas_call(
        functools.partial(pack_kernel, "tm", "space"),
        out_shape=[jax.ShapeDtypeStruct((half + 32, modes), BF16)] * (space - 1) + [row_block],
        in_specs=[VMEM, VMEM, VMEM, ANY],
        out_specs=[VMEM] * space,
        scratch_shapes=[pltpu.SemaphoreType.DMA((space,))],
        compiler_params=LIMIT,
        name="pack",
    )(coupling, other, spec, spatial_basis)
    zin = [swap(zmsg, "tm", 2 * e) for e in range(1, chips)]
    direct = [swap(m, "space", d + 1) for d, m in enumerate(messages)]

    def noise_of(offsets, name):
        count = len(offsets) * steps * vecs * modes
        return pl.pallas_call(
            functools.partial(noise_kernel, "tm", "space", offsets),
            out_shape=[jax.ShapeDtypeStruct((steps, vecs, modes), F32)] * len(offsets),
            in_specs=[VMEM] * 2,
            out_specs=[VMEM] * len(offsets),
            scratch_shapes=[pltpu.VMEM((vecs, 128), jnp.int32)],
            compiler_params=LIMIT,
            cost_estimate=pl.CostEstimate(flops=count * 60, transcendentals=count * 2, bytes_accessed=count * 4),
            name=name,
        )(keys, counters)

    noise = list(noise_of((0,), "noise_own"))
    offset, weights, sums = pl.pallas_call(
        functools.partial(offset_kernel, "tm"),
        out_shape=[
            jax.ShapeDtypeStruct((vecs, modes), BF16),
            jax.ShapeDtypeStruct((tm, 8, modes), F32),
            row_block,
        ],
        in_specs=[VMEM] * (4 + len(zin)),
        out_specs=[VMEM] * 3,
        scratch_shapes=[
            pltpu.VMEM((chips, 8, modes), F32),
            pltpu.VMEM((steps, modes), F32),
            pltpu.VMEM((steps, modes), F32),
            pltpu.VMEM((8, 128), F32),
        ],
        compiler_params=LIMIT,
        name="offset",
    )(noise[0], coupling, spec, zmsg, *zin)
    later = [
        lax.ppermute(offset, "tm", [(i, i - 2 * e) for i in range(2 * e, tm)]) for e in range(1, chips)
    ]
    for d in range(1, space):
        noise += noise_of((d,), f"noise_{d}")
    swapped = [swap(m, "tm", 1) for m in direct]
    u_own, u_other = pl.pallas_call(
        functools.partial(combine_kernel, "tm"),
        out_shape=[jax.ShapeDtypeStruct((vecs, modes), F32), jax.ShapeDtypeStruct((vecs, modes), BF16)],
        in_specs=[VMEM] * (2 + len(later)),
        out_specs=[VMEM] * 2,
        compiler_params=LIMIT,
        name="combine",
    )(offset, weights, *later)
    carry = pl.pallas_call(
        carry_kernel,
        out_shape=jax.ShapeDtypeStruct((vecs + 16, modes), BF16),
        in_specs=[VMEM] * 3,
        out_specs=VMEM,
        compiler_params=LIMIT,
        name="carry",
    )(u_own, swap(u_other, "tm", 1), sums)
    carries = [carry] + [swap(carry, "space", d) for d in range(1, space)]
    return pl.pallas_call(
        functools.partial(final_kernel, "tm", "space", space),
        out_shape=jax.ShapeDtypeStruct((nodes_here, steps * vecs), F32),
        in_specs=[VMEM, VMEM, ANY] + [ANY] * (2 * (space - 1)) + [VMEM] * (2 * space),
        out_specs=VMEM,
        scratch_shapes=[
            pltpu.VMEM((nodes_here, space * modes), BF16),
            pltpu.VMEM((steps * vecs, space * modes), BF16),
            pltpu.VMEM((space, 32, modes), BF16),
            pltpu.VMEM((steps, modes), F32),
            pltpu.VMEM((steps, modes), F32),
            pltpu.VMEM((steps, modes), F32),
            pltpu.SemaphoreType.DMA((3 * space,)),
        ],
        compiler_params=LIMIT,
        name="final",
    )(coupling, spec, spatial_basis, *direct, *swapped, *noise, *carries)


def solution(mesh):
    in_specs = (P("space"), P("tm", "space"), P(None, "space"), P(), P())
    out_specs = P("space", "tm")
    return jax.shard_map(local, mesh=mesh, in_specs=in_specs, out_specs=out_specs, check_vma=False)
```

```python
import functools

import jax
import jax.numpy as jnp
from jax import lax
from jax.experimental import pallas as pl
from jax.experimental.pallas import tpu as pltpu
from jax.sharding import PartitionSpec as P


F32 = jnp.float32
BF16 = jnp.bfloat16
VMEM = pl.BlockSpec(memory_space=pltpu.VMEM)
ANY = pl.BlockSpec(memory_space=pl.ANY)
HBM = pl.BlockSpec(memory_space=pltpu.HBM)
LIMIT = pltpu.CompilerParams(vmem_limit_bytes=48 << 20)
SINE = (6.28318516, -41.34165503, 81.60100406, -76.54978208, 39.53670436)


def swap(x, axis, offset):
    count = lax.axis_size(axis)
    return lax.ppermute(x, axis, [(i, i ^ offset) for i in range(count)])


def send(x, axis, offset):
    count = lax.axis_size(axis)
    return lax.ppermute(x, axis, [(i, i - offset) for i in range(offset, count)])


def split3(x):
    high = x.astype(BF16).astype(F32)
    rest = x - high
    middle = rest.astype(BF16).astype(F32)
    return high, middle, rest - middle


def mix_bits(state):
    state = state ^ lax.shift_right_logical(state, jnp.int32(16))
    state = state * jnp.int32(-2048144789)
    state = state ^ lax.shift_right_logical(state, jnp.int32(13))
    state = state * jnp.int32(-1028477387)
    return state ^ lax.shift_right_logical(state, jnp.int32(16))


def gaussian(seeded):
    first = mix_bits(seeded)
    second = mix_bits(first + jnp.int32(1013904223))
    unit = (lax.shift_right_logical(first, jnp.int32(8)).astype(F32) + 0.5) * (1.0 / 16777216.0)
    square = -2.0 * jnp.log(unit)
    radius = square * lax.rsqrt(jnp.maximum(square, 1e-30))
    turn = (lax.shift_right_arithmetic(second, jnp.int32(8)).astype(F32) + 0.5) * (1.0 / 16777216.0)
    w = 0.25 - jnp.abs(turn)
    z = w * w
    sine = SINE[4]
    for c in SINE[3::-1]:
        sine = sine * z + c
    return radius * (sine * w)


def pack_kernel(tm_axis, sp_axis, coup, spec, basis, *rest):
    *outs, coup_out, spec_out, sems = rest
    me, sp = lax.axis_index(tm_axis), lax.axis_index(sp_axis)
    core = lax.rem(me, 2)
    rows = outs[0].shape[0] - 32
    small = [
        pltpu.make_async_copy(coup, coup_out, sems.at[len(outs)]),
        pltpu.make_async_copy(spec, spec_out, sems.at[len(outs) + 1]),
    ]
    large = []
    for i, out in enumerate(outs):
        start = pl.multiple_of(((sp ^ (i + 1)) * 2 + core) * rows, rows)
        large.append(
            pltpu.make_async_copy(basis.at[pl.ds(start, rows), :], out.at[pl.ds(0, rows), :], sems.at[i])
        )
    for copy in small + large:
        copy.start()
    for copy in small:
        copy.wait()
    x = coup_out[...]
    parts = split3(x)
    tail = [jnp.concatenate(parts[:2], 0).astype(BF16)]
    row = lax.broadcasted_iota(jnp.int32, x.shape, 0)
    sparts = split3(spec_out[...])
    extra = jnp.zeros_like(x)
    for j in range(3):
        extra = jnp.where(row == j, sparts[j], extra)
    tail.append(jnp.concatenate([parts[2], extra], 0).astype(BF16))
    for out in outs:
        out[pl.ds(rows, 16), :] = tail[0]
        out[pl.ds(rows + 16, 16), :] = tail[1]
    for copy in large:
        copy.wait()


def totals(ref):
    product = square = total = None
    for t in range(ref.shape[0]):
        c = ref[pl.ds(t, 1), :]
        product = c if t == 0 else product * c
        square = c * c if t == 0 else square * (c * c)
        total = square if t == 0 else total + square
    return product, total


def table_kernel(tm_axis, coup, other, out):
    first = lax.rem(lax.axis_index(tm_axis), 2) == 0
    mine, theirs = totals(coup), totals(other)
    row = lax.broadcasted_iota(jnp.int32, out.shape, 0)
    table = jnp.zeros(out.shape, F32)
    for j in range(2):
        table = jnp.where(row == j, jnp.where(first, mine[j], theirs[j]), table)
        table = jnp.where(row == j + 2, jnp.where(first, theirs[j], mine[j]), table)
    out[...] = table


def noise_kernel(tm_axis, sp_axis, blocks, extras, keys, counters, *rest):
    *outs, base = rest[extras:]
    outs = outs[: len(blocks)]
    steps, vecs, modes = outs[0].shape
    me, sp = lax.axis_index(tm_axis), lax.axis_index(sp_axis)
    diagonal = lax.broadcasted_iota(jnp.int32, (vecs, vecs), 0) == lax.broadcasted_iota(
        jnp.int32, (vecs, vecs), 1
    )

    def column(ref):
        row = jnp.broadcast_to(ref[...].astype(F32), (vecs, vecs))
        return jnp.sum(jnp.where(diagonal, row, 0.0), axis=1, keepdims=True).astype(jnp.int32)

    start = column(keys) * jnp.int32(668265261) + column(counters) * jnp.int32(374761393)
    base[...] = jnp.broadcast_to(start, base.shape)
    group = 8
    for out, (block, offset) in zip(outs, blocks):
        ids = (sp ^ offset) * modes + lax.broadcasted_iota(jnp.int32, (1, modes), 1)
        lane = ids * jnp.int32(-1640531535)
        first_step = (me ^ block) * steps

        def step(t, _):
            shifted = lane + (first_step + t) * jnp.int32(374761393)
            for v in range(vecs // group):
                seeded = jnp.tile(base[pl.ds(v * group, group), :], (1, modes // 128)) + shifted
                out[t, pl.ds(v * group, group), :] = gaussian(seeded)
            return 0

        lax.fori_loop(0, steps, step, 0)


def chain(coup, spec, d_start, f_start):
    before, after = [], []
    square, total = None, None
    d_now = d_start
    for t in range(coup.shape[0]):
        c = coup[t : t + 1, :]
        square = c * c if t == 0 else square * (c * c)
        total = square if t == 0 else total + square
        before.append(d_now)
        d_now = d_start + f_start * total
        after.append(d_now)
    ratio = jnp.concatenate(before, 0) / jnp.concatenate(after, 0)
    return jnp.sqrt(ratio / spec), ratio


def offset_kernel(tm_axis, noise_own, noise_other, coup, coup_other, spec, zown, *rest):
    zin = rest[:-10]
    o_ref, base_ref, wts, df, table, *coefs, tmp = rest[len(zin) :]
    steps, vecs, modes = noise_own.shape
    me = lax.axis_index(tm_axis)
    chip = me // 2
    first = lax.rem(me, 2) == 0
    chips = len(zin) + 1
    table[chip] = zown[...]
    for e, ref in enumerate(zin):
        table[chip ^ (e + 1)] = ref[...]
    one = jnp.ones((1, modes), F32)
    d_now, f_now = one, one
    starts = [one] * 4
    gains = [one] * 2
    weight = jnp.zeros((1, modes), F32)
    for b in range(chips):
        wts[b] = jnp.broadcast_to(weight, (8, modes))
        here = chip == b
        gain = one
        for half in range(2):
            product = table[b, pl.ds(2 * half, 1), :]
            total = table[b, pl.ds(2 * half + 1, 1), :]
            starts[2 * half] = jnp.where(here, d_now, starts[2 * half])
            starts[2 * half + 1] = jnp.where(here, f_now, starts[2 * half + 1])
            d_next = d_now + f_now * total
            part = product * d_now / d_next
            gains[half] = jnp.where(here, part, gains[half])
            gain = gain * part
            d_now, f_now = d_next, f_now * (product * product)
        weight = jnp.where(here, 1.0, weight * gain)
    row = lax.broadcasted_iota(jnp.int32, (8, modes), 0)
    mine = [jnp.where(first, starts[j], starts[2 + j]) for j in range(2)]
    theirs = [jnp.where(first, starts[2 + j], starts[j]) for j in range(2)]
    outer = jnp.where(first, gains[1], 1.0)
    df[...] = jnp.where(row == 0, mine[0], jnp.where(row == 1, mine[1], jnp.where(row == 2, outer, 0.0)))
    for j, (ref, sums) in enumerate(((coup, mine), (coup_other, theirs))):
        c = ref[...]
        a, ratio = chain(c, spec[...], *sums)
        coefs[2 * j][...] = c * a
        coefs[2 * j + 1][...] = c * ratio
    tmp[...] = jnp.broadcast_to(gains[0], tmp.shape)

    def tile(v, _):
        at = pl.ds(pl.multiple_of(v * 16, 16), 16)
        ends = []
        for j, noise in enumerate((noise_own, noise_other)):
            alpha, beta = coefs[2 * j], coefs[2 * j + 1]
            carry = jnp.zeros((16, modes), F32)
            for t in range(steps - 1, -1, -1):
                carry = alpha[pl.ds(t, 1), :] * noise[t, at, :] + beta[pl.ds(t, 1), :] * carry
            ends.append(carry)
        early = jnp.where(first, ends[0], ends[1])
        late = jnp.where(first, ends[1], ends[0])
        o_ref[at, :] = (early + tmp[pl.ds(0, 1), :] * late).astype(BF16)
        base_ref[at, :] = jnp.where(first, late, 0.0)
        return 0

    lax.fori_loop(0, vecs // 16, tile, 0)


def carry_kernel(tm_axis, extras, base, wts, df, *rest):
    others, out = rest[: -1 - extras], rest[-1]
    vecs, modes = base.shape
    chip = lax.axis_index(tm_axis) // 2
    last = wts.shape[0] - 1
    total = jnp.zeros(base.shape, F32)
    for e, ref in enumerate(others):
        total = total + wts[jnp.minimum(chip + (e + 1), last)][0:1, :] * ref[...].astype(F32)
    out[pl.ds(0, vecs), :] = (base[...] + df[pl.ds(2, 1), :] * total).astype(BF16)
    row = lax.broadcasted_iota(jnp.int32, (16, modes), 0)
    block = jnp.zeros((16, modes), F32)
    parts = split3(df[pl.ds(0, 1), :]) + split3(df[pl.ds(1, 1), :])
    for j, part in enumerate(parts):
        block = jnp.where(row == j, part, block)
    out[pl.ds(vecs, 16), :] = block.astype(BF16)


def values(noise, message, c, lam, coefs, rhs, column):
    steps, vecs, modes = noise.shape
    df = message[pl.ds(vecs, 16), :].astype(F32)
    a, ratio = chain(c, lam, df[0:1] + df[1:2] + df[2:3], df[3:4] + df[4:5] + df[5:6])
    a_ref, ratio_ref, c_ref = coefs
    a_ref[...] = a
    ratio_ref[...] = ratio
    c_ref[...] = c

    def tile(v, _):
        at = pl.ds(pl.multiple_of(v * 16, 16), 16)
        carry = message[at, :].astype(F32)
        for t in range(steps - 1, -1, -1):
            value = a_ref[pl.ds(t, 1), :] * noise[t, at, :] + ratio_ref[pl.ds(t, 1), :] * carry
            if t:
                carry = c_ref[pl.ds(t, 1), :] * value
            rhs[pl.ds(pl.multiple_of(t * vecs + v * 16, 16), 16), pl.ds(column, modes)] = value.astype(BF16)
        return 0

    lax.fori_loop(0, vecs // 16, tile, 0)


def product(lhs, rhs):
    return lax.dot_general(lhs[...], rhs[...], (((1,), (1,)), ((), ())), preferred_element_type=F32)


def own_kernel(sp_axis, coup, spec, basis, noise, message, out, lhs, rhs, *rest):
    *coefs, sem = rest
    rows = lhs.shape[0]
    start = pl.multiple_of(lax.axis_index(sp_axis) * rows, rows)
    copy = pltpu.make_async_copy(basis.at[pl.ds(start, rows), :], lhs, sem)
    copy.start()
    values(noise, message, coup[...], spec[...], coefs, rhs, 0)
    copy.wait()
    out[...] = product(lhs, rhs)


def final_kernel(tm_axis, count, partial, *rest):
    direct, rest = rest[:count], rest[count:]
    swapped, rest = rest[:count], rest[count:]
    noise, rest = rest[:count], rest[count:]
    messages, rest = rest[:count], rest[count:]
    out, lhs, rhs, tails, *coefs, sems = rest
    _, _, modes = noise[0].shape
    core = lax.rem(lax.axis_index(tm_axis), 2)
    rows = lhs.shape[0] // 2
    here = pl.ds(pl.multiple_of(core * rows, rows), rows)
    there = pl.ds(pl.multiple_of((1 - core) * rows, rows), rows)
    copies, heads = [], []
    for d in range(count):
        at = pl.ds(d * modes, modes)
        for j, (source, place) in enumerate(((direct[d], here), (swapped[d], there))):
            copies.append(
                pltpu.make_async_copy(source.at[pl.ds(0, rows), :], lhs.at[place, at], sems.at[3 * d + j])
            )
        heads.append(
            pltpu.make_async_copy(direct[d].at[pl.ds(rows, 32), :], tails.at[d], sems.at[3 * d + 2])
        )
    for copy in heads + copies:
        copy.start()
    for copy in heads:
        copy.wait()
    for d in range(count):
        upper = tails[d, pl.ds(0, 16), :].astype(F32)
        lower = tails[d, pl.ds(16, 16), :].astype(F32)
        c = upper[0:8] + upper[8:16] + lower[0:8]
        values(noise[d], messages[d], c, lower[8:9] + lower[9:10] + lower[10:11], coefs, rhs, d * modes)
    for copy in copies:
        copy.wait()
    out[...] = partial[...] + product(lhs, rhs)


def kernel_call(body, **options):
    return pl.pallas_call(body, **options)


def local(spectrum, coupling, spatial_basis, noise_keys, noise_counters):
    steps, modes = coupling.shape
    vecs = noise_keys.shape[0]
    tm, space = lax.axis_size("tm"), lax.axis_size("space")
    chips = tm // 2
    nodes_here = spatial_basis.shape[0] // space
    half = nodes_here // 2
    keys, counters = noise_keys.reshape(1, vecs), noise_counters.reshape(1, vecs)
    row_block = jax.ShapeDtypeStruct((steps, modes), F32)
    noise_block = jax.ShapeDtypeStruct((steps, vecs, modes), F32)
    coef_scratch = [pltpu.VMEM((steps, modes), F32)] * 3

    other = swap(coupling, "tm", 1)
    *messages, coup, spec = kernel_call(
        functools.partial(pack_kernel, "tm", "space"),
        out_shape=[jax.ShapeDtypeStruct((half + 32, modes), BF16)] * (space - 1)
        + [row_block, jax.ShapeDtypeStruct((1, modes), F32)],
        in_specs=[HBM] * 3,
        out_specs=[VMEM] * (space + 1),
        scratch_shapes=[pltpu.SemaphoreType.DMA((space + 1,))],
        compiler_params=LIMIT,
    )(*(pltpu.with_memory_space_constraint(x, pltpu.HBM) for x in (coupling, spectrum.reshape(1, modes), spatial_basis)))
    direct = [swap(m, "space", d + 1) for d, m in enumerate(messages)]
    table = kernel_call(
        functools.partial(table_kernel, "tm"),
        out_shape=row_block,
        in_specs=[VMEM] * 2,
        out_specs=VMEM,
        compiler_params=LIMIT,
    )(coup, other)
    zin = [swap(table, "tm", 2 * e) for e in range(1, chips)]

    def noise_of(blocks, after=(), through=()):
        count = len(blocks) * steps * vecs * modes
        extras = len(after) + len(through)
        return kernel_call(
            functools.partial(noise_kernel, "tm", "space", blocks, extras),
            out_shape=[noise_block] * len(blocks) + [jax.ShapeDtypeStruct(x.shape, x.dtype) for x in through],
            in_specs=[VMEM] * 2 + [ANY] * extras,
            out_specs=[VMEM] * len(blocks) + [ANY] * len(through),
            scratch_shapes=[pltpu.VMEM((vecs, 128), jnp.int32)],
            input_output_aliases={2 + len(after) + i: len(blocks) + i for i in range(len(through))},
            compiler_params=LIMIT,
            cost_estimate=pl.CostEstimate(flops=count * 60, transcendentals=count * 2, bytes_accessed=count * 4),
        )(keys, counters, *after, *through)

    own, paired = noise_of(((0, 0), (1, 0)))
    offset, base, weights, sums = kernel_call(
        functools.partial(offset_kernel, "tm"),
        out_shape=[
            jax.ShapeDtypeStruct((vecs, modes), BF16),
            jax.ShapeDtypeStruct((vecs, modes), F32),
            jax.ShapeDtypeStruct((chips, 8, modes), F32),
            jax.ShapeDtypeStruct((8, modes), F32),
        ],
        in_specs=[VMEM] * (6 + len(zin)),
        out_specs=[VMEM] * 4,
        scratch_shapes=[pltpu.VMEM((chips, 8, modes), F32)] + [pltpu.VMEM((steps, modes), F32)] * 5,
        compiler_params=LIMIT,
    )(own, paired, coup, other, spec, table, *zin)
    later = [send(offset, "tm", 2 * e) for e in range(1, chips)]
    middle = max(1, (space - 1) // 3)
    offsets = list(range(1, space))
    one, two, three = offsets[:middle], offsets[middle : 2 * middle], offsets[2 * middle :]
    noise = list(noise_of([(0, d) for d in one], after=(offset,)))
    if two:
        out = noise_of([(0, d) for d in two], after=(noise[-1],), through=direct)
        noise += out[: len(two)]
        direct = out[len(two) :]
    swapped = [swap(m, "tm", 1) for m in direct]
    carry = kernel_call(
        functools.partial(carry_kernel, "tm", 1),
        out_shape=jax.ShapeDtypeStruct((vecs + 16, modes), BF16),
        in_specs=[VMEM] * (3 + len(later)) + [ANY],
        out_specs=VMEM,
        compiler_params=LIMIT,
    )(base, weights, sums, *later, noise[-1])
    carries = [swap(carry, "space", d) for d in range(1, space)]
    if three:
        noise += noise_of([(0, d) for d in three], after=(carry,))
    flops = 2 * nodes_here * modes * steps * vecs
    partial = kernel_call(
        functools.partial(own_kernel, "space"),
        out_shape=jax.ShapeDtypeStruct((nodes_here, steps * vecs), F32),
        in_specs=[VMEM, VMEM, HBM, VMEM, VMEM],
        out_specs=VMEM,
        scratch_shapes=[pltpu.VMEM((nodes_here, modes), BF16), pltpu.VMEM((steps * vecs, modes), BF16)]
        + coef_scratch
        + [pltpu.SemaphoreType.DMA],
        compiler_params=LIMIT,
        cost_estimate=pl.CostEstimate(flops=flops, transcendentals=0, bytes_accessed=4 * steps * vecs * modes),
    )(coup, spec, spatial_basis, own, carry)
    return kernel_call(
        functools.partial(final_kernel, "tm", space - 1),
        out_shape=jax.ShapeDtypeStruct((nodes_here, steps * vecs), F32),
        in_specs=[VMEM] + [ANY] * (2 * (space - 1)) + [VMEM] * (2 * (space - 1)),
        out_specs=VMEM,
        scratch_shapes=[
            pltpu.VMEM((nodes_here, (space - 1) * modes), BF16),
            pltpu.VMEM((steps * vecs, (space - 1) * modes), BF16),
            pltpu.VMEM((space - 1, 32, modes), BF16),
        ]
        + coef_scratch
        + [pltpu.SemaphoreType.DMA((3 * (space - 1),))],
        compiler_params=LIMIT,
        cost_estimate=pl.CostEstimate(
            flops=flops * (space - 1), transcendentals=0, bytes_accessed=4 * steps * vecs * modes * space
        ),
    )(partial, *direct, *swapped, *noise, *carries)


def solution(mesh):
    in_specs = (P("space"), P("tm", "space"), P(None, "space"), P(), P())
    out_specs = P("space", "tm")
    return jax.shard_map(local, mesh=mesh, in_specs=in_specs, out_specs=out_specs, check_vma=False)
```

```python
import functools

import jax
import jax.numpy as jnp
from jax import lax
from jax.experimental import pallas as pl
from jax.experimental.pallas import tpu as pltpu
from jax.sharding import PartitionSpec as P


F32 = jnp.float32
BF16 = jnp.bfloat16
VMEM = pl.BlockSpec(memory_space=pltpu.VMEM)
ANY = pl.BlockSpec(memory_space=pl.ANY)
HBM = pl.BlockSpec(memory_space=pltpu.HBM)
LIMIT = pltpu.CompilerParams(vmem_limit_bytes=48 << 20)
SINE = (6.28318516, -41.34165503, 81.60100406, -76.54978208, 39.53670436)


def partners(count):
    pairs = [(i, i + 1) for i in range(1, count - 2, 2)]
    return pairs, ([count - 1] if count > 1 else [])


def exchange(x, move):
    tm, space = lax.axis_size("tm"), lax.axis_size("space")
    moves = []
    for t in range(tm):
        for s in range(space):
            to = move(t, s)
            if to is not None:
                moves.append((t * space + s, to[0] * space + to[1]))
    return lax.ppermute(x, ("tm", "space"), moves)


def core_swap(x):
    return exchange(x, lambda t, s: (t ^ 1, s))


def split3(x):
    high = x.astype(BF16).astype(F32)
    rest = x - high
    middle = rest.astype(BF16).astype(F32)
    return high, middle, rest - middle


def mix_bits(state):
    state = state ^ lax.shift_right_logical(state, jnp.int32(16))
    state = state * jnp.int32(-2048144789)
    state = state ^ lax.shift_right_logical(state, jnp.int32(13))
    state = state * jnp.int32(-1028477387)
    return state ^ lax.shift_right_logical(state, jnp.int32(16))


def gaussian(seeded):
    first = mix_bits(seeded)
    second = mix_bits(first + jnp.int32(1013904223))
    unit = (lax.shift_right_logical(first, jnp.int32(8)).astype(F32) + 0.5) * (1.0 / 16777216.0)
    square = -2.0 * jnp.log(unit)
    radius = square * lax.rsqrt(jnp.maximum(square, 1e-30))
    turn = (lax.shift_right_arithmetic(second, jnp.int32(8)).astype(F32) + 0.5) * (1.0 / 16777216.0)
    w = 0.25 - jnp.abs(turn)
    z = w * w
    sine = SINE[4]
    for c in SINE[3::-1]:
        sine = sine * z + c
    return radius * (sine * w)


TAIL = 64


def pick(core, offsets):
    return offsets[0] if offsets[0] == offsets[1] else jnp.where(core == 0, offsets[0], offsets[1])


def pack_kernel(tm_axis, sp_axis, offsets, coup, spec, basis, *rest):
    *outs, coup_out, spec_out, sems = rest
    me, sp = lax.axis_index(tm_axis), lax.axis_index(sp_axis)
    core = lax.rem(me, 2)
    copies = [
        pltpu.make_async_copy(coup, coup_out, sems.at[len(outs)]),
        pltpu.make_async_copy(spec, spec_out, sems.at[len(outs) + 1]),
    ]
    for i, (out, offset) in enumerate(zip(outs, offsets)):
        rows = out.shape[0] - TAIL
        block = sp ^ pick(core, offset)
        if offset[0] == offset[1]:
            block = block * 2 + core
        start = pl.multiple_of(block * rows, rows)
        copies.append(
            pltpu.make_async_copy(basis.at[pl.ds(start, rows), :], out.at[pl.ds(0, rows), :], sems.at[i])
        )
    for copy in copies:
        copy.start()
    for copy in copies:
        copy.wait()


def totals(ref):
    product = square = total = None
    for t in range(ref.shape[0]):
        c = ref[pl.ds(t, 1), :]
        product = c if t == 0 else product * c
        square = c * c if t == 0 else square * (c * c)
        total = square if t == 0 else total + square
    return product, total


def joined(early, late):
    return early[0] * late[0], early[1] + (early[0] * early[0]) * late[1]


def table_rows(shape, rows):
    row = lax.broadcasted_iota(jnp.int32, shape, 0)
    table = jnp.zeros(shape, F32)
    for j, value in enumerate(rows):
        table = jnp.where(row == j, value, table)
    return table


def ordered(first, mine, theirs):
    early = tuple(jnp.where(first, x, y) for x, y in zip(mine, theirs))
    late = tuple(jnp.where(first, y, x) for x, y in zip(mine, theirs))
    return early, late


def table_kernel(tm_axis, count, coup, other, spec, *rest):
    out, *messages, tail, sems = rest[count:]
    first = lax.rem(lax.axis_index(tm_axis), 2) == 0
    (x,), (y,) = ordered(first, (coup[...],), (other[...],))
    parts = split3(x) + split3(y)
    parts = parts + (table_rows(x.shape, split3(spec[...])), jnp.zeros_like(x))
    for j in range(4):
        tail[pl.ds(16 * j, 16), :] = jnp.concatenate(parts[2 * j : 2 * j + 2], 0).astype(BF16)
    copies = []
    for i, message in enumerate(messages):
        rows = message.shape[0] - TAIL
        copies.append(pltpu.make_async_copy(tail, message.at[pl.ds(rows, TAIL), :], sems.at[i]))
        copies[-1].start()
    early, late = ordered(first, totals(coup), totals(other))
    out[...] = table_rows(out.shape, (*joined(early, late), *early, *late))
    for copy in copies:
        copy.wait()


def noise_kernel(tm_axis, sp_axis, blocks, extras, keys, counters, *rest):
    *outs, base = rest[extras:]
    outs = outs[: len(blocks)]
    steps, vecs, modes = outs[0].shape
    me, sp = lax.axis_index(tm_axis), lax.axis_index(sp_axis)
    diagonal = lax.broadcasted_iota(jnp.int32, (vecs, vecs), 0) == lax.broadcasted_iota(
        jnp.int32, (vecs, vecs), 1
    )

    def column(ref):
        row = jnp.broadcast_to(ref[...].astype(F32), (vecs, vecs))
        return jnp.sum(jnp.where(diagonal, row, 0.0), axis=1, keepdims=True).astype(jnp.int32)

    start = column(keys) * jnp.int32(668265261) + column(counters) * jnp.int32(374761393)
    base[...] = jnp.broadcast_to(start, base.shape)
    group = 8
    for out, (block, offset) in zip(outs, blocks):
        ids = (sp ^ pick(lax.rem(me, 2), offset)) * modes + lax.broadcasted_iota(jnp.int32, (1, modes), 1)
        lane = ids * jnp.int32(-1640531535)
        first_step = (me ^ block) * steps

        def step(t, _):
            shifted = lane + (first_step + t) * jnp.int32(374761393)
            for v in range(vecs // group):
                seeded = jnp.tile(base[pl.ds(v * group, group), :], (1, modes // 128)) + shifted
                out[t, pl.ds(v * group, group), :] = gaussian(seeded)
            return 0

        lax.fori_loop(0, steps, step, 0)


def chain(coup, spec, d_start, f_start):
    before, after = [], []
    square, total = None, None
    d_now = d_start
    for t in range(coup.shape[0]):
        c = coup[t : t + 1, :]
        square = c * c if t == 0 else square * (c * c)
        total = square if t == 0 else total + square
        before.append(d_now)
        d_now = d_start + f_start * total
        after.append(d_now)
    ratio = jnp.concatenate(before, 0) / jnp.concatenate(after, 0)
    return jnp.sqrt(ratio / spec), ratio


def after(start, total):
    return start[0] + start[1] * total[1], start[1] * (total[0] * total[0])


def select(flag, x, y):
    return tuple(jnp.where(flag, p, q) for p, q in zip(x, y))


def gain_of(start, total):
    return total[0] * start[0] / (start[0] + start[1] * total[1])


def offset_kernel(tm_axis, pairs, single, noise_own, noise_other, coup, coup_other, spec, table, *rest):
    count = 2 * (len(pairs) + len(single))
    received, rest = rest[:count], rest[count:]
    o_ref, late_ref, wts, df, tables, *coefs, tmp = rest
    steps, vecs, modes = noise_own.shape
    me = lax.axis_index(tm_axis)
    chip, core = me // 2, lax.rem(me, 2)
    first = core == 0
    one = jnp.ones((1, modes), F32)
    tables[chip] = table[...]
    for j, offsets in enumerate(pairs):
        tables[chip ^ pick(core, offsets)] = received[2 * j][...]
        tables[chip ^ pick(core, offsets[::-1])] = received[2 * j + 1][...]
    for e in single:
        tables[chip ^ e] = received[-2][...] + received[-1][...]
    now, start, weight = (one, one), (one, one), jnp.zeros((1, modes), F32)
    for b in range(tables.shape[0]):
        wts[b] = jnp.broadcast_to(weight, (8, modes))
        total = tables[b, pl.ds(0, 1), :], tables[b, pl.ds(1, 1), :]
        here = chip == b
        start = select(here, now, start)
        weight = jnp.where(here, 1.0, weight * gain_of(now, total))
        now = after(now, total)
    early = table[pl.ds(2, 1), :], table[pl.ds(3, 1), :]
    late = table[pl.ds(4, 1), :], table[pl.ds(5, 1), :]
    second = after(start, early)
    gain_early, gain_late = gain_of(start, early), gain_of(second, late)
    df[...] = table_rows((8, modes), (*start, *second, gain_late))
    own, other = ordered(first, start, second)
    for j, (ref, sums) in enumerate(((coup, own), (coup_other, other))):
        c = ref[...]
        a, ratio = chain(c, spec[...], *sums)
        coefs[2 * j][...] = c * a
        coefs[2 * j + 1][...] = c * ratio
    tmp[...] = jnp.broadcast_to(gain_early, tmp.shape)

    def tile(v, _):
        at = pl.ds(pl.multiple_of(v * 16, 16), 16)
        ends = []
        for j, noise in enumerate((noise_own, noise_other)):
            alpha, beta = coefs[2 * j], coefs[2 * j + 1]
            carry = jnp.zeros((16, modes), F32)
            for t in range(steps - 1, -1, -1):
                carry = alpha[pl.ds(t, 1), :] * noise[t, at, :] + beta[pl.ds(t, 1), :] * carry
            ends.append(carry)
        (early,), (late,) = ordered(first, ends[:1], ends[1:])
        o_ref[at, :] = (early + tmp[pl.ds(0, 1), :] * late).astype(BF16)
        late_ref[at, :] = late
        return 0

    lax.fori_loop(0, vecs // 16, tile, 0)


def combine_kernel(tm_axis, pairs, single, wts, *rest):
    *received, partial, sent = rest
    me = lax.axis_index(tm_axis)
    chip, core = me // 2, lax.rem(me, 2)
    last = wts.shape[0] - 1
    total = jnp.zeros(partial.shape, F32)
    for offsets, ref in zip(pairs + [(e, e) for e in single], received):
        at = jnp.minimum(chip + pick(core, offsets), last)
        total = total + wts[at][0:1, :] * ref[...].astype(F32)
    partial[...] = total
    sent[...] = total.astype(BF16)


def carry_kernel(tm_axis, partial, theirs, late, df, _, near, own):
    vecs, modes = partial.shape
    is_first = lax.rem(lax.axis_index(tm_axis), 2) == 0
    carry = partial[...] + theirs[...].astype(F32)
    before = (late[...] + df[pl.ds(4, 1), :] * carry).astype(BF16)
    carry = carry.astype(BF16)
    parts = ()
    for j in range(4):
        parts = parts + split3(df[pl.ds(j, 1), :])
    sums = table_rows((16, modes), parts).astype(BF16)
    near[pl.ds(0, vecs), :] = before
    near[pl.ds(vecs, vecs), :] = carry
    near[pl.ds(2 * vecs, 16), :] = sums
    own[pl.ds(0, vecs), :] = jnp.where(is_first, before, carry)
    own[pl.ds(vecs, 16), :] = sums


def values(core, noise, message, c, lam, coefs, rhs):
    steps, vecs, _ = noise.shape
    rows = message.shape[0] - 16
    df = message[pl.ds(rows, 16), :].astype(F32)
    sums = [df[3 * j : 3 * j + 1] + df[3 * j + 1 : 3 * j + 2] + df[3 * j + 2 : 3 * j + 3] for j in range(4)]
    sums = select(core == 0, sums[:2], sums[2:])
    a, ratio = chain(c, lam, *sums)
    a_ref, ratio_ref, c_ref = coefs
    a_ref[...] = a
    ratio_ref[...] = ratio
    c_ref[...] = c
    base = core * vecs if rows > vecs else 0

    def tile(v, _):
        at = pl.ds(pl.multiple_of(v * 16, 16), 16)
        carry = message[pl.ds(pl.multiple_of(base + v * 16, 16), 16), :].astype(F32)
        for t in range(steps - 1, -1, -1):
            value = a_ref[pl.ds(t, 1), :] * noise[t, at, :] + ratio_ref[pl.ds(t, 1), :] * carry
            if t:
                carry = c_ref[pl.ds(t, 1), :] * value
            rhs[pl.ds(pl.multiple_of(t * vecs + v * 16, 16), 16), :] = value.astype(BF16)
        return 0

    lax.fori_loop(0, vecs // 16, tile, 0)


def product(lhs, rhs):
    return lax.dot_general(lhs, rhs, (((1,), (1,)), ((), ())), preferred_element_type=F32)


def own_kernel(tm_axis, sp_axis, coup, spec, basis, noise, message, out, lhs, rhs, *rest):
    *coefs, sem = rest
    rows = lhs.shape[0]
    start = pl.multiple_of(lax.axis_index(sp_axis) * rows, rows)
    copy = pltpu.make_async_copy(basis.at[pl.ds(start, rows), :], lhs, sem)
    copy.start()
    values(lax.rem(lax.axis_index(tm_axis), 2), noise, message, coup[...], spec[...], coefs, rhs)
    copy.wait()
    out[...] = product(lhs[...], rhs[...])


def tail_of(core, tail):
    x = [tail[16 * j : 16 * j + 16].astype(F32) for j in range(4)]
    early = x[0][0:8] + x[0][8:16] + x[1][0:8]
    late = x[1][8:16] + x[2][0:8] + x[2][8:16]
    return jnp.where(core == 0, early, late), x[3][0:1] + x[3][1:2] + x[3][2:3]


def halves_kernel(tm_axis, partial, direct, swapped, noise, message, out, lhs, rhs, *rest):
    *coefs, sems = rest
    core = lax.rem(lax.axis_index(tm_axis), 2)
    rows = lhs.shape[0] // 2
    copies = []
    for j, source in enumerate((direct, swapped)):
        place = pl.multiple_of((core if j == 0 else 1 - core) * rows, rows)
        copies.append(
            pltpu.make_async_copy(source.at[pl.ds(0, rows), :], lhs.at[pl.ds(place, rows), :], sems.at[j])
        )
        copies[-1].start()
    c, lam = tail_of(core, direct[pl.ds(rows, TAIL), :])
    values(core, noise, message, c, lam, coefs, rhs)
    for copy in copies:
        copy.wait()
    out[...] = partial[...] + product(lhs[...], rhs[...])


def block_kernel(tm_axis, partial, basis, noise, message, out, rhs, *coefs):
    core = lax.rem(lax.axis_index(tm_axis), 2)
    rows = basis.shape[0] - TAIL
    c, lam = tail_of(core, basis[pl.ds(rows, TAIL), :])
    values(core, noise, message, c, lam, coefs, rhs)
    out[...] = partial[...] + product(basis[pl.ds(0, rows), :], rhs[...])


def last_kernel(tm_axis, partial, basis, noise, message, out, rhs, result, sems, *coefs):
    core = lax.rem(lax.axis_index(tm_axis), 2)
    rows = basis.shape[0] - TAIL
    c, lam = tail_of(core, basis[pl.ds(rows, TAIL), :])
    values(core, noise, message, c, lam, coefs, rhs)
    width = 128
    copies = []
    for i in range(result.shape[1] // width):
        at = pl.ds(i * width, width)
        result[:, at] = partial[:, at] + product(basis[pl.ds(0, rows), :], rhs[at, :])
        copies.append(pltpu.make_async_copy(result.at[:, at], out.at[:, at], sems.at[i]))
        copies[-1].start()
    for copy in copies:
        copy.wait()


def kernel_call(body, **options):
    return pl.pallas_call(body, **options)


def local(spectrum, coupling, spatial_basis, noise_keys, noise_counters):
    steps, modes = coupling.shape
    vecs = noise_keys.shape[0]
    tm, space = lax.axis_size("tm"), lax.axis_size("space")
    chips = tm // 2
    nodes_here = spatial_basis.shape[0] // space
    half = nodes_here // 2
    keys, counters = noise_keys.reshape(1, vecs), noise_counters.reshape(1, vecs)
    f32 = lambda *shape: jax.ShapeDtypeStruct(shape, F32)
    bf16 = lambda *shape: jax.ShapeDtypeStruct(shape, BF16)
    sp_pairs, sp_single = partners(space)
    z_pairs, z_single = partners(chips)
    routes = sp_pairs + [(d, d) for d in sp_single]
    fast = dict(compiler_params=LIMIT)

    other = core_swap(coupling)
    sizes = [nodes_here + TAIL] * len(sp_pairs) + [half + TAIL] * len(sp_single)
    *messages, coup, spec = kernel_call(
        functools.partial(pack_kernel, "tm", "space", routes),
        out_shape=[bf16(n, modes) for n in sizes] + [f32(steps, modes), f32(1, modes)],
        in_specs=[HBM] * 3,
        out_specs=[VMEM] * (len(sizes) + 2),
        scratch_shapes=[pltpu.SemaphoreType.DMA((len(sizes) + 2,))],
        **fast,
    )(*(pltpu.with_memory_space_constraint(x, pltpu.HBM) for x in (coupling, spectrum.reshape(1, modes), spatial_basis)))
    table, *messages = kernel_call(
        functools.partial(table_kernel, "tm", len(sizes)),
        out_shape=[f32(8, modes)] + [bf16(n, modes) for n in sizes],
        in_specs=[VMEM] * 3 + [ANY] * len(sizes),
        out_specs=[VMEM] + [ANY] * len(sizes),
        scratch_shapes=[pltpu.VMEM((TAIL, modes), BF16), pltpu.SemaphoreType.DMA((len(sizes),))],
        input_output_aliases={3 + i: 1 + i for i in range(len(sizes))},
        **fast,
    )(coup, other, spec, *messages)
    basis = [exchange(m, lambda t, s, r=r: (t, s ^ r[t % 2])) for m, r in zip(messages, routes)]

    def noise_of(blocks, after=(), through=()):
        count = len(blocks) * steps * vecs * modes
        extras = len(after) + len(through)
        return kernel_call(
            functools.partial(noise_kernel, "tm", "space", blocks, extras),
            out_shape=[f32(steps, vecs, modes)] * len(blocks)
            + [jax.ShapeDtypeStruct(x.shape, x.dtype) for x in through],
            in_specs=[VMEM] * 2 + [ANY] * extras,
            out_specs=[VMEM] * len(blocks) + [ANY] * len(through),
            scratch_shapes=[pltpu.VMEM((vecs, 128), jnp.int32)],
            input_output_aliases={2 + len(after) + i: len(blocks) + i for i in range(len(through))},
            cost_estimate=pl.CostEstimate(flops=count * 60, transcendentals=count * 2, bytes_accessed=count * 4),
            **fast,
        )(keys, counters, *after, *through)

    tables = [exchange(table, lambda t, s, r=r: (t ^ (2 * r[t % 2]), s)) for r in z_pairs]
    alone = [exchange(table, lambda t, s, e=e: (t ^ (2 * e), s) if t % 2 == 0 else None) for e in z_single]
    (own,) = noise_of([(0, (0, 0))], after=(table,))
    received = []
    for x in tables:
        received += [x, core_swap(x)]
    for x in alone:
        received += [x, exchange(x, lambda t, s: (t + 1, s) if t % 2 == 0 else None)]
    (paired,) = noise_of([(1, (0, 0))], after=(own,))

    total, late, weights, sums = kernel_call(
        functools.partial(offset_kernel, "tm", z_pairs, z_single),
        out_shape=[bf16(vecs, modes), f32(vecs, modes), f32(chips, 8, modes), f32(8, modes)],
        in_specs=[VMEM] * (6 + len(received)),
        out_specs=[VMEM] * 4,
        scratch_shapes=[pltpu.VMEM((chips, 8, modes), F32)] + [pltpu.VMEM((steps, modes), F32)] * 5,
        **fast,
    )(own, paired, coup, other, spec, table, *received)
    back = lambda t, s, e: (t - 2 * e, s) if t >= 2 * e else None
    later = [exchange(total, lambda t, s, r=r: back(t, s, r[t % 2])) for r in z_pairs]
    later += [exchange(total, lambda t, s, e=e: back(t, s, e) if t % 2 == 0 else None) for e in z_single]
    noise_single = noise_of([(0, (d, d)) for d in sp_single], after=(total,))
    partial, sent = kernel_call(
        functools.partial(combine_kernel, "tm", z_pairs, z_single),
        out_shape=[f32(vecs, modes), bf16(vecs, modes)],
        in_specs=[VMEM] * (1 + len(later)) + [ANY],
        out_specs=[VMEM] * 2,
        **fast,
    )(weights, *later, noise_single[0])
    theirs = core_swap(sent)
    out = noise_of([(0, r) for r in sp_pairs], after=(sent,), through=basis)
    noise_near, basis = out[: len(sp_pairs)], out[len(sp_pairs) :]
    basis_swapped = [core_swap(m) for m in basis]
    near, mine = kernel_call(
        functools.partial(carry_kernel, "tm"),
        out_shape=[bf16(2 * vecs + 16, modes), bf16(vecs + 16, modes)],
        in_specs=[VMEM] * 4 + [ANY],
        out_specs=[VMEM] * 2,
        **fast,
    )(partial, theirs, late, sums, noise_near[0])

    gather_near = [exchange(near, lambda t, s, r=r: (t, s ^ r[t % 2])) for r in sp_pairs]
    gather_single = [exchange(mine, lambda t, s, d=d: (t, s ^ d)) for d in sp_single]
    noise_far = noise_of([(0, r[::-1]) for r in sp_pairs], after=(mine,))

    flops = 2 * nodes_here * modes * steps * vecs
    rhs = pltpu.VMEM((steps * vecs, modes), BF16)
    lhs = pltpu.VMEM((nodes_here, modes), BF16)
    coefs = [pltpu.VMEM((steps, modes), F32)] * 3
    result = f32(nodes_here, steps * vecs)
    cost = pl.CostEstimate(flops=flops, transcendentals=0, bytes_accessed=4 * steps * vecs * modes)
    out = kernel_call(
        functools.partial(own_kernel, "tm", "space"),
        out_shape=result,
        in_specs=[VMEM, VMEM, HBM, VMEM, VMEM],
        out_specs=VMEM,
        scratch_shapes=[lhs, rhs] + coefs + [pltpu.SemaphoreType.DMA],
        cost_estimate=cost,
        **fast,
    )(coup, spec, spatial_basis, own, mine)
    count = len(sp_pairs)
    for j in range(len(sp_single)):
        out = kernel_call(
            functools.partial(halves_kernel, "tm"),
            out_shape=result,
            in_specs=[VMEM] * 5,
            out_specs=VMEM,
            scratch_shapes=[lhs, rhs] + coefs + [pltpu.SemaphoreType.DMA((2,))],
            cost_estimate=cost,
            **fast,
        )(out, basis[count + j], basis_swapped[count + j], noise_single[j], gather_single[j])
    gather_far = [core_swap(m) for m in gather_near]
    for group, (rows, noise, states) in enumerate(
        ((basis, noise_near, gather_near), (basis_swapped, noise_far, gather_far))
    ):
        for j in range(count):
            last = group == 1 and j == count - 1
            chunks = steps * vecs // 128
            out = kernel_call(
                functools.partial(last_kernel if last else block_kernel, "tm"),
                out_shape=result,
                in_specs=[VMEM] * 4,
                out_specs=HBM if last else VMEM,
                scratch_shapes=[rhs]
                + ([pltpu.VMEM(result.shape, F32), pltpu.SemaphoreType.DMA((chunks,))] if last else [])
                + coefs,
                cost_estimate=cost,
                **fast,
            )(out, rows[j], noise[j], states[j])
    return out


def solution(mesh):
    in_specs = (P("space"), P("tm", "space"), P(None, "space"), P(), P())
    out_specs = P("space", "tm")
    return jax.shard_map(local, mesh=mesh, in_specs=in_specs, out_specs=out_specs, check_vma=False)
```

```python
import functools

import jax
import jax.numpy as jnp
from jax import lax
from jax.experimental import pallas as pl
from jax.experimental.pallas import tpu as pltpu
from jax.sharding import PartitionSpec as P


F32 = jnp.float32
BF16 = jnp.bfloat16
VMEM = pl.BlockSpec(memory_space=pltpu.VMEM)
ANY = pl.BlockSpec(memory_space=pl.ANY)
HBM = pl.BlockSpec(memory_space=pltpu.HBM)
LIMIT = pltpu.CompilerParams(vmem_limit_bytes=48 << 20)
SINE = (6.28318516, -41.34165503, 81.60100406, -76.54978208, 39.53670436)


def swap(x, axis, offset):
    count = lax.axis_size(axis)
    return lax.ppermute(x, axis, [(i, i ^ offset) for i in range(count)])


def split3(x):
    high = x.astype(BF16).astype(F32)
    rest = x - high
    middle = rest.astype(BF16).astype(F32)
    return high, middle, rest - middle


def mix_bits(state):
    state = state ^ lax.shift_right_logical(state, jnp.int32(16))
    state = state * jnp.int32(-2048144789)
    state = state ^ lax.shift_right_logical(state, jnp.int32(13))
    state = state * jnp.int32(-1028477387)
    return state ^ lax.shift_right_logical(state, jnp.int32(16))


def gaussian(seeded):
    first = mix_bits(seeded)
    second = mix_bits(first + jnp.int32(1013904223))
    unit = (lax.shift_right_logical(first, jnp.int32(8)).astype(F32) + 0.5) * (1.0 / 16777216.0)
    square = -2.0 * jnp.log(unit)
    radius = square * lax.rsqrt(jnp.maximum(square, 1e-30))
    turn = (lax.shift_right_arithmetic(second, jnp.int32(8)).astype(F32) + 0.5) * (1.0 / 16777216.0)
    w = 0.25 - jnp.abs(turn)
    z = w * w
    sine = SINE[4]
    for c in SINE[3::-1]:
        sine = sine * z + c
    return radius * (sine * w)


TAIL = 32


def pack_kernel(tm_axis, sp_axis, coup, spec, basis, *rest):
    *outs, coup_out, spec_out, sems = rest
    me, sp = lax.axis_index(tm_axis), lax.axis_index(sp_axis)
    core = lax.rem(me, 2)
    rows = outs[0].shape[0] - TAIL
    small = [
        pltpu.make_async_copy(coup, coup_out, sems.at[len(outs)]),
        pltpu.make_async_copy(spec, spec_out, sems.at[len(outs) + 1]),
    ]
    large = []
    for i, out in enumerate(outs):
        start = pl.multiple_of(((sp ^ (i + 1)) * 2 + core) * rows, rows)
        large.append(
            pltpu.make_async_copy(basis.at[pl.ds(start, rows), :], out.at[pl.ds(0, rows), :], sems.at[i])
        )
    for copy in small + large:
        copy.start()
    for copy in small:
        copy.wait()
    x = coup_out[...]
    parts = split3(x)
    upper = jnp.concatenate(parts[:2], 0).astype(BF16)
    lower = jnp.concatenate([parts[2], table_rows(x.shape, split3(spec_out[...]))], 0).astype(BF16)
    for out in outs:
        out[pl.ds(rows, 16), :] = upper
        out[pl.ds(rows + 16, 16), :] = lower
    for copy in large:
        copy.wait()


def totals(ref):
    product = square = total = None
    for t in range(ref.shape[0]):
        c = ref[pl.ds(t, 1), :]
        product = c if t == 0 else product * c
        square = c * c if t == 0 else square * (c * c)
        total = square if t == 0 else total + square
    return product, total


def joined(early, late):
    return early[0] * late[0], early[1] + (early[0] * early[0]) * late[1]


def table_rows(shape, rows):
    row = lax.broadcasted_iota(jnp.int32, shape, 0)
    table = jnp.zeros(shape, F32)
    for j, value in enumerate(rows):
        table = jnp.where(row == j, value, table)
    return table


def ordered(first, mine, theirs):
    early = tuple(jnp.where(first, x, y) for x, y in zip(mine, theirs))
    late = tuple(jnp.where(first, y, x) for x, y in zip(mine, theirs))
    return early, late


def table_kernel(tm_axis, coup, other, out):
    first = lax.rem(lax.axis_index(tm_axis), 2) == 0
    early, late = ordered(first, totals(coup), totals(other))
    out[...] = table_rows(out.shape, (*joined(early, late), *early, *late))


def noise_kernel(tm_axis, sp_axis, blocks, extras, keys, counters, *rest):
    *outs, base = rest[extras:]
    outs = outs[: len(blocks)]
    steps, vecs, modes = outs[0].shape
    me, sp = lax.axis_index(tm_axis), lax.axis_index(sp_axis)
    diagonal = lax.broadcasted_iota(jnp.int32, (vecs, vecs), 0) == lax.broadcasted_iota(
        jnp.int32, (vecs, vecs), 1
    )

    def column(ref):
        row = jnp.broadcast_to(ref[...].astype(F32), (vecs, vecs))
        return jnp.sum(jnp.where(diagonal, row, 0.0), axis=1, keepdims=True).astype(jnp.int32)

    start = column(keys) * jnp.int32(668265261) + column(counters) * jnp.int32(374761393)
    base[...] = jnp.broadcast_to(start, base.shape)
    group = 8
    for out, (block, offset) in zip(outs, blocks):
        ids = (sp ^ offset) * modes + lax.broadcasted_iota(jnp.int32, (1, modes), 1)
        lane = ids * jnp.int32(-1640531535)
        first_step = (me ^ block) * steps

        def step(t, _):
            shifted = lane + (first_step + t) * jnp.int32(374761393)
            for v in range(vecs // group):
                seeded = jnp.tile(base[pl.ds(v * group, group), :], (1, modes // 128)) + shifted
                out[t, pl.ds(v * group, group), :] = gaussian(seeded)
            return 0

        lax.fori_loop(0, steps, step, 0)


def chain(coup, spec, d_start, f_start):
    before, after = [], []
    square, total = None, None
    d_now = d_start
    for t in range(coup.shape[0]):
        c = coup[t : t + 1, :]
        square = c * c if t == 0 else square * (c * c)
        total = square if t == 0 else total + square
        before.append(d_now)
        d_now = d_start + f_start * total
        after.append(d_now)
    ratio = jnp.concatenate(before, 0) / jnp.concatenate(after, 0)
    return jnp.sqrt(ratio / spec), ratio


def after(start, total):
    return start[0] + start[1] * total[1], start[1] * (total[0] * total[0])


def select(flag, x, y):
    return tuple(jnp.where(flag, p, q) for p, q in zip(x, y))


def gain_of(start, total):
    return total[0] * start[0] / (start[0] + start[1] * total[1])


def offset_kernel(tm_axis, noise_own, noise_other, coup, coup_other, spec, table, *rest):
    received, rest = rest[:-10], rest[-10:]
    o_ref, late_ref, wts, df, tables, *coefs, tmp = rest
    steps, vecs, modes = noise_own.shape
    me = lax.axis_index(tm_axis)
    chip = me // 2
    first = lax.rem(me, 2) == 0
    one = jnp.ones((1, modes), F32)
    tables[chip] = table[...]
    for e, ref in enumerate(received):
        tables[chip ^ (e + 1)] = ref[...]
    now, start, weight = (one, one), (one, one), jnp.zeros((1, modes), F32)
    for b in range(tables.shape[0]):
        wts[b] = jnp.broadcast_to(weight, (8, modes))
        total = tables[b, pl.ds(0, 1), :], tables[b, pl.ds(1, 1), :]
        here = chip == b
        start = select(here, now, start)
        weight = jnp.where(here, 1.0, weight * gain_of(now, total))
        now = after(now, total)
    early = table[pl.ds(2, 1), :], table[pl.ds(3, 1), :]
    late = table[pl.ds(4, 1), :], table[pl.ds(5, 1), :]
    second = after(start, early)
    gain_early, gain_late = gain_of(start, early), gain_of(second, late)
    df[...] = table_rows((8, modes), (*start, *second, gain_late))
    own, other = ordered(first, start, second)
    for j, (ref, sums) in enumerate(((coup, own), (coup_other, other))):
        c = ref[...]
        a, ratio = chain(c, spec[...], *sums)
        coefs[2 * j][...] = c * a
        coefs[2 * j + 1][...] = c * ratio
    tmp[...] = jnp.broadcast_to(gain_early, tmp.shape)

    def tile(v, _):
        at = pl.ds(pl.multiple_of(v * 16, 16), 16)
        ends = []
        for j, noise in enumerate((noise_own, noise_other)):
            alpha, beta = coefs[2 * j], coefs[2 * j + 1]
            carry = jnp.zeros((16, modes), F32)
            for t in range(steps - 1, -1, -1):
                carry = alpha[pl.ds(t, 1), :] * noise[t, at, :] + beta[pl.ds(t, 1), :] * carry
            ends.append(carry)
        (early,), (late,) = ordered(first, ends[:1], ends[1:])
        o_ref[at, :] = (early + tmp[pl.ds(0, 1), :] * late).astype(BF16)
        late_ref[at, :] = late
        return 0

    lax.fori_loop(0, vecs // 16, tile, 0)


def carry_kernel(tm_axis, late, wts, df, *rest):
    *received, _, out = rest
    vecs, modes = late.shape
    me = lax.axis_index(tm_axis)
    first = lax.rem(me, 2) == 0
    carry = jnp.zeros(late.shape, F32)
    for e, ref in enumerate(received):
        carry = carry + wts[(me // 2) ^ (e + 1)][0:1, :] * ref[...].astype(F32)
    out[pl.ds(0, vecs), :] = jnp.where(first, late[...] + df[pl.ds(4, 1), :] * carry, carry).astype(BF16)
    own = select(first, (df[pl.ds(0, 1), :], df[pl.ds(1, 1), :]), (df[pl.ds(2, 1), :], df[pl.ds(3, 1), :]))
    out[pl.ds(vecs, 16), :] = table_rows((16, modes), split3(own[0]) + split3(own[1])).astype(BF16)


def values(noise, message, c, lam, coefs, rhs):
    steps, vecs, _ = noise.shape
    df = message[pl.ds(vecs, 16), :].astype(F32)
    a, ratio = chain(c, lam, df[0:1] + df[1:2] + df[2:3], df[3:4] + df[4:5] + df[5:6])
    a_ref, ratio_ref, c_ref = coefs
    a_ref[...] = a
    ratio_ref[...] = ratio
    c_ref[...] = c

    def tile(v, _):
        at = pl.ds(pl.multiple_of(v * 16, 16), 16)
        carry = message[at, :].astype(F32)
        for t in range(steps - 1, -1, -1):
            value = a_ref[pl.ds(t, 1), :] * noise[t, at, :] + ratio_ref[pl.ds(t, 1), :] * carry
            if t:
                carry = c_ref[pl.ds(t, 1), :] * value
            rhs[pl.ds(pl.multiple_of(t * vecs + v * 16, 16), 16), :] = value.astype(BF16)
        return 0

    lax.fori_loop(0, vecs // 16, tile, 0)


def product(lhs, rhs):
    return lax.dot_general(lhs, rhs, (((1,), (1,)), ((), ())), preferred_element_type=F32)


def own_kernel(sp_axis, coup, spec, basis, noise, message, out, lhs, rhs, *rest):
    *coefs, sem = rest
    rows = lhs.shape[0]
    start = pl.multiple_of(lax.axis_index(sp_axis) * rows, rows)
    copy = pltpu.make_async_copy(basis.at[pl.ds(start, rows), :], lhs, sem)
    copy.start()
    values(noise, message, coup[...], spec[...], coefs, rhs)
    copy.wait()
    out[...] = product(lhs[...], rhs[...])


def block_kernel(tm_axis, last, partial, direct, swapped, noise, message, out, lhs, rhs, sems, *rest):
    coefs = rest[:3]
    core = lax.rem(lax.axis_index(tm_axis), 2)
    rows = lhs.shape[0] // 2
    copies = []
    for j, source in enumerate((direct, swapped)):
        place = pl.multiple_of((core if j == 0 else 1 - core) * rows, rows)
        copies.append(
            pltpu.make_async_copy(source.at[pl.ds(0, rows), :], lhs.at[pl.ds(place, rows), :], sems.at[j])
        )
        copies[-1].start()
    upper = direct[pl.ds(rows, 16), :].astype(F32)
    lower = direct[pl.ds(rows + 16, 16), :].astype(F32)
    c = upper[0:8] + upper[8:16] + lower[0:8]
    values(noise, message, c, lower[8:9] + lower[9:10] + lower[10:11], coefs, rhs)
    for copy in copies:
        copy.wait()
    if not last:
        out[...] = partial[...] + product(lhs[...], rhs[...])
        return
    result = rest[3]
    copies = []
    width = result.shape[2]
    for i in range(result.shape[0]):
        at = pl.ds(i * width, width)
        result[i] = partial[:, at] + product(lhs[...], rhs[at, :])
        copies.append(pltpu.make_async_copy(result.at[i], out.at[:, at], sems.at[2 + i]))
        copies[-1].start()
    for copy in copies:
        copy.wait()


def kernel_call(body, **options):
    return pl.pallas_call(body, **options)


def local(spectrum, coupling, spatial_basis, noise_keys, noise_counters):
    steps, modes = coupling.shape
    vecs = noise_keys.shape[0]
    tm, space = lax.axis_size("tm"), lax.axis_size("space")
    chips = tm // 2
    nodes_here = spatial_basis.shape[0] // space
    half = nodes_here // 2
    keys, counters = noise_keys.reshape(1, vecs), noise_counters.reshape(1, vecs)
    f32 = lambda *shape: jax.ShapeDtypeStruct(shape, F32)
    bf16 = lambda *shape: jax.ShapeDtypeStruct(shape, BF16)
    fast = dict(compiler_params=LIMIT)
    in_hbm = [
        pltpu.with_memory_space_constraint(x, pltpu.HBM)
        for x in (coupling, spectrum.reshape(1, modes), spatial_basis)
    ]

    other = swap(coupling, "tm", 1)
    *messages, coup, spec = kernel_call(
        functools.partial(pack_kernel, "tm", "space"),
        out_shape=[bf16(half + TAIL, modes)] * (space - 1) + [f32(steps, modes), f32(1, modes)],
        in_specs=[HBM] * 3,
        out_specs=[VMEM] * (space + 1),
        scratch_shapes=[pltpu.SemaphoreType.DMA((space + 1,))],
        **fast,
    )(*in_hbm)
    table = kernel_call(
        functools.partial(table_kernel, "tm"),
        out_shape=f32(8, modes),
        in_specs=[VMEM] * 2,
        out_specs=VMEM,
        **fast,
    )(coup, other)
    tables = [swap(table, "tm", 2 * e) for e in range(1, chips)]
    direct = [swap(m, "space", d + 1) for d, m in enumerate(messages)]

    def noise_of(blocks, after):
        count = len(blocks) * steps * vecs * modes
        return kernel_call(
            functools.partial(noise_kernel, "tm", "space", blocks, len(after)),
            out_shape=[f32(steps, vecs, modes)] * len(blocks),
            in_specs=[VMEM] * 2 + [ANY] * len(after),
            out_specs=[VMEM] * len(blocks),
            scratch_shapes=[pltpu.VMEM((vecs, 128), jnp.int32)],
            cost_estimate=pl.CostEstimate(flops=count * 60, transcendentals=count * 2, bytes_accessed=count * 4),
            **fast,
        )(keys, counters, *after)

    own, paired = noise_of(((0, 0), (1, 0)), (table,))
    total, late, weights, sums = kernel_call(
        functools.partial(offset_kernel, "tm"),
        out_shape=[bf16(vecs, modes), f32(vecs, modes), f32(chips, 8, modes), f32(8, modes)],
        in_specs=[VMEM] * (6 + len(tables)),
        out_specs=[VMEM] * 4,
        scratch_shapes=[pltpu.VMEM((chips, 8, modes), F32)] + [pltpu.VMEM((steps, modes), F32)] * 5,
        **fast,
    )(own, paired, coup, other, spec, table, *tables)
    later = [swap(total, "tm", 2 * e) for e in range(1, chips)]
    third = max(1, (space - 1) // 3)
    parts = [range(1, 1 + third), range(1 + third, 1 + 2 * third), range(1 + 2 * third, space)]
    noise = list(noise_of([(0, d) for d in parts[0]], (total,)))
    noise += noise_of([(0, d) for d in parts[1]], (noise[-1],))
    carry = kernel_call(
        functools.partial(carry_kernel, "tm"),
        out_shape=bf16(vecs + 16, modes),
        in_specs=[VMEM] * (3 + len(later)) + [ANY],
        out_specs=VMEM,
        **fast,
    )(late, weights, sums, *later, noise[-1])
    carries = [swap(carry, "space", d) for d in range(1, space)]
    swapped = [swap(m, "tm", 1) for m in direct]
    noise += noise_of([(0, d) for d in parts[2]], (carry,))

    flops = 2 * nodes_here * modes * steps * vecs
    lhs, rhs = pltpu.VMEM((nodes_here, modes), BF16), pltpu.VMEM((steps * vecs, modes), BF16)
    coefs = [pltpu.VMEM((steps, modes), F32)] * 3
    result = f32(nodes_here, steps * vecs)
    cost = pl.CostEstimate(flops=flops, transcendentals=0, bytes_accessed=4 * steps * vecs * modes)
    out = kernel_call(
        functools.partial(own_kernel, "space"),
        out_shape=result,
        in_specs=[VMEM, VMEM, HBM, VMEM, VMEM],
        out_specs=VMEM,
        scratch_shapes=[lhs, rhs] + coefs + [pltpu.SemaphoreType.DMA],
        cost_estimate=cost,
        **fast,
    )(coup, spec, spatial_basis, own, carry)
    width = 128
    chunks = steps * vecs // width
    for d in range(space - 2, -1, -1):
        last = d == 0
        out = kernel_call(
            functools.partial(block_kernel, "tm", last),
            out_shape=result,
            in_specs=[VMEM] * 5,
            out_specs=HBM if last else VMEM,
            scratch_shapes=[lhs, rhs, pltpu.SemaphoreType.DMA((2 + chunks if last else 2,))]
            + coefs
            + ([pltpu.VMEM((chunks, nodes_here, width), F32)] if last else []),
            cost_estimate=cost,
            **fast,
        )(out, direct[d], swapped[d], noise[d], carries[d])
    return out


def solution(mesh):
    in_specs = (P("space"), P("tm", "space"), P(None, "space"), P(), P())
    out_specs = P("space", "tm")
    return jax.shard_map(local, mesh=mesh, in_specs=in_specs, out_specs=out_specs, check_vma=False)
```

```python
import functools

import jax
import jax.numpy as jnp
from jax import lax
from jax.experimental import pallas as pl
from jax.experimental.pallas import tpu as pltpu
from jax.sharding import PartitionSpec as P


F32 = jnp.float32
BF16 = jnp.bfloat16
VMEM = pl.BlockSpec(memory_space=pltpu.VMEM)
ANY = pl.BlockSpec(memory_space=pl.ANY)
HBM = pl.BlockSpec(memory_space=pltpu.HBM)
LIMIT = pltpu.CompilerParams(vmem_limit_bytes=48 << 20)
SINE = (6.28318516, -41.34165503, 81.60100406, -76.54978208, 39.53670436)


def partners(count):
    pairs = [(i, i + 1) for i in range(1, count - 2, 2)]
    return pairs, ([count - 1] if count > 1 else [])


def exchange(x, move):
    tm, space = lax.axis_size("tm"), lax.axis_size("space")
    moves = []
    for t in range(tm):
        for s in range(space):
            to = move(t, s)
            if to is not None:
                moves.append((t * space + s, to[0] * space + to[1]))
    return lax.ppermute(x, ("tm", "space"), moves)


def swap(x, axis, offset):
    count = lax.axis_size(axis)
    return lax.ppermute(x, axis, [(i, i ^ offset) for i in range(count)])


def split3(x):
    high = x.astype(BF16).astype(F32)
    rest = x - high
    middle = rest.astype(BF16).astype(F32)
    return high, middle, rest - middle


def mix_bits(state):
    state = state ^ lax.shift_right_logical(state, jnp.int32(16))
    state = state * jnp.int32(-2048144789)
    state = state ^ lax.shift_right_logical(state, jnp.int32(13))
    state = state * jnp.int32(-1028477387)
    return state ^ lax.shift_right_logical(state, jnp.int32(16))


def gaussian(seeded):
    first = mix_bits(seeded)
    second = mix_bits(first + jnp.int32(1013904223))
    unit = (lax.shift_right_logical(first, jnp.int32(8)).astype(F32) + 0.5) * (1.0 / 16777216.0)
    square = -2.0 * jnp.log(unit)
    radius = square * lax.rsqrt(jnp.maximum(square, 1e-30))
    turn = (lax.shift_right_arithmetic(second, jnp.int32(8)).astype(F32) + 0.5) * (1.0 / 16777216.0)
    w = 0.25 - jnp.abs(turn)
    z = w * w
    sine = SINE[4]
    for c in SINE[3::-1]:
        sine = sine * z + c
    return radius * (sine * w)


TAIL = 64


def pick(core, offsets):
    return offsets[0] if offsets[0] == offsets[1] else jnp.where(core == 0, offsets[0], offsets[1])


def pack_kernel(tm_axis, sp_axis, offsets, coup, spec, basis, *rest):
    *outs, coup_out, spec_out, sems = rest
    me, sp = lax.axis_index(tm_axis), lax.axis_index(sp_axis)
    core = lax.rem(me, 2)
    copies = [
        pltpu.make_async_copy(coup, coup_out, sems.at[len(outs)]),
        pltpu.make_async_copy(spec, spec_out, sems.at[len(outs) + 1]),
    ]
    for i, (out, offset) in enumerate(zip(outs, offsets)):
        rows = out.shape[0] - TAIL
        block = sp ^ pick(core, offset)
        if offset[0] == offset[1]:
            block = block * 2 + core
        start = pl.multiple_of(block * rows, rows)
        copies.append(
            pltpu.make_async_copy(basis.at[pl.ds(start, rows), :], out.at[pl.ds(0, rows), :], sems.at[i])
        )
    for copy in copies:
        copy.start()
    for copy in copies:
        copy.wait()


def totals(ref):
    product = square = total = None
    for t in range(ref.shape[0]):
        c = ref[pl.ds(t, 1), :]
        product = c if t == 0 else product * c
        square = c * c if t == 0 else square * (c * c)
        total = square if t == 0 else total + square
    return product, total


def joined(early, late):
    return early[0] * late[0], early[1] + (early[0] * early[0]) * late[1]


def table_rows(shape, rows):
    row = lax.broadcasted_iota(jnp.int32, shape, 0)
    table = jnp.zeros(shape, F32)
    for j, value in enumerate(rows):
        table = jnp.where(row == j, value, table)
    return table


def ordered(first, mine, theirs):
    early = tuple(jnp.where(first, x, y) for x, y in zip(mine, theirs))
    late = tuple(jnp.where(first, y, x) for x, y in zip(mine, theirs))
    return early, late


def table_kernel(tm_axis, count, coup, other, spec, *rest):
    out, *messages, tail, sems = rest[count:]
    first = lax.rem(lax.axis_index(tm_axis), 2) == 0
    (x,), (y,) = ordered(first, (coup[...],), (other[...],))
    parts = split3(x) + split3(y)
    parts = parts + (table_rows(x.shape, split3(spec[...])), jnp.zeros_like(x))
    for j in range(4):
        tail[pl.ds(16 * j, 16), :] = jnp.concatenate(parts[2 * j : 2 * j + 2], 0).astype(BF16)
    copies = []
    for i, message in enumerate(messages):
        rows = message.shape[0] - TAIL
        copies.append(pltpu.make_async_copy(tail, message.at[pl.ds(rows, TAIL), :], sems.at[i]))
        copies[-1].start()
    early, late = ordered(first, totals(coup), totals(other))
    out[...] = table_rows(out.shape, (*joined(early, late), *early, *late))
    for copy in copies:
        copy.wait()


def noise_kernel(tm_axis, sp_axis, blocks, extras, keys, counters, *rest):
    *outs, base = rest[extras:]
    outs = outs[: len(blocks)]
    steps, vecs, modes = outs[0].shape
    me, sp = lax.axis_index(tm_axis), lax.axis_index(sp_axis)
    diagonal = lax.broadcasted_iota(jnp.int32, (vecs, vecs), 0) == lax.broadcasted_iota(
        jnp.int32, (vecs, vecs), 1
    )

    def column(ref):
        row = jnp.broadcast_to(ref[...].astype(F32), (vecs, vecs))
        return jnp.sum(jnp.where(diagonal, row, 0.0), axis=1, keepdims=True).astype(jnp.int32)

    start = column(keys) * jnp.int32(668265261) + column(counters) * jnp.int32(374761393)
    base[...] = jnp.broadcast_to(start, base.shape)
    group = 8
    for out, (block, offset) in zip(outs, blocks):
        ids = (sp ^ offset) * modes + lax.broadcasted_iota(jnp.int32, (1, modes), 1)
        lane = ids * jnp.int32(-1640531535)
        first_step = (me ^ block) * steps

        def step(t, _):
            shifted = lane + (first_step + t) * jnp.int32(374761393)
            for v in range(vecs // group):
                seeded = jnp.tile(base[pl.ds(v * group, group), :], (1, modes // 128)) + shifted
                out[t, pl.ds(v * group, group), :] = gaussian(seeded)
            return 0

        lax.fori_loop(0, steps, step, 0)


def chain(coup, spec, d_start, f_start):
    before, after = [], []
    square, total = None, None
    d_now = d_start
    for t in range(coup.shape[0]):
        c = coup[t : t + 1, :]
        square = c * c if t == 0 else square * (c * c)
        total = square if t == 0 else total + square
        before.append(d_now)
        d_now = d_start + f_start * total
        after.append(d_now)
    ratio = jnp.concatenate(before, 0) / jnp.concatenate(after, 0)
    return jnp.sqrt(ratio / spec), ratio


def after(start, total):
    return start[0] + start[1] * total[1], start[1] * (total[0] * total[0])


def select(flag, x, y):
    return tuple(jnp.where(flag, p, q) for p, q in zip(x, y))


def gain_of(start, total):
    return total[0] * start[0] / (start[0] + start[1] * total[1])


def offset_kernel(tm_axis, noise_own, noise_other, coup, coup_other, spec, table, *rest):
    received, rest = rest[:-10], rest[-10:]
    o_ref, late_ref, wts, df, tables, *coefs, tmp = rest
    steps, vecs, modes = noise_own.shape
    me = lax.axis_index(tm_axis)
    chip = me // 2
    first = lax.rem(me, 2) == 0
    one = jnp.ones((1, modes), F32)
    tables[chip] = table[...]
    for e, ref in enumerate(received):
        tables[chip ^ (e + 1)] = ref[...]
    now, start, weight = (one, one), (one, one), jnp.zeros((1, modes), F32)
    for b in range(tables.shape[0]):
        wts[b] = jnp.broadcast_to(weight, (8, modes))
        total = tables[b, pl.ds(0, 1), :], tables[b, pl.ds(1, 1), :]
        here = chip == b
        start = select(here, now, start)
        weight = jnp.where(here, 1.0, weight * gain_of(now, total))
        now = after(now, total)
    early = table[pl.ds(2, 1), :], table[pl.ds(3, 1), :]
    late = table[pl.ds(4, 1), :], table[pl.ds(5, 1), :]
    second = after(start, early)
    gain_early, gain_late = gain_of(start, early), gain_of(second, late)
    df[...] = table_rows((8, modes), (*start, *second, gain_late))
    own, other = ordered(first, start, second)
    for j, (ref, sums) in enumerate(((coup, own), (coup_other, other))):
        c = ref[...]
        a, ratio = chain(c, spec[...], *sums)
        coefs[2 * j][...] = c * a
        coefs[2 * j + 1][...] = c * ratio
    tmp[...] = jnp.broadcast_to(gain_early, tmp.shape)

    def tile(v, _):
        at = pl.ds(pl.multiple_of(v * 16, 16), 16)
        ends = []
        for j, noise in enumerate((noise_own, noise_other)):
            alpha, beta = coefs[2 * j], coefs[2 * j + 1]
            carry = jnp.zeros((16, modes), F32)
            for t in range(steps - 1, -1, -1):
                carry = alpha[pl.ds(t, 1), :] * noise[t, at, :] + beta[pl.ds(t, 1), :] * carry
            ends.append(carry)
        (early,), (late,) = ordered(first, ends[:1], ends[1:])
        o_ref[at, :] = (early + tmp[pl.ds(0, 1), :] * late).astype(BF16)
        late_ref[at, :] = late
        return 0

    lax.fori_loop(0, vecs // 16, tile, 0)


def carry_kernel(tm_axis, late, wts, df, *rest):
    *received, _, out = rest
    vecs, modes = late.shape
    me = lax.axis_index(tm_axis)
    first = lax.rem(me, 2) == 0
    carry = jnp.zeros(late.shape, F32)
    for e, ref in enumerate(received):
        carry = carry + wts[(me // 2) ^ (e + 1)][0:1, :] * ref[...].astype(F32)
    out[pl.ds(0, vecs), :] = jnp.where(first, late[...] + df[pl.ds(4, 1), :] * carry, carry).astype(BF16)
    own = select(first, (df[pl.ds(0, 1), :], df[pl.ds(1, 1), :]), (df[pl.ds(2, 1), :], df[pl.ds(3, 1), :]))
    out[pl.ds(vecs, 16), :] = table_rows((16, modes), split3(own[0]) + split3(own[1])).astype(BF16)


def values(noise, message, c, lam, coefs, rhs):
    steps, vecs, _ = noise.shape
    df = message[pl.ds(vecs, 16), :].astype(F32)
    a, ratio = chain(c, lam, df[0:1] + df[1:2] + df[2:3], df[3:4] + df[4:5] + df[5:6])
    a_ref, ratio_ref, c_ref = coefs
    a_ref[...] = a
    ratio_ref[...] = ratio
    c_ref[...] = c

    def tile(v, _):
        at = pl.ds(pl.multiple_of(v * 16, 16), 16)
        carry = message[at, :].astype(F32)
        for t in range(steps - 1, -1, -1):
            value = a_ref[pl.ds(t, 1), :] * noise[t, at, :] + ratio_ref[pl.ds(t, 1), :] * carry
            if t:
                carry = c_ref[pl.ds(t, 1), :] * value
            rhs[pl.ds(pl.multiple_of(t * vecs + v * 16, 16), 16), :] = value.astype(BF16)
        return 0

    lax.fori_loop(0, vecs // 16, tile, 0)


def product(lhs, rhs):
    return lax.dot_general(lhs, rhs, (((1,), (1,)), ((), ())), preferred_element_type=F32)


def own_kernel(sp_axis, coup, spec, basis, noise, message, out, lhs, rhs, *rest):
    *coefs, sem = rest
    rows = lhs.shape[0]
    start = pl.multiple_of(lax.axis_index(sp_axis) * rows, rows)
    copy = pltpu.make_async_copy(basis.at[pl.ds(start, rows), :], lhs, sem)
    copy.start()
    values(noise, message, coup[...], spec[...], coefs, rhs)
    copy.wait()
    out[...] = product(lhs[...], rhs[...])


def block_kernel(tm_axis, place, last, partial, direct, swapped, noise, message, out, lhs, rhs, tail, sems, *rest):
    coefs = rest[:3]
    core = lax.rem(lax.axis_index(tm_axis), 2)
    rows = direct.shape[0] - TAIL
    if place is None:
        head = pltpu.make_async_copy(direct.at[pl.ds(rows, TAIL), :], tail, sems.at[0])
        head.start()
        for j, source in enumerate((direct, swapped)):
            at = pl.multiple_of((core if j == 0 else 1 - core) * rows, rows)
            pltpu.make_async_copy(source.at[pl.ds(0, rows), :], lhs.at[pl.ds(at, rows), :], sems.at[1 + j]).start()
        head.wait()
    else:
        for j, source in enumerate((direct, swapped)):

            @pl.when((core == place) == (j == 0))
            def _():
                pltpu.make_async_copy(source.at[pl.ds(rows, TAIL), :], tail, sems.at[0]).start()
                pltpu.make_async_copy(source.at[pl.ds(0, rows), :], lhs, sems.at[1]).start()

        pltpu.make_async_copy(direct.at[pl.ds(rows, TAIL), :], tail, sems.at[0]).wait()
    x = [tail[pl.ds(16 * j, 16), :].astype(F32) for j in range(4)]
    early = x[0][0:8] + x[0][8:16] + x[1][0:8]
    late = x[1][8:16] + x[2][0:8] + x[2][8:16]
    c = jnp.where(core == 0, early, late)
    values(noise, message, c, x[3][0:1] + x[3][1:2] + x[3][2:3], coefs, rhs)
    if place is None:
        for j, source in enumerate((direct, swapped)):
            at = pl.multiple_of((core if j == 0 else 1 - core) * rows, rows)
            pltpu.make_async_copy(source.at[pl.ds(0, rows), :], lhs.at[pl.ds(at, rows), :], sems.at[1 + j]).wait()
    else:
        pltpu.make_async_copy(direct.at[pl.ds(0, rows), :], lhs, sems.at[1]).wait()
    if not last:
        out[...] = partial[...] + product(lhs[...], rhs[...])
        return
    result = rest[3]
    copies = []
    width = result.shape[2]
    for i in range(result.shape[0]):
        at = pl.ds(i * width, width)
        result[i] = partial[:, at] + product(lhs[...], rhs[at, :])
        copies.append(pltpu.make_async_copy(result.at[i], out.at[:, at], sems.at[3 + i]))
        copies[-1].start()
    for copy in copies:
        copy.wait()


def kernel_call(body, **options):
    return pl.pallas_call(body, **options)


def local(spectrum, coupling, spatial_basis, noise_keys, noise_counters):
    steps, modes = coupling.shape
    vecs = noise_keys.shape[0]
    tm, space = lax.axis_size("tm"), lax.axis_size("space")
    chips = tm // 2
    nodes_here = spatial_basis.shape[0] // space
    half = nodes_here // 2
    keys, counters = noise_keys.reshape(1, vecs), noise_counters.reshape(1, vecs)
    f32 = lambda *shape: jax.ShapeDtypeStruct(shape, F32)
    bf16 = lambda *shape: jax.ShapeDtypeStruct(shape, BF16)
    fast = dict(compiler_params=LIMIT)
    in_hbm = [
        pltpu.with_memory_space_constraint(x, pltpu.HBM)
        for x in (coupling, spectrum.reshape(1, modes), spatial_basis)
    ]

    pairs, single = partners(space)
    routes = [(d, d) for d in single] + pairs
    sizes = [half + TAIL] * len(single) + [nodes_here + TAIL] * len(pairs)
    other = swap(coupling, "tm", 1)
    *messages, coup, spec = kernel_call(
        functools.partial(pack_kernel, "tm", "space", routes),
        out_shape=[bf16(n, modes) for n in sizes] + [f32(steps, modes), f32(1, modes)],
        in_specs=[HBM] * 3,
        out_specs=[VMEM] * (len(sizes) + 2),
        scratch_shapes=[pltpu.SemaphoreType.DMA((len(sizes) + 2,))],
        **fast,
    )(*in_hbm)
    table, *messages = kernel_call(
        functools.partial(table_kernel, "tm", len(sizes)),
        out_shape=[f32(8, modes)] + [bf16(n, modes) for n in sizes],
        in_specs=[VMEM] * 3 + [ANY] * len(sizes),
        out_specs=[VMEM] + [ANY] * len(sizes),
        scratch_shapes=[pltpu.VMEM((TAIL, modes), BF16), pltpu.SemaphoreType.DMA((len(sizes),))],
        input_output_aliases={3 + i: 1 + i for i in range(len(sizes))},
        **fast,
    )(coup, other, spec, *messages)
    tables = [swap(table, "tm", 2 * e) for e in range(1, chips)]
    direct = [exchange(m, lambda t, s, r=r: (t, s ^ r[t % 2])) for m, r in zip(messages, routes)]

    def noise_of(blocks, after):
        count = len(blocks) * steps * vecs * modes
        return kernel_call(
            functools.partial(noise_kernel, "tm", "space", blocks, len(after)),
            out_shape=[f32(steps, vecs, modes)] * len(blocks),
            in_specs=[VMEM] * 2 + [ANY] * len(after),
            out_specs=[VMEM] * len(blocks),
            scratch_shapes=[pltpu.VMEM((vecs, 128), jnp.int32)],
            cost_estimate=pl.CostEstimate(flops=count * 60, transcendentals=count * 2, bytes_accessed=count * 4),
            **fast,
        )(keys, counters, *after)

    own, paired = noise_of(((0, 0), (1, 0)), (table,))
    total, late, weights, sums = kernel_call(
        functools.partial(offset_kernel, "tm"),
        out_shape=[bf16(vecs, modes), f32(vecs, modes), f32(chips, 8, modes), f32(8, modes)],
        in_specs=[VMEM] * (6 + len(tables)),
        out_specs=[VMEM] * 4,
        scratch_shapes=[pltpu.VMEM((chips, 8, modes), F32)] + [pltpu.VMEM((steps, modes), F32)] * 5,
        **fast,
    )(own, paired, coup, other, spec, table, *tables)
    later = [swap(total, "tm", 2 * e) for e in range(1, chips)]
    third = max(1, (space - 1) // 3)
    parts = [range(1, 1 + third), range(1 + third, 1 + 2 * third), range(1 + 2 * third, space)]
    noise = list(noise_of([(0, d) for d in parts[0]], (total,)))
    noise += noise_of([(0, d) for d in parts[1]], (noise[-1],))
    carry = kernel_call(
        functools.partial(carry_kernel, "tm"),
        out_shape=bf16(vecs + 16, modes),
        in_specs=[VMEM] * (3 + len(later)) + [ANY],
        out_specs=VMEM,
        **fast,
    )(late, weights, sums, *later, noise[-1])
    carries = [swap(carry, "space", d) for d in range(1, space)]
    swapped = [swap(m, "tm", 1) for m in direct]
    noise += noise_of([(0, d) for d in parts[2]], (carry,))

    flops = 2 * nodes_here * modes * steps * vecs
    lhs, rhs = pltpu.VMEM((nodes_here, modes), BF16), pltpu.VMEM((steps * vecs, modes), BF16)
    coefs = [pltpu.VMEM((steps, modes), F32)] * 3
    result = f32(nodes_here, steps * vecs)
    cost = pl.CostEstimate(flops=flops, transcendentals=0, bytes_accessed=4 * steps * vecs * modes)
    out = kernel_call(
        functools.partial(own_kernel, "space"),
        out_shape=result,
        in_specs=[VMEM, VMEM, HBM, VMEM, VMEM],
        out_specs=VMEM,
        scratch_shapes=[lhs, rhs] + coefs + [pltpu.SemaphoreType.DMA],
        cost_estimate=cost,
        **fast,
    )(coup, spec, spatial_basis, own, carry)
    width = 128
    chunks = steps * vecs // width
    order = [(d, 0, None) for d in single]
    order += [(d, len(single) + j, place) for j, pair in enumerate(pairs) for place, d in enumerate(pair)]
    for n, (d, i, place) in enumerate(order):
        last = n == len(order) - 1
        out = kernel_call(
            functools.partial(block_kernel, "tm", place, last),
            out_shape=result,
            in_specs=[VMEM, ANY, ANY, VMEM, VMEM],
            out_specs=HBM if last else VMEM,
            scratch_shapes=[
                lhs,
                rhs,
                pltpu.VMEM((TAIL, modes), BF16),
                pltpu.SemaphoreType.DMA((3 + chunks if last else 3,)),
            ]
            + coefs
            + ([pltpu.VMEM((chunks, nodes_here, width), F32)] if last else []),
            cost_estimate=cost,
            **fast,
        )(out, direct[i], swapped[i], noise[d - 1], carries[d - 1])
    return out


def solution(mesh):
    in_specs = (P("space"), P("tm", "space"), P(None, "space"), P(), P())
    out_specs = P("space", "tm")
    return jax.shard_map(local, mesh=mesh, in_specs=in_specs, out_specs=out_specs, check_vma=False)
```

```python
import functools

import jax
import jax.numpy as jnp
from jax import lax
from jax.experimental import pallas as pl
from jax.experimental.pallas import tpu as pltpu
from jax.sharding import PartitionSpec as P


F32 = jnp.float32
BF16 = jnp.bfloat16
VMEM = pl.BlockSpec(memory_space=pltpu.VMEM)
ANY = pl.BlockSpec(memory_space=pl.ANY)
HBM = pl.BlockSpec(memory_space=pltpu.HBM)
LIMIT = pltpu.CompilerParams(vmem_limit_bytes=48 << 20)
SINE = (6.28318516, -41.34165503, 81.60100406, -76.54978208, 39.53670436)


def partners(count):
    pairs = [(i, i + 1) for i in range(1, count - 2, 2)]
    return pairs, ([count - 1] if count > 1 else [])


def exchange(x, move):
    tm, space = lax.axis_size("tm"), lax.axis_size("space")
    moves = []
    for t in range(tm):
        for s in range(space):
            to = move(t, s)
            if to is not None:
                moves.append((t * space + s, to[0] * space + to[1]))
    return lax.ppermute(x, ("tm", "space"), moves)


def swap(x, axis, offset):
    count = lax.axis_size(axis)
    return lax.ppermute(x, axis, [(i, i ^ offset) for i in range(count)])


def split3(x):
    high = x.astype(BF16).astype(F32)
    rest = x - high
    middle = rest.astype(BF16).astype(F32)
    return high, middle, rest - middle


def mix_bits(state):
    state = state ^ lax.shift_right_logical(state, jnp.int32(16))
    state = state * jnp.int32(-2048144789)
    state = state ^ lax.shift_right_logical(state, jnp.int32(13))
    state = state * jnp.int32(-1028477387)
    return state ^ lax.shift_right_logical(state, jnp.int32(16))


def gaussian(seeded):
    first = mix_bits(seeded)
    second = mix_bits(first + jnp.int32(1013904223))
    unit = (lax.shift_right_logical(first, jnp.int32(8)).astype(F32) + 0.5) * (1.0 / 16777216.0)
    square = -2.0 * jnp.log(unit)
    radius = square * lax.rsqrt(jnp.maximum(square, 1e-30))
    turn = (lax.shift_right_arithmetic(second, jnp.int32(8)).astype(F32) + 0.5) * (1.0 / 16777216.0)
    w = 0.25 - jnp.abs(turn)
    z = w * w
    sine = SINE[4]
    for c in SINE[3::-1]:
        sine = sine * z + c
    return radius * (sine * w)


TAIL = 64


def pick(core, offsets):
    return offsets[0] if offsets[0] == offsets[1] else jnp.where(core == 0, offsets[0], offsets[1])


def pack_kernel(tm_axis, sp_axis, offsets, coup, spec, basis, *rest):
    *outs, coup_out, spec_out, sems = rest
    me, sp = lax.axis_index(tm_axis), lax.axis_index(sp_axis)
    core = lax.rem(me, 2)
    copies = [
        pltpu.make_async_copy(coup, coup_out, sems.at[len(outs)]),
        pltpu.make_async_copy(spec, spec_out, sems.at[len(outs) + 1]),
    ]
    for i, (out, offset) in enumerate(zip(outs, offsets)):
        rows = out.shape[0] - TAIL
        block = sp ^ pick(core, offset)
        if offset[0] == offset[1]:
            block = block * 2 + core
        start = pl.multiple_of(block * rows, rows)
        copies.append(
            pltpu.make_async_copy(basis.at[pl.ds(start, rows), :], out.at[pl.ds(0, rows), :], sems.at[i])
        )
    for copy in copies:
        copy.start()
    for copy in copies:
        copy.wait()


def totals(ref):
    product = square = total = None
    for t in range(ref.shape[0]):
        c = ref[pl.ds(t, 1), :]
        product = c if t == 0 else product * c
        square = c * c if t == 0 else square * (c * c)
        total = square if t == 0 else total + square
    return product, total


def joined(early, late):
    return early[0] * late[0], early[1] + (early[0] * early[0]) * late[1]


def table_rows(shape, rows):
    row = lax.broadcasted_iota(jnp.int32, shape, 0)
    table = jnp.zeros(shape, F32)
    for j, value in enumerate(rows):
        table = jnp.where(row == j, value, table)
    return table


def ordered(first, mine, theirs):
    early = tuple(jnp.where(first, x, y) for x, y in zip(mine, theirs))
    late = tuple(jnp.where(first, y, x) for x, y in zip(mine, theirs))
    return early, late


def table_kernel(tm_axis, count, coup, other, spec, *rest):
    out, *messages, tail, sems = rest[count:]
    first = lax.rem(lax.axis_index(tm_axis), 2) == 0
    (x,), (y,) = ordered(first, (coup[...],), (other[...],))
    parts = split3(x) + split3(y)
    parts = parts + (table_rows(x.shape, split3(spec[...])), jnp.zeros_like(x))
    for j in range(4):
        tail[pl.ds(16 * j, 16), :] = jnp.concatenate(parts[2 * j : 2 * j + 2], 0).astype(BF16)
    copies = []
    for i, message in enumerate(messages):
        rows = message.shape[0] - TAIL
        copies.append(pltpu.make_async_copy(tail, message.at[pl.ds(rows, TAIL), :], sems.at[i]))
        copies[-1].start()
    early, late = ordered(first, totals(coup), totals(other))
    total = joined(early, late)
    out[...] = table_rows(out.shape, (*total, *early, *late, 1.0 + total[1], total[0] * total[0]))
    for copy in copies:
        copy.wait()


def sums_kernel(tm_axis, table, *rest):
    *received, out = rest
    start = start_of(tm_axis, received, out.shape[1])
    total = table[pl.ds(0, 1), :], table[pl.ds(1, 1), :]
    out[...] = table_rows(out.shape, (one_row(out), ) * 6 + after(start, total))


def one_row(ref):
    return jnp.ones((1, ref.shape[1]), F32)


def start_of(tm_axis, received, modes):
    chip = lax.axis_index(tm_axis) // 2
    one = jnp.ones((1, modes), F32)
    start = (one, one)
    for r, ref in enumerate(received):
        start = select(chip == r + 1, (ref[pl.ds(6, 1), :], ref[pl.ds(7, 1), :]), start)
    return start


def noise_kernel(tm_axis, sp_axis, blocks, extras, keys, counters, *rest):
    *outs, base = rest[extras:]
    outs = outs[: len(blocks)]
    steps, vecs, modes = outs[0].shape
    me, sp = lax.axis_index(tm_axis), lax.axis_index(sp_axis)
    diagonal = lax.broadcasted_iota(jnp.int32, (vecs, vecs), 0) == lax.broadcasted_iota(
        jnp.int32, (vecs, vecs), 1
    )

    def column(ref):
        row = jnp.broadcast_to(ref[...].astype(F32), (vecs, vecs))
        return jnp.sum(jnp.where(diagonal, row, 0.0), axis=1, keepdims=True).astype(jnp.int32)

    start = column(keys) * jnp.int32(668265261) + column(counters) * jnp.int32(374761393)
    base[...] = jnp.broadcast_to(start, base.shape)
    group = 8
    for out, (block, offset) in zip(outs, blocks):
        ids = (sp ^ offset) * modes + lax.broadcasted_iota(jnp.int32, (1, modes), 1)
        lane = ids * jnp.int32(-1640531535)
        first_step = (me ^ block) * steps

        def step(t, _):
            shifted = lane + (first_step + t) * jnp.int32(374761393)
            for v in range(vecs // group):
                seeded = jnp.tile(base[pl.ds(v * group, group), :], (1, modes // 128)) + shifted
                out[t, pl.ds(v * group, group), :] = gaussian(seeded)
            return 0

        lax.fori_loop(0, steps, step, 0)


def chain(coup, spec, d_start, f_start):
    before, after = [], []
    square, total = None, None
    d_now = d_start
    for t in range(coup.shape[0]):
        c = coup[t : t + 1, :]
        square = c * c if t == 0 else square * (c * c)
        total = square if t == 0 else total + square
        before.append(d_now)
        d_now = d_start + f_start * total
        after.append(d_now)
    ratio = jnp.concatenate(before, 0) / jnp.concatenate(after, 0)
    return jnp.sqrt(ratio / spec), ratio


def after(start, total):
    return start[0] + start[1] * total[1], start[1] * (total[0] * total[0])


def select(flag, x, y):
    return tuple(jnp.where(flag, p, q) for p, q in zip(x, y))


def gain_of(start, total):
    return total[0] * start[0] / (start[0] + start[1] * total[1])


def offset_kernel(tm_axis, noise_own, noise_other, coup, coup_other, spec, table, *rest):
    received, rest = rest[:-8], rest[-8:]
    o_ref, late_ref, df, *coefs, tmp = rest
    steps, vecs, modes = noise_own.shape
    first = lax.rem(lax.axis_index(tm_axis), 2) == 0
    start = start_of(tm_axis, received, modes)
    early = table[pl.ds(2, 1), :], table[pl.ds(3, 1), :]
    late = table[pl.ds(4, 1), :], table[pl.ds(5, 1), :]
    second = after(start, early)
    gain_early, gain_late = gain_of(start, early), gain_of(second, late)
    df[...] = table_rows((8, modes), (*start, *second, gain_late))
    own, other = ordered(first, start, second)
    for j, (ref, sums) in enumerate(((coup, own), (coup_other, other))):
        c = ref[...]
        a, ratio = chain(c, spec[...], *sums)
        coefs[2 * j][...] = c * a
        coefs[2 * j + 1][...] = c * ratio
    tmp[...] = jnp.broadcast_to(gain_early, tmp.shape)

    def tile(v, _):
        at = pl.ds(pl.multiple_of(v * 16, 16), 16)
        ends = []
        for j, noise in enumerate((noise_own, noise_other)):
            alpha, beta = coefs[2 * j], coefs[2 * j + 1]
            carry = jnp.zeros((16, modes), F32)
            for t in range(steps - 1, -1, -1):
                carry = alpha[pl.ds(t, 1), :] * noise[t, at, :] + beta[pl.ds(t, 1), :] * carry
            ends.append(carry)
        (early,), (late,) = ordered(first, ends[:1], ends[1:])
        o_ref[at, :] = (early + tmp[pl.ds(0, 1), :] * late).astype(BF16)
        late_ref[at, :] = late
        return 0

    lax.fori_loop(0, vecs // 16, tile, 0)
    o_ref[pl.ds(vecs, 16), :] = table_rows((16, modes), split3(gain_early * gain_late)).astype(BF16)


def carry_kernel(tm_axis, late, df, *rest):
    *received, _, out = rest
    vecs, modes = late.shape
    first = lax.rem(lax.axis_index(tm_axis), 2) == 0
    carry = jnp.zeros(late.shape, F32)
    for ref in received[::-1]:
        gain = ref[pl.ds(vecs, 16), :].astype(F32)
        carry = ref[pl.ds(0, vecs), :].astype(F32) + (gain[0:1] + gain[1:2] + gain[2:3]) * carry
    out[pl.ds(0, vecs), :] = jnp.where(first, late[...] + df[pl.ds(4, 1), :] * carry, carry).astype(BF16)
    own = select(first, (df[pl.ds(0, 1), :], df[pl.ds(1, 1), :]), (df[pl.ds(2, 1), :], df[pl.ds(3, 1), :]))
    out[pl.ds(vecs, 16), :] = table_rows((16, modes), split3(own[0]) + split3(own[1])).astype(BF16)


def values(noise, message, c, lam, coefs, rhs):
    steps, vecs, _ = noise.shape
    df = message[pl.ds(vecs, 16), :].astype(F32)
    a, ratio = chain(c, lam, df[0:1] + df[1:2] + df[2:3], df[3:4] + df[4:5] + df[5:6])
    a_ref, ratio_ref, c_ref = coefs
    a_ref[...] = a
    ratio_ref[...] = ratio
    c_ref[...] = c

    def tile(v, _):
        at = pl.ds(pl.multiple_of(v * 16, 16), 16)
        carry = message[at, :].astype(F32)
        for t in range(steps - 1, -1, -1):
            value = a_ref[pl.ds(t, 1), :] * noise[t, at, :] + ratio_ref[pl.ds(t, 1), :] * carry
            if t:
                carry = c_ref[pl.ds(t, 1), :] * value
            rhs[pl.ds(pl.multiple_of(t * vecs + v * 16, 16), 16), :] = value.astype(BF16)
        return 0

    lax.fori_loop(0, vecs // 16, tile, 0)


def product(lhs, rhs):
    return lax.dot_general(lhs, rhs, (((1,), (1,)), ((), ())), preferred_element_type=F32)


def own_kernel(sp_axis, coup, spec, basis, noise, message, out, lhs, rhs, *rest):
    *coefs, sem = rest
    rows = lhs.shape[0]
    start = pl.multiple_of(lax.axis_index(sp_axis) * rows, rows)
    copy = pltpu.make_async_copy(basis.at[pl.ds(start, rows), :], lhs, sem)
    copy.start()
    values(noise, message, coup[...], spec[...], coefs, rhs)
    copy.wait()
    out[...] = product(lhs[...], rhs[...])


def block_kernel(tm_axis, place, last, partial, direct, swapped, noise, message, out, lhs, rhs, tail, sems, *rest):
    coefs = rest[:3]
    core = lax.rem(lax.axis_index(tm_axis), 2)
    rows = direct.shape[0] - TAIL
    if place is None:
        head = pltpu.make_async_copy(direct.at[pl.ds(rows, TAIL), :], tail, sems.at[0])
        head.start()
        for j, source in enumerate((direct, swapped)):
            at = pl.multiple_of((core if j == 0 else 1 - core) * rows, rows)
            pltpu.make_async_copy(source.at[pl.ds(0, rows), :], lhs.at[pl.ds(at, rows), :], sems.at[1 + j]).start()
        head.wait()
    else:
        for j, source in enumerate((direct, swapped)):

            @pl.when((core == place) == (j == 0))
            def _():
                pltpu.make_async_copy(source.at[pl.ds(rows, TAIL), :], tail, sems.at[0]).start()
                pltpu.make_async_copy(source.at[pl.ds(0, rows), :], lhs, sems.at[1]).start()

        pltpu.make_async_copy(direct.at[pl.ds(rows, TAIL), :], tail, sems.at[0]).wait()
    x = [tail[pl.ds(16 * j, 16), :].astype(F32) for j in range(4)]
    early = x[0][0:8] + x[0][8:16] + x[1][0:8]
    late = x[1][8:16] + x[2][0:8] + x[2][8:16]
    c = jnp.where(core == 0, early, late)
    values(noise, message, c, x[3][0:1] + x[3][1:2] + x[3][2:3], coefs, rhs)
    if place is None:
        for j, source in enumerate((direct, swapped)):
            at = pl.multiple_of((core if j == 0 else 1 - core) * rows, rows)
            pltpu.make_async_copy(source.at[pl.ds(0, rows), :], lhs.at[pl.ds(at, rows), :], sems.at[1 + j]).wait()
    else:
        pltpu.make_async_copy(direct.at[pl.ds(0, rows), :], lhs, sems.at[1]).wait()
    if not last:
        out[...] = partial[...] + product(lhs[...], rhs[...])
        return
    result = rest[3]
    copies = []
    width = result.shape[2]
    for i in range(result.shape[0]):
        at = pl.ds(i * width, width)
        result[i] = partial[:, at] + product(lhs[...], rhs[at, :])
        copies.append(pltpu.make_async_copy(result.at[i], out.at[:, at], sems.at[3 + i]))
        copies[-1].start()
    for copy in copies:
        copy.wait()


def kernel_call(body, **options):
    return pl.pallas_call(body, **options)


def local(spectrum, coupling, spatial_basis, noise_keys, noise_counters):
    steps, modes = coupling.shape
    vecs = noise_keys.shape[0]
    tm, space = lax.axis_size("tm"), lax.axis_size("space")
    chips = tm // 2
    nodes_here = spatial_basis.shape[0] // space
    half = nodes_here // 2
    keys, counters = noise_keys.reshape(1, vecs), noise_counters.reshape(1, vecs)
    f32 = lambda *shape: jax.ShapeDtypeStruct(shape, F32)
    bf16 = lambda *shape: jax.ShapeDtypeStruct(shape, BF16)
    fast = dict(compiler_params=LIMIT)
    in_hbm = [
        pltpu.with_memory_space_constraint(x, pltpu.HBM)
        for x in (coupling, spectrum.reshape(1, modes), spatial_basis)
    ]

    pairs, single = partners(space)
    routes = [(d, d) for d in single] + pairs
    sizes = [half + TAIL] * len(single) + [nodes_here + TAIL] * len(pairs)
    other = swap(coupling, "tm", 1)
    *messages, coup, spec = kernel_call(
        functools.partial(pack_kernel, "tm", "space", routes),
        out_shape=[bf16(n, modes) for n in sizes] + [f32(steps, modes), f32(1, modes)],
        in_specs=[HBM] * 3,
        out_specs=[VMEM] * (len(sizes) + 2),
        scratch_shapes=[pltpu.SemaphoreType.DMA((len(sizes) + 2,))],
        **fast,
    )(*in_hbm)
    table, *messages = kernel_call(
        functools.partial(table_kernel, "tm", len(sizes)),
        out_shape=[f32(8, modes)] + [bf16(n, modes) for n in sizes],
        in_specs=[VMEM] * 3 + [ANY] * len(sizes),
        out_specs=[VMEM] + [ANY] * len(sizes),
        scratch_shapes=[pltpu.VMEM((TAIL, modes), BF16), pltpu.SemaphoreType.DMA((len(sizes),))],
        input_output_aliases={3 + i: 1 + i for i in range(len(sizes))},
        **fast,
    )(coup, other, spec, *messages)
    direct = [exchange(m, lambda t, s, r=r: (t, s ^ r[t % 2])) for m, r in zip(messages, routes)]

    def noise_of(blocks, after):
        count = len(blocks) * steps * vecs * modes
        return kernel_call(
            functools.partial(noise_kernel, "tm", "space", blocks, len(after)),
            out_shape=[f32(steps, vecs, modes)] * len(blocks),
            in_specs=[VMEM] * 2 + [ANY] * len(after),
            out_specs=[VMEM] * len(blocks),
            scratch_shapes=[pltpu.VMEM((vecs, 128), jnp.int32)],
            cost_estimate=pl.CostEstimate(flops=count * 60, transcendentals=count * 2, bytes_accessed=count * 4),
            **fast,
        )(keys, counters, *after)

    received, chip_noise, message = [], [], table
    for r in range(chips - 1):
        received.append(exchange(message, lambda t, s: (t + 2, s) if t // 2 == r else None))
        if 1 <= r <= 2:
            chip_noise += noise_of([(r - 1, 0)], (message,))
        if r < chips - 2:
            message = kernel_call(
                functools.partial(sums_kernel, "tm"),
                out_shape=f32(8, modes),
                in_specs=[VMEM] * (1 + len(received)),
                out_specs=VMEM,
                **fast,
            )(table, *received)
    for r in range(len(chip_noise), 2):
        chip_noise += noise_of([(r, 0)], (message,))
    own, paired = chip_noise
    total, late, sums = kernel_call(
        functools.partial(offset_kernel, "tm"),
        out_shape=[bf16(vecs + 16, modes), f32(vecs, modes), f32(8, modes)],
        in_specs=[VMEM] * (6 + len(received)),
        out_specs=[VMEM] * 3,
        scratch_shapes=[pltpu.VMEM((steps, modes), F32)] * 5,
        **fast,
    )(own, paired, coup, other, spec, table, *received)
    later = [exchange(total, lambda t, s: (t - 2 * e, s) if t >= 2 * e else None) for e in range(1, chips)]
    third = max(1, (space - 1) // 3)
    parts = [range(1, 1 + third), range(1 + third, 1 + 2 * third), range(1 + 2 * third, space)]
    noise = list(noise_of([(0, d) for d in parts[0]], (total,)))
    noise += noise_of([(0, d) for d in parts[1]], (noise[-1],))
    noise += noise_of([(0, d) for d in parts[2]], (noise[-1],))
    carry = kernel_call(
        functools.partial(carry_kernel, "tm"),
        out_shape=bf16(vecs + 16, modes),
        in_specs=[VMEM] * (2 + len(later)) + [ANY],
        out_specs=VMEM,
        **fast,
    )(late, sums, *later, noise[-1])
    carries = [swap(carry, "space", d) for d in range(1, space)]
    swapped = [swap(m, "tm", 1) for m in direct]

    flops = 2 * nodes_here * modes * steps * vecs
    lhs, rhs = pltpu.VMEM((nodes_here, modes), BF16), pltpu.VMEM((steps * vecs, modes), BF16)
    coefs = [pltpu.VMEM((steps, modes), F32)] * 3
    result = f32(nodes_here, steps * vecs)
    cost = pl.CostEstimate(flops=flops, transcendentals=0, bytes_accessed=4 * steps * vecs * modes)
    out = kernel_call(
        functools.partial(own_kernel, "space"),
        out_shape=result,
        in_specs=[VMEM, VMEM, HBM, VMEM, VMEM],
        out_specs=VMEM,
        scratch_shapes=[lhs, rhs] + coefs + [pltpu.SemaphoreType.DMA],
        cost_estimate=cost,
        **fast,
    )(coup, spec, spatial_basis, own, carry)
    width = 128
    chunks = steps * vecs // width
    order = [(d, 0, None) for d in single]
    order += [(d, len(single) + j, place) for j, pair in enumerate(pairs) for place, d in enumerate(pair)]
    for n, (d, i, place) in enumerate(order):
        last = n == len(order) - 1
        out = kernel_call(
            functools.partial(block_kernel, "tm", place, last),
            out_shape=result,
            in_specs=[VMEM, ANY, ANY, VMEM, VMEM],
            out_specs=HBM if last else VMEM,
            scratch_shapes=[
                lhs,
                rhs,
                pltpu.VMEM((TAIL, modes), BF16),
                pltpu.SemaphoreType.DMA((3 + chunks if last else 3,)),
            ]
            + coefs
            + ([pltpu.VMEM((chunks, nodes_here, width), F32)] if last else []),
            cost_estimate=cost,
            **fast,
        )(out, direct[i], swapped[i], noise[d - 1], carries[d - 1])
    return out


def solution(mesh):
    in_specs = (P("space"), P("tm", "space"), P(None, "space"), P(), P())
    out_specs = P("space", "tm")
    return jax.shard_map(local, mesh=mesh, in_specs=in_specs, out_specs=out_specs, check_vma=False)
```

```python
import functools

import jax
import jax.numpy as jnp
from jax import lax
from jax.experimental import pallas as pl
from jax.experimental.pallas import tpu as pltpu
from jax.sharding import PartitionSpec as P


F32 = jnp.float32
BF16 = jnp.bfloat16
VMEM = pl.BlockSpec(memory_space=pltpu.VMEM)
ANY = pl.BlockSpec(memory_space=pl.ANY)
HBM = pl.BlockSpec(memory_space=pltpu.HBM)
LIMIT = pltpu.CompilerParams(vmem_limit_bytes=24 << 20)
SINE = (6.28318516, -41.34165503, 81.60100406, -76.54978208, 39.53670436)


def partners(count):
    pairs = [(i, i + 1) for i in range(1, count - 2, 2)]
    return pairs, ([count - 1] if count > 1 else [])


def exchange(x, move):
    tm, space = lax.axis_size("tm"), lax.axis_size("space")
    moves = []
    for t in range(tm):
        for s in range(space):
            to = move(t, s)
            if to is not None:
                moves.append((t * space + s, to[0] * space + to[1]))
    return lax.ppermute(x, ("tm", "space"), moves)


def swap(x, axis, offset):
    count = lax.axis_size(axis)
    return lax.ppermute(x, axis, [(i, i ^ offset) for i in range(count)])


def split3(x):
    high = x.astype(BF16).astype(F32)
    rest = x - high
    middle = rest.astype(BF16).astype(F32)
    return high, middle, rest - middle


def mix_bits(state):
    state = state ^ lax.shift_right_logical(state, jnp.int32(16))
    state = state * jnp.int32(-2048144789)
    state = state ^ lax.shift_right_logical(state, jnp.int32(13))
    state = state * jnp.int32(-1028477387)
    return state ^ lax.shift_right_logical(state, jnp.int32(16))


def gaussian(seeded):
    first = mix_bits(seeded)
    second = mix_bits(first + jnp.int32(1013904223))
    unit = (lax.shift_right_logical(first, jnp.int32(8)).astype(F32) + 0.5) * (1.0 / 16777216.0)
    square = -2.0 * jnp.log(unit)
    radius = square * lax.rsqrt(jnp.maximum(square, 1e-30))
    turn = (lax.shift_right_arithmetic(second, jnp.int32(8)).astype(F32) + 0.5) * (1.0 / 16777216.0)
    w = 0.25 - jnp.abs(turn)
    z = w * w
    sine = SINE[4]
    for c in SINE[3::-1]:
        sine = sine * z + c
    return radius * (sine * w)


TAIL = 64


def pick(core, offsets):
    return offsets[0] if offsets[0] == offsets[1] else jnp.where(core == 0, offsets[0], offsets[1])


def pack_kernel(tm_axis, sp_axis, offsets, coup, spec, basis, *rest):
    *outs, coup_out, spec_out, sems = rest
    me, sp = lax.axis_index(tm_axis), lax.axis_index(sp_axis)
    core = lax.rem(me, 2)
    copies = [
        pltpu.make_async_copy(coup, coup_out, sems.at[len(outs)]),
        pltpu.make_async_copy(spec, spec_out, sems.at[len(outs) + 1]),
    ]
    for i, (out, offset) in enumerate(zip(outs, offsets)):
        rows = out.shape[0] - TAIL
        block = sp ^ pick(core, offset)
        if offset[0] == offset[1]:
            block = block * 2 + core
        start = pl.multiple_of(block * rows, rows)
        copies.append(
            pltpu.make_async_copy(basis.at[pl.ds(start, rows), :], out.at[pl.ds(0, rows), :], sems.at[i])
        )
    for copy in copies:
        copy.start()
    for copy in copies:
        copy.wait()


def totals(ref):
    product = square = total = None
    for t in range(ref.shape[0]):
        c = ref[pl.ds(t, 1), :]
        product = c if t == 0 else product * c
        square = c * c if t == 0 else square * (c * c)
        total = square if t == 0 else total + square
    return product, total


def joined(early, late):
    return early[0] * late[0], early[1] + (early[0] * early[0]) * late[1]


def table_rows(shape, rows):
    row = lax.broadcasted_iota(jnp.int32, shape, 0)
    table = jnp.zeros(shape, F32)
    for j, value in enumerate(rows):
        table = jnp.where(row == j, value, table)
    return table


def ordered(first, mine, theirs):
    early = tuple(jnp.where(first, x, y) for x, y in zip(mine, theirs))
    late = tuple(jnp.where(first, y, x) for x, y in zip(mine, theirs))
    return early, late


def table_kernel(tm_axis, count, coup, other, spec, *rest):
    out, *messages, tail, sems = rest[count:]
    first = lax.rem(lax.axis_index(tm_axis), 2) == 0
    (x,), (y,) = ordered(first, (coup[...],), (other[...],))
    parts = split3(x) + split3(y)
    parts = parts + (table_rows(x.shape, split3(spec[...])), jnp.zeros_like(x))
    for j in range(4):
        tail[pl.ds(16 * j, 16), :] = jnp.concatenate(parts[2 * j : 2 * j + 2], 0).astype(BF16)
    copies = []
    for i, message in enumerate(messages):
        rows = message.shape[0] - TAIL
        copies.append(pltpu.make_async_copy(tail, message.at[pl.ds(rows, TAIL), :], sems.at[i]))
        copies[-1].start()
    early, late = ordered(first, totals(coup), totals(other))
    out[...] = table_rows(out.shape, (*joined(early, late), *early, *late))
    for copy in copies:
        copy.wait()


def noise_kernel(tm_axis, sp_axis, blocks, extras, keys, counters, *rest):
    *outs, base = rest[extras:]
    outs = outs[: len(blocks)]
    steps, vecs, modes = outs[0].shape
    me, sp = lax.axis_index(tm_axis), lax.axis_index(sp_axis)
    diagonal = lax.broadcasted_iota(jnp.int32, (vecs, vecs), 0) == lax.broadcasted_iota(
        jnp.int32, (vecs, vecs), 1
    )

    def column(ref):
        row = jnp.broadcast_to(ref[...].astype(F32), (vecs, vecs))
        return jnp.sum(jnp.where(diagonal, row, 0.0), axis=1, keepdims=True).astype(jnp.int32)

    start = column(keys) * jnp.int32(668265261) + column(counters) * jnp.int32(374761393)
    base[...] = jnp.broadcast_to(start, base.shape)
    group = 8
    for out, (block, offset) in zip(outs, blocks):
        ids = (sp ^ pick(lax.rem(me, 2), offset)) * modes + lax.broadcasted_iota(jnp.int32, (1, modes), 1)
        lane = ids * jnp.int32(-1640531535)
        first_step = (me ^ block) * steps

        def step(t, _):
            shifted = lane + (first_step + t) * jnp.int32(374761393)
            for v in range(vecs // group):
                seeded = jnp.tile(base[pl.ds(v * group, group), :], (1, modes // 128)) + shifted
                out[t, pl.ds(v * group, group), :] = gaussian(seeded)
            return 0

        lax.fori_loop(0, steps, step, 0)


def chain(coup, spec, d_start, f_start):
    before, after = [], []
    square, total = None, None
    d_now = d_start
    for t in range(coup.shape[0]):
        c = coup[t : t + 1, :]
        square = c * c if t == 0 else square * (c * c)
        total = square if t == 0 else total + square
        before.append(d_now)
        d_now = d_start + f_start * total
        after.append(d_now)
    ratio = jnp.concatenate(before, 0) / jnp.concatenate(after, 0)
    return jnp.sqrt(ratio / spec), ratio


def after(start, total):
    return start[0] + start[1] * total[1], start[1] * (total[0] * total[0])


def select(flag, x, y):
    return tuple(jnp.where(flag, p, q) for p, q in zip(x, y))


def gain_of(start, total):
    return total[0] * start[0] / (start[0] + start[1] * total[1])


def offset_kernel(tm_axis, noise_own, noise_other, coup, coup_other, spec, table, *rest):
    received, rest = rest[:-10], rest[-10:]
    o_ref, late_ref, wts, df, tables, *coefs, tmp = rest
    steps, vecs, modes = noise_own.shape
    me = lax.axis_index(tm_axis)
    chip = me // 2
    first = lax.rem(me, 2) == 0
    one = jnp.ones((1, modes), F32)
    tables[chip] = table[...]
    for e, ref in enumerate(received):
        tables[chip ^ (e + 1)] = ref[...]
    now, start, weight = (one, one), (one, one), jnp.zeros((1, modes), F32)
    for b in range(tables.shape[0]):
        wts[b] = jnp.broadcast_to(weight, (8, modes))
        total = tables[b, pl.ds(0, 1), :], tables[b, pl.ds(1, 1), :]
        here = chip == b
        start = select(here, now, start)
        weight = jnp.where(here, 1.0, weight * gain_of(now, total))
        now = after(now, total)
    early = table[pl.ds(2, 1), :], table[pl.ds(3, 1), :]
    late = table[pl.ds(4, 1), :], table[pl.ds(5, 1), :]
    second = after(start, early)
    gain_early, gain_late = gain_of(start, early), gain_of(second, late)
    df[...] = table_rows((8, modes), (*start, *second, gain_late))
    own, other = ordered(first, start, second)
    for j, (ref, sums) in enumerate(((coup, own), (coup_other, other))):
        c = ref[...]
        a, ratio = chain(c, spec[...], *sums)
        coefs[2 * j][...] = c * a
        coefs[2 * j + 1][...] = c * ratio
    tmp[...] = jnp.broadcast_to(gain_early, tmp.shape)

    def tile(v, _):
        at = pl.ds(pl.multiple_of(v * 16, 16), 16)
        ends = []
        for j, noise in enumerate((noise_own, noise_other)):
            alpha, beta = coefs[2 * j], coefs[2 * j + 1]
            carry = jnp.zeros((16, modes), F32)
            for t in range(steps - 1, -1, -1):
                carry = alpha[pl.ds(t, 1), :] * noise[t, at, :] + beta[pl.ds(t, 1), :] * carry
            ends.append(carry)
        (early,), (late,) = ordered(first, ends[:1], ends[1:])
        o_ref[at, :] = (early + tmp[pl.ds(0, 1), :] * late).astype(BF16)
        late_ref[at, :] = late
        return 0

    lax.fori_loop(0, vecs // 16, tile, 0)


def carry_kernel(tm_axis, late, wts, df, *rest):
    *received, _, out = rest
    vecs, modes = late.shape
    me = lax.axis_index(tm_axis)
    first = lax.rem(me, 2) == 0
    carry = jnp.zeros(late.shape, F32)
    for e, ref in enumerate(received):
        carry = carry + wts[(me // 2) ^ (e + 1)][0:1, :] * ref[...].astype(F32)
    out[pl.ds(0, vecs), :] = jnp.where(first, late[...] + df[pl.ds(4, 1), :] * carry, carry).astype(BF16)
    own = select(first, (df[pl.ds(0, 1), :], df[pl.ds(1, 1), :]), (df[pl.ds(2, 1), :], df[pl.ds(3, 1), :]))
    out[pl.ds(vecs, 16), :] = table_rows((16, modes), split3(own[0]) + split3(own[1])).astype(BF16)


def sums_of(block):
    return block[0:1] + block[1:2] + block[2:3], block[3:4] + block[4:5] + block[5:6]


def set_coefs(coefs, c, lam, sums):
    a, ratio = chain(c, lam, *sums)
    coefs[0] = a
    coefs[1] = ratio
    coefs[2] = c


def values(noise, start, coefs, state, rhs, times):
    vecs = noise.shape[1]
    for v in range(0, vecs, 16):
        at = pl.ds(v, 16)
        carry = start(at)
        for n, t in enumerate(times):
            row = pl.ds(t, 1)
            value = coefs[0, row, :] * noise[t, at, :] + coefs[1, row, :] * carry
            if t:
                carry = coefs[2, row, :] * value
            rhs[pl.ds((len(times) - 1 - n) * vecs + v, 16), :] = value.astype(BF16)
        if times[-1]:
            state[at, :] = carry


def product(lhs, rhs):
    return lax.dot_general(lhs, rhs, (((1,), (1,)), ((), ())), preferred_element_type=F32)


def halves_of(steps):
    times = list(range(steps - 1, -1, -1))
    return times[: steps // 2], times[steps // 2 :]


def own_kernel(sp_axis, coup, spec, basis, noise, message, out, lhs, rhs, state, coefs, sem):
    rows = lhs.shape[0]
    steps, vecs, _ = noise.shape
    start = pl.multiple_of(lax.axis_index(sp_axis) * rows, rows)
    copy = pltpu.make_async_copy(basis.at[pl.ds(start, rows), :], lhs, sem)
    copy.start()
    set_coefs(coefs, coup[...], spec[...], sums_of(message[pl.ds(vecs, 16), :].astype(F32)))
    late, early = halves_of(steps)
    width = vecs * len(late)
    values(noise, lambda at: message[at, :].astype(F32), coefs, state, rhs.at[0], late)
    copy.wait()
    values(noise, lambda at: state[at, :], coefs, state, rhs.at[1], early)
    out[:, pl.ds(width, width)] = product(lhs[...], rhs[0])
    out[:, pl.ds(0, width)] = product(lhs[...], rhs[1])


def final_kernel(tm_axis, pairs, single, partial, *rest):
    fetched = len(pairs) + len(single)
    count = 2 * len(pairs) + len(single)
    direct, rest = rest[:fetched], rest[fetched:]
    swapped, rest = rest[:fetched], rest[fetched:]
    noise, rest = rest[:count], rest[count:]
    messages, rest = rest[:count], rest[count:]
    out, lhs, rhs, state, coefs, result, sems = rest
    steps, vecs, _ = noise[0].shape
    core = lax.rem(lax.axis_index(tm_axis), 2)
    first = core == 0
    copies = []
    for i in range(len(single)):
        rows = lhs.shape[1] // 2
        for j, source in enumerate((direct[i], swapped[i])):
            at = pl.multiple_of((core if j == 0 else 1 - core) * rows, rows)
            copies.append(
                pltpu.make_async_copy(
                    source.at[pl.ds(0, rows), :], lhs.at[i, pl.ds(at, rows), :], sems.at[2 * i + j]
                )
            )
            copies[-1].start()

    def chosen(x, y):
        return lambda at: jnp.where(first, messages[x][at, :].astype(F32), messages[y][at, :].astype(F32))

    items = []
    for j, (x, y) in enumerate(pairs):
        i = len(single) + j
        rows = direct[i].shape[0] - TAIL
        near = lambda i=i, rows=rows: direct[i][pl.ds(0, rows), :]
        far = lambda i=i, rows=rows: swapped[i][pl.ds(0, rows), :]
        items.append((near, direct[i], noise[len(single) + j], chosen(x - 1, y - 1)))
        items.append((far, swapped[i], noise[len(single) + len(pairs) + j], chosen(y - 1, x - 1)))
    for i, d in enumerate(single):
        items.append((lambda i=i: lhs[i], direct[i], noise[i], chosen(d - 1, d - 1)))
    for n, (_, source, _, message) in enumerate(items):
        rows = source.shape[0] - TAIL
        x = [source[pl.ds(rows + 16 * j, 16), :].astype(F32) for j in range(4)]
        before = x[0][0:8] + x[0][8:16] + x[1][0:8]
        behind = x[1][8:16] + x[2][0:8] + x[2][8:16]
        lam = x[3][0:1] + x[3][1:2] + x[3][2:3]
        set_coefs(coefs.at[n], jnp.where(first, before, behind), lam, sums_of(message(pl.ds(vecs, 16))))
    late, early = halves_of(steps)
    width = vecs * len(late)
    work = [(h, n) for h in range(2) for n in range(count)]

    def fill(h, n):
        start = items[n][3] if h == 0 else lambda at: state[n, at, :]
        values(items[n][2], start, coefs.at[n], state.at[n], rhs.at[h, n], late if h == 0 else early)

    fill(*work[0])
    outs = []
    for k, (h, n) in enumerate(work):
        if k + 1 < len(work):
            fill(*work[k + 1])
        if h == 0 and n == count - len(single):
            for copy in copies:
                copy.wait()
        term = product(items[n][0](), rhs[h, n])
        at = pl.ds((1 - h) * width, width)
        result[h] = (partial[:, at] if n == 0 else result[h]) + term
        if n == count - 1:
            outs.append(pltpu.make_async_copy(result.at[h], out.at[:, at], sems.at[2 * len(single) + h]))
            outs[-1].start()
    for copy in outs:
        copy.wait()


def kernel_call(body, **options):
    return pl.pallas_call(body, **options)


def local(spectrum, coupling, spatial_basis, noise_keys, noise_counters):
    steps, modes = coupling.shape
    vecs = noise_keys.shape[0]
    tm, space = lax.axis_size("tm"), lax.axis_size("space")
    chips = tm // 2
    nodes_here = spatial_basis.shape[0] // space
    half = nodes_here // 2
    keys, counters = noise_keys.reshape(1, vecs), noise_counters.reshape(1, vecs)
    f32 = lambda *shape: jax.ShapeDtypeStruct(shape, F32)
    bf16 = lambda *shape: jax.ShapeDtypeStruct(shape, BF16)
    fast = dict(compiler_params=LIMIT)
    in_hbm = [
        pltpu.with_memory_space_constraint(x, pltpu.HBM)
        for x in (coupling, spectrum.reshape(1, modes), spatial_basis)
    ]

    pairs, single = partners(space)
    routes = [(d, d) for d in single] + pairs
    sizes = [half + TAIL] * len(single) + [nodes_here + TAIL] * len(pairs)
    other = swap(coupling, "tm", 1)
    *messages, coup, spec = kernel_call(
        functools.partial(pack_kernel, "tm", "space", routes),
        out_shape=[bf16(n, modes) for n in sizes] + [f32(steps, modes), f32(1, modes)],
        in_specs=[HBM] * 3,
        out_specs=[VMEM] * (len(sizes) + 2),
        scratch_shapes=[pltpu.SemaphoreType.DMA((len(sizes) + 2,))],
        **fast,
    )(*in_hbm)
    table, *messages = kernel_call(
        functools.partial(table_kernel, "tm", len(sizes)),
        out_shape=[f32(8, modes)] + [bf16(n, modes) for n in sizes],
        in_specs=[VMEM] * 3 + [ANY] * len(sizes),
        out_specs=[VMEM] + [ANY] * len(sizes),
        scratch_shapes=[pltpu.VMEM((TAIL, modes), BF16), pltpu.SemaphoreType.DMA((len(sizes),))],
        input_output_aliases={3 + i: 1 + i for i in range(len(sizes))},
        **fast,
    )(coup, other, spec, *messages)
    tables = [swap(table, "tm", 2 * e) for e in range(1, chips)]
    direct = [exchange(m, lambda t, s, r=r: (t, s ^ r[t % 2])) for m, r in zip(messages, routes)]

    def noise_of(blocks, after):
        count = len(blocks) * steps * vecs * modes
        return kernel_call(
            functools.partial(noise_kernel, "tm", "space", blocks, len(after)),
            out_shape=[f32(steps, vecs, modes)] * len(blocks),
            in_specs=[VMEM] * 2 + [ANY] * len(after),
            out_specs=[VMEM] * len(blocks),
            scratch_shapes=[pltpu.VMEM((vecs, 128), jnp.int32)],
            cost_estimate=pl.CostEstimate(flops=count * 60, transcendentals=count * 2, bytes_accessed=count * 4),
            **fast,
        )(keys, counters, *after)

    own, paired = noise_of(((0, (0, 0)), (1, (0, 0))), (table,))
    total, late, weights, sums = kernel_call(
        functools.partial(offset_kernel, "tm"),
        out_shape=[bf16(vecs, modes), f32(vecs, modes), f32(chips, 8, modes), f32(8, modes)],
        in_specs=[VMEM] * (6 + len(tables)),
        out_specs=[VMEM] * 4,
        scratch_shapes=[pltpu.VMEM((chips, 8, modes), F32)] + [pltpu.VMEM((steps, modes), F32)] * 5,
        **fast,
    )(own, paired, coup, other, spec, table, *tables)
    later = [swap(total, "tm", 2 * e) for e in range(1, chips)]
    noise = noise_of([(0, (d, d)) for d in single], (total,))
    noise += noise_of([(0, r) for r in pairs], (noise[-1],))
    carry = kernel_call(
        functools.partial(carry_kernel, "tm"),
        out_shape=bf16(vecs + 16, modes),
        in_specs=[VMEM] * (3 + len(later)) + [ANY],
        out_specs=VMEM,
        **fast,
    )(late, weights, sums, *later, noise[-1])
    carries = [swap(carry, "space", d) for d in range(1, space)]
    swapped = [swap(m, "tm", 1) for m in direct]
    noise += noise_of([(0, r[::-1]) for r in pairs], (carry,))

    flops = 2 * nodes_here * modes * steps * vecs
    half_cols = steps // 2 * vecs
    result = f32(nodes_here, steps * vecs)
    out = kernel_call(
        functools.partial(own_kernel, "space"),
        out_shape=result,
        in_specs=[VMEM, VMEM, HBM, VMEM, VMEM],
        out_specs=VMEM,
        scratch_shapes=[
            pltpu.VMEM((nodes_here, modes), BF16),
            pltpu.VMEM((2, half_cols, modes), BF16),
            pltpu.VMEM((vecs, modes), F32),
            pltpu.VMEM((3, steps, modes), F32),
            pltpu.SemaphoreType.DMA,
        ],
        cost_estimate=pl.CostEstimate(flops=flops, transcendentals=0, bytes_accessed=4 * steps * vecs * modes),
        **fast,
    )(coup, spec, spatial_basis, own, carry)
    count = space - 1
    return kernel_call(
        functools.partial(final_kernel, "tm", pairs, single),
        out_shape=result,
        in_specs=[VMEM] * (1 + len(direct) + len(swapped) + len(noise) + len(carries)),
        out_specs=HBM,
        scratch_shapes=[
            pltpu.VMEM((len(single), nodes_here, modes), BF16),
            pltpu.VMEM((2, count, half_cols, modes), BF16),
            pltpu.VMEM((count, vecs, modes), F32),
            pltpu.VMEM((count, 3, steps, modes), F32),
            pltpu.VMEM((2, nodes_here, half_cols), F32),
            pltpu.SemaphoreType.DMA((2 * len(single) + 2,)),
        ],
        cost_estimate=pl.CostEstimate(
            flops=flops * count, transcendentals=0, bytes_accessed=4 * steps * vecs * modes * count
        ),
        **fast,
    )(out, *direct, *swapped, *noise, *carries)


def solution(mesh):
    in_specs = (P("space"), P("tm", "space"), P(None, "space"), P(), P())
    out_specs = P("space", "tm")
    return jax.shard_map(local, mesh=mesh, in_specs=in_specs, out_specs=out_specs, check_vma=False)
```

```python
import functools

import jax
import jax.numpy as jnp
from jax import lax
from jax.experimental import pallas as pl
from jax.experimental.pallas import tpu as pltpu
from jax.sharding import PartitionSpec as P


F32 = jnp.float32
BF16 = jnp.bfloat16
VMEM = pl.BlockSpec(memory_space=pltpu.VMEM)
ANY = pl.BlockSpec(memory_space=pl.ANY)
HBM = pl.BlockSpec(memory_space=pltpu.HBM)
LIMIT = pltpu.CompilerParams(vmem_limit_bytes=24 << 20)
SINE = (6.28318516, -41.34165503, 81.60100406, -76.54978208, 39.53670436)


def partners(count):
    pairs = [(i, i + 1) for i in range(1, count - 2, 2)]
    return pairs, ([count - 1] if count > 1 else [])


def exchange(x, move):
    tm, space = lax.axis_size("tm"), lax.axis_size("space")
    moves = []
    for t in range(tm):
        for s in range(space):
            to = move(t, s)
            if to is not None:
                moves.append((t * space + s, to[0] * space + to[1]))
    return lax.ppermute(x, ("tm", "space"), moves)


def swap(x, axis, offset):
    count = lax.axis_size(axis)
    return lax.ppermute(x, axis, [(i, i ^ offset) for i in range(count)])


def split3(x):
    high = x.astype(BF16).astype(F32)
    rest = x - high
    middle = rest.astype(BF16).astype(F32)
    return high, middle, rest - middle


def mix_bits(state):
    state = state ^ lax.shift_right_logical(state, jnp.int32(16))
    state = state * jnp.int32(-2048144789)
    state = state ^ lax.shift_right_logical(state, jnp.int32(13))
    state = state * jnp.int32(-1028477387)
    return state ^ lax.shift_right_logical(state, jnp.int32(16))


def gaussian(seeded):
    first = mix_bits(seeded)
    second = mix_bits(first + jnp.int32(1013904223))
    unit = (lax.shift_right_logical(first, jnp.int32(8)).astype(F32) + 0.5) * (1.0 / 16777216.0)
    square = -2.0 * jnp.log(unit)
    radius = square * lax.rsqrt(jnp.maximum(square, 1e-30))
    turn = (lax.shift_right_arithmetic(second, jnp.int32(8)).astype(F32) + 0.5) * (1.0 / 16777216.0)
    w = 0.25 - jnp.abs(turn)
    z = w * w
    sine = SINE[4]
    for c in SINE[3::-1]:
        sine = sine * z + c
    return radius * (sine * w)


TAIL = 64


def pick(core, offsets):
    return offsets[0] if offsets[0] == offsets[1] else jnp.where(core == 0, offsets[0], offsets[1])


def pack_kernel(tm_axis, sp_axis, offsets, coup, spec, basis, *rest):
    *outs, coup_out, spec_out, sems = rest
    me, sp = lax.axis_index(tm_axis), lax.axis_index(sp_axis)
    core = lax.rem(me, 2)
    copies = [
        pltpu.make_async_copy(coup, coup_out, sems.at[len(outs)]),
        pltpu.make_async_copy(spec, spec_out, sems.at[len(outs) + 1]),
    ]
    for i, (out, offset) in enumerate(zip(outs, offsets)):
        rows = out.shape[0] - TAIL
        block = sp ^ pick(core, offset)
        if offset[0] == offset[1]:
            block = block * 2 + core
        start = pl.multiple_of(block * rows, rows)
        copies.append(
            pltpu.make_async_copy(basis.at[pl.ds(start, rows), :], out.at[pl.ds(0, rows), :], sems.at[i])
        )
    for copy in copies:
        copy.start()
    for copy in copies:
        copy.wait()


def totals(ref):
    product = square = total = None
    for t in range(ref.shape[0]):
        c = ref[pl.ds(t, 1), :]
        product = c if t == 0 else product * c
        square = c * c if t == 0 else square * (c * c)
        total = square if t == 0 else total + square
    return product, total


def joined(early, late):
    return early[0] * late[0], early[1] + (early[0] * early[0]) * late[1]


def table_rows(shape, rows):
    row = lax.broadcasted_iota(jnp.int32, shape, 0)
    table = jnp.zeros(shape, F32)
    for j, value in enumerate(rows):
        table = jnp.where(row == j, value, table)
    return table


def ordered(first, mine, theirs):
    early = tuple(jnp.where(first, x, y) for x, y in zip(mine, theirs))
    late = tuple(jnp.where(first, y, x) for x, y in zip(mine, theirs))
    return early, late


def table_kernel(tm_axis, count, coup, other, spec, *rest):
    out, *messages, tail, sems = rest[count:]
    first = lax.rem(lax.axis_index(tm_axis), 2) == 0
    (x,), (y,) = ordered(first, (coup[...],), (other[...],))
    parts = split3(x) + split3(y)
    parts = parts + (table_rows(x.shape, split3(spec[...])), jnp.zeros_like(x))
    for j in range(4):
        tail[pl.ds(16 * j, 16), :] = jnp.concatenate(parts[2 * j : 2 * j + 2], 0).astype(BF16)
    copies = []
    for i, message in enumerate(messages):
        rows = message.shape[0] - TAIL
        copies.append(pltpu.make_async_copy(tail, message.at[pl.ds(rows, TAIL), :], sems.at[i]))
        copies[-1].start()
    early, late = ordered(first, totals(coup), totals(other))
    out[...] = table_rows(out.shape, (*joined(early, late), *early, *late))
    for copy in copies:
        copy.wait()


def noise_kernel(tm_axis, sp_axis, blocks, extras, keys, counters, *rest):
    *outs, base = rest[extras:]
    outs = outs[: len(blocks)]
    steps, vecs, modes = outs[0].shape
    me, sp = lax.axis_index(tm_axis), lax.axis_index(sp_axis)
    diagonal = lax.broadcasted_iota(jnp.int32, (vecs, vecs), 0) == lax.broadcasted_iota(
        jnp.int32, (vecs, vecs), 1
    )

    def column(ref):
        row = jnp.broadcast_to(ref[...].astype(F32), (vecs, vecs))
        return jnp.sum(jnp.where(diagonal, row, 0.0), axis=1, keepdims=True).astype(jnp.int32)

    start = column(keys) * jnp.int32(668265261) + column(counters) * jnp.int32(374761393)
    base[...] = jnp.broadcast_to(start, base.shape)
    group = 8
    for out, (block, offset) in zip(outs, blocks):
        ids = (sp ^ pick(lax.rem(me, 2), offset)) * modes + lax.broadcasted_iota(jnp.int32, (1, modes), 1)
        lane = ids * jnp.int32(-1640531535)
        first_step = (me ^ block) * steps

        def step(t, _):
            shifted = lane + (first_step + t) * jnp.int32(374761393)
            for v in range(vecs // group):
                seeded = jnp.tile(base[pl.ds(v * group, group), :], (1, modes // 128)) + shifted
                out[t, pl.ds(v * group, group), :] = gaussian(seeded)
            return 0

        lax.fori_loop(0, steps, step, 0)


def chain(coup, spec, d_start, f_start):
    before, after = [], []
    square, total = None, None
    d_now = d_start
    for t in range(coup.shape[0]):
        c = coup[t : t + 1, :]
        square = c * c if t == 0 else square * (c * c)
        total = square if t == 0 else total + square
        before.append(d_now)
        d_now = d_start + f_start * total
        after.append(d_now)
    ratio = jnp.concatenate(before, 0) / jnp.concatenate(after, 0)
    return jnp.sqrt(ratio / spec), ratio


def after(start, total):
    return start[0] + start[1] * total[1], start[1] * (total[0] * total[0])


def select(flag, x, y):
    return tuple(jnp.where(flag, p, q) for p, q in zip(x, y))


def gain_of(start, total):
    return total[0] * start[0] / (start[0] + start[1] * total[1])


def offset_kernel(tm_axis, noise_own, noise_other, coup, coup_other, spec, table, *rest):
    received, rest = rest[:-10], rest[-10:]
    o_ref, late_ref, wts, df, tables, *coefs, tmp = rest
    steps, vecs, modes = noise_own.shape
    me = lax.axis_index(tm_axis)
    chip = me // 2
    first = lax.rem(me, 2) == 0
    one = jnp.ones((1, modes), F32)
    tables[chip] = table[...]
    for e, ref in enumerate(received):
        tables[chip ^ (e + 1)] = ref[...]
    now, start, weight = (one, one), (one, one), jnp.zeros((1, modes), F32)
    for b in range(tables.shape[0]):
        wts[b] = jnp.broadcast_to(weight, (8, modes))
        total = tables[b, pl.ds(0, 1), :], tables[b, pl.ds(1, 1), :]
        here = chip == b
        start = select(here, now, start)
        weight = jnp.where(here, 1.0, weight * gain_of(now, total))
        now = after(now, total)
    early = table[pl.ds(2, 1), :], table[pl.ds(3, 1), :]
    late = table[pl.ds(4, 1), :], table[pl.ds(5, 1), :]
    second = after(start, early)
    gain_early, gain_late = gain_of(start, early), gain_of(second, late)
    df[...] = table_rows((8, modes), (*start, *second, gain_late))
    own, other = ordered(first, start, second)
    for j, (ref, sums) in enumerate(((coup, own), (coup_other, other))):
        c = ref[...]
        a, ratio = chain(c, spec[...], *sums)
        coefs[2 * j][...] = c * a
        coefs[2 * j + 1][...] = c * ratio
    tmp[...] = jnp.broadcast_to(gain_early, tmp.shape)

    def tile(v, _):
        at = pl.ds(pl.multiple_of(v * 16, 16), 16)
        ends = []
        for j, noise in enumerate((noise_own, noise_other)):
            alpha, beta = coefs[2 * j], coefs[2 * j + 1]
            carry = jnp.zeros((16, modes), F32)
            for t in range(steps - 1, -1, -1):
                carry = alpha[pl.ds(t, 1), :] * noise[t, at, :] + beta[pl.ds(t, 1), :] * carry
            ends.append(carry)
        (early,), (late,) = ordered(first, ends[:1], ends[1:])
        o_ref[at, :] = (early + tmp[pl.ds(0, 1), :] * late).astype(BF16)
        late_ref[at, :] = late
        return 0

    lax.fori_loop(0, vecs // 16, tile, 0)


def carry_kernel(tm_axis, late, wts, df, *rest):
    *received, _, out = rest
    vecs, modes = late.shape
    me = lax.axis_index(tm_axis)
    first = lax.rem(me, 2) == 0
    carry = jnp.zeros(late.shape, F32)
    for e, ref in enumerate(received):
        carry = carry + wts[(me // 2) ^ (e + 1)][0:1, :] * ref[...].astype(F32)
    out[pl.ds(0, vecs), :] = jnp.where(first, late[...] + df[pl.ds(4, 1), :] * carry, carry).astype(BF16)
    own = select(first, (df[pl.ds(0, 1), :], df[pl.ds(1, 1), :]), (df[pl.ds(2, 1), :], df[pl.ds(3, 1), :]))
    out[pl.ds(vecs, 16), :] = table_rows((16, modes), split3(own[0]) + split3(own[1])).astype(BF16)


def sums_of(block):
    return block[0:1] + block[1:2] + block[2:3], block[3:4] + block[4:5] + block[5:6]


def set_coefs(coefs, c, lam, sums):
    a, ratio = chain(c, lam, *sums)
    coefs[0] = a
    coefs[1] = ratio
    coefs[2] = c


def values(noise, start, coefs, state, rhs, times):
    vecs = noise.shape[1]
    for v in range(0, vecs, 16):
        at = pl.ds(v, 16)
        carry = start(at)
        for n, t in enumerate(times):
            row = pl.ds(t, 1)
            value = coefs[0, row, :] * noise[t, at, :] + coefs[1, row, :] * carry
            if t:
                carry = coefs[2, row, :] * value
            rhs[pl.ds((len(times) - 1 - n) * vecs + v, 16), :] = value.astype(BF16)
        if times[-1]:
            state[at, :] = carry


def product(lhs, rhs):
    return lax.dot_general(lhs, rhs, (((1,), (1,)), ((), ())), preferred_element_type=F32)


def halves_of(steps):
    times = list(range(steps - 1, -1, -1))
    return times[: steps // 2], times[steps // 2 :]


def own_kernel(sp_axis, coup, spec, basis, noise, message, out, lhs, rhs, state, coefs, sem):
    rows = lhs.shape[0]
    steps, vecs, _ = noise.shape
    start = pl.multiple_of(lax.axis_index(sp_axis) * rows, rows)
    copy = pltpu.make_async_copy(basis.at[pl.ds(start, rows), :], lhs, sem)
    copy.start()
    set_coefs(coefs, coup[...], spec[...], sums_of(message[pl.ds(vecs, 16), :].astype(F32)))
    late, early = halves_of(steps)
    width = vecs * len(late)
    values(noise, lambda at: message[at, :].astype(F32), coefs, state, rhs.at[0], late)
    copy.wait()
    values(noise, lambda at: state[at, :], coefs, state, rhs.at[1], early)
    out[:, pl.ds(width, width)] = product(lhs[...], rhs[0])
    out[:, pl.ds(0, width)] = product(lhs[...], rhs[1])


def final_kernel(tm_axis, pairs, single, partial, *rest):
    fetched = len(pairs) + len(single)
    count = 2 * len(pairs) + len(single)
    direct, rest = rest[:fetched], rest[fetched:]
    swapped, rest = rest[:fetched], rest[fetched:]
    noise, rest = rest[:count], rest[count:]
    messages, rest = rest[:count], rest[count:]
    out, lhs, rhs, state, coefs, result, sems = rest
    steps, vecs, _ = noise[0].shape
    core = lax.rem(lax.axis_index(tm_axis), 2)
    first = core == 0
    copies = []
    for i in range(len(single)):
        rows = lhs.shape[1] // 2
        for j, source in enumerate((direct[i], swapped[i])):
            at = pl.multiple_of((core if j == 0 else 1 - core) * rows, rows)
            copies.append(
                pltpu.make_async_copy(
                    source.at[pl.ds(0, rows), :], lhs.at[i, pl.ds(at, rows), :], sems.at[2 * i + j]
                )
            )
            copies[-1].start()

    def chosen(x, y):
        return lambda at: jnp.where(first, messages[x][at, :].astype(F32), messages[y][at, :].astype(F32))

    items = []
    for j, (x, y) in enumerate(pairs):
        i = len(single) + j
        rows = direct[i].shape[0] - TAIL
        near = lambda i=i, rows=rows: direct[i][pl.ds(0, rows), :]
        far = lambda i=i, rows=rows: swapped[i][pl.ds(0, rows), :]
        items.append((near, direct[i], noise[len(single) + j], chosen(x - 1, y - 1)))
        items.append((far, swapped[i], noise[len(single) + len(pairs) + j], chosen(y - 1, x - 1)))
    for i, d in enumerate(single):
        items.append((lambda i=i: lhs[i], direct[i], noise[i], chosen(d - 1, d - 1)))
    for n, (_, source, _, message) in enumerate(items):
        rows = source.shape[0] - TAIL
        x = [source[pl.ds(rows + 16 * j, 16), :].astype(F32) for j in range(4)]
        before = x[0][0:8] + x[0][8:16] + x[1][0:8]
        behind = x[1][8:16] + x[2][0:8] + x[2][8:16]
        lam = x[3][0:1] + x[3][1:2] + x[3][2:3]
        set_coefs(coefs.at[n], jnp.where(first, before, behind), lam, sums_of(message(pl.ds(vecs, 16))))
    late, early = halves_of(steps)
    width = vecs * len(late)
    work = [(h, n) for h in range(2) for n in range(count)]

    def fill(h, n):
        start = items[n][3] if h == 0 else lambda at: state[n, at, :]
        values(items[n][2], start, coefs.at[n], state.at[n], rhs.at[h, n], late if h == 0 else early)

    fill(*work[0])
    outs = []
    for k, (h, n) in enumerate(work):
        if k + 1 < len(work):
            fill(*work[k + 1])
        if h == 0 and n == count - len(single):
            for copy in copies:
                copy.wait()
        term = product(items[n][0](), rhs[h, n])
        at = pl.ds((1 - h) * width, width)
        result[h] = (partial[:, at] if n == 0 else result[h]) + term
        if n == count - 1:
            outs.append(pltpu.make_async_copy(result.at[h], out.at[:, at], sems.at[2 * len(single) + h]))
            outs[-1].start()
    for copy in outs:
        copy.wait()


def kernel_call(body, **options):
    return pl.pallas_call(body, **options)


def local(spectrum, coupling, spatial_basis, noise_keys, noise_counters):
    steps, modes = coupling.shape
    vecs = noise_keys.shape[0]
    tm, space = lax.axis_size("tm"), lax.axis_size("space")
    chips = tm // 2
    nodes_here = spatial_basis.shape[0] // space
    half = nodes_here // 2
    keys, counters = noise_keys.reshape(1, vecs), noise_counters.reshape(1, vecs)
    f32 = lambda *shape: jax.ShapeDtypeStruct(shape, F32)
    bf16 = lambda *shape: jax.ShapeDtypeStruct(shape, BF16)
    fast = dict(compiler_params=LIMIT)
    in_hbm = [
        pltpu.with_memory_space_constraint(x, pltpu.HBM)
        for x in (coupling, spectrum.reshape(1, modes), spatial_basis)
    ]

    pairs, single = partners(space)
    routes = [(d, d) for d in single] + pairs
    sizes = [half + TAIL] * len(single) + [nodes_here + TAIL] * len(pairs)
    other = swap(coupling, "tm", 1)
    *messages, coup, spec = kernel_call(
        functools.partial(pack_kernel, "tm", "space", routes),
        out_shape=[bf16(n, modes) for n in sizes] + [f32(steps, modes), f32(1, modes)],
        in_specs=[HBM] * 3,
        out_specs=[VMEM] * (len(sizes) + 2),
        scratch_shapes=[pltpu.SemaphoreType.DMA((len(sizes) + 2,))],
        **fast,
    )(*in_hbm)
    table, *messages = kernel_call(
        functools.partial(table_kernel, "tm", len(sizes)),
        out_shape=[f32(8, modes)] + [bf16(n, modes) for n in sizes],
        in_specs=[VMEM] * 3 + [ANY] * len(sizes),
        out_specs=[VMEM] + [ANY] * len(sizes),
        scratch_shapes=[pltpu.VMEM((TAIL, modes), BF16), pltpu.SemaphoreType.DMA((len(sizes),))],
        input_output_aliases={3 + i: 1 + i for i in range(len(sizes))},
        **fast,
    )(coup, other, spec, *messages)
    tables = [swap(table, "tm", 2 * e) for e in range(1, chips)]
    direct = [exchange(m, lambda t, s, r=r: (t, s ^ r[t % 2])) for m, r in zip(messages, routes)]

    def noise_of(blocks, after, through=()):
        count = len(blocks) * steps * vecs * modes
        extras = len(after) + len(through)
        return kernel_call(
            functools.partial(noise_kernel, "tm", "space", blocks, extras),
            out_shape=[f32(steps, vecs, modes)] * len(blocks)
            + [jax.ShapeDtypeStruct(x.shape, x.dtype) for x in through],
            in_specs=[VMEM] * 2 + [ANY] * extras,
            out_specs=[VMEM] * len(blocks) + [ANY] * len(through),
            scratch_shapes=[pltpu.VMEM((vecs, 128), jnp.int32)],
            input_output_aliases={2 + len(after) + i: len(blocks) + i for i in range(len(through))},
            cost_estimate=pl.CostEstimate(flops=count * 60, transcendentals=count * 2, bytes_accessed=count * 4),
            **fast,
        )(keys, counters, *after, *through)

    own, paired = noise_of(((0, (0, 0)), (1, (0, 0))), (table,))
    total, late, weights, sums = kernel_call(
        functools.partial(offset_kernel, "tm"),
        out_shape=[bf16(vecs, modes), f32(vecs, modes), f32(chips, 8, modes), f32(8, modes)],
        in_specs=[VMEM] * (6 + len(tables)),
        out_specs=[VMEM] * 4,
        scratch_shapes=[pltpu.VMEM((chips, 8, modes), F32)] + [pltpu.VMEM((steps, modes), F32)] * 5,
        **fast,
    )(own, paired, coup, other, spec, table, *tables)
    later = [swap(total, "tm", 2 * e) for e in range(1, chips)]
    alone = len(single)
    out = noise_of([(0, (d, d)) for d in single], (total,), direct[alone:])
    noise, direct = list(out[:alone]), direct[:alone] + list(out[alone:])
    noise += noise_of([(0, r) for r in pairs], (noise[-1],))
    carry = kernel_call(
        functools.partial(carry_kernel, "tm"),
        out_shape=bf16(vecs + 16, modes),
        in_specs=[VMEM] * (3 + len(later)) + [ANY],
        out_specs=VMEM,
        **fast,
    )(late, weights, sums, *later, noise[-1])
    carries = [swap(carry, "space", d) for d in range(1, space)]
    swapped = [swap(m, "tm", 1) for m in direct]
    noise += noise_of([(0, r[::-1]) for r in pairs], (carry,))

    flops = 2 * nodes_here * modes * steps * vecs
    half_cols = steps // 2 * vecs
    result = f32(nodes_here, steps * vecs)
    out = kernel_call(
        functools.partial(own_kernel, "space"),
        out_shape=result,
        in_specs=[VMEM, VMEM, HBM, VMEM, VMEM],
        out_specs=VMEM,
        scratch_shapes=[
            pltpu.VMEM((nodes_here, modes), BF16),
            pltpu.VMEM((2, half_cols, modes), BF16),
            pltpu.VMEM((vecs, modes), F32),
            pltpu.VMEM((3, steps, modes), F32),
            pltpu.SemaphoreType.DMA,
        ],
        cost_estimate=pl.CostEstimate(flops=flops, transcendentals=0, bytes_accessed=4 * steps * vecs * modes),
        **fast,
    )(coup, spec, spatial_basis, own, carry)
    count = space - 1
    return kernel_call(
        functools.partial(final_kernel, "tm", pairs, single),
        out_shape=result,
        in_specs=[VMEM] * (1 + len(direct) + len(swapped) + len(noise) + len(carries)),
        out_specs=HBM,
        scratch_shapes=[
            pltpu.VMEM((len(single), nodes_here, modes), BF16),
            pltpu.VMEM((2, count, half_cols, modes), BF16),
            pltpu.VMEM((count, vecs, modes), F32),
            pltpu.VMEM((count, 3, steps, modes), F32),
            pltpu.VMEM((2, nodes_here, half_cols), F32),
            pltpu.SemaphoreType.DMA((2 * len(single) + 2,)),
        ],
        cost_estimate=pl.CostEstimate(
            flops=flops * count, transcendentals=0, bytes_accessed=4 * steps * vecs * modes * count
        ),
        **fast,
    )(out, *direct, *swapped, *noise, *carries)


def solution(mesh):
    in_specs = (P("space"), P("tm", "space"), P(None, "space"), P(), P())
    out_specs = P("space", "tm")
    return jax.shard_map(local, mesh=mesh, in_specs=in_specs, out_specs=out_specs, check_vma=False)
```

```python
import functools

import jax
import jax.numpy as jnp
from jax import lax
from jax.experimental import pallas as pl
from jax.experimental.pallas import tpu as pltpu
from jax.sharding import PartitionSpec as P


F32 = jnp.float32
BF16 = jnp.bfloat16
VMEM = pl.BlockSpec(memory_space=pltpu.VMEM)
ANY = pl.BlockSpec(memory_space=pl.ANY)
HBM = pl.BlockSpec(memory_space=pltpu.HBM)
LIMIT = pltpu.CompilerParams(vmem_limit_bytes=24 << 20)
SINE = (6.28318516, -41.34165503, 81.60100406, -76.54978208, 39.53670436)


def partners(count):
    pairs = [(i, i + 1) for i in range(1, count - 2, 2)]
    return pairs, ([count - 1] if count > 1 else [])


def exchange(x, move):
    tm, space = lax.axis_size("tm"), lax.axis_size("space")
    moves = []
    for t in range(tm):
        for s in range(space):
            to = move(t, s)
            if to is not None:
                moves.append((t * space + s, to[0] * space + to[1]))
    return lax.ppermute(x, ("tm", "space"), moves)


def swap(x, axis, offset):
    count = lax.axis_size(axis)
    return lax.ppermute(x, axis, [(i, i ^ offset) for i in range(count)])


def split3(x):
    high = x.astype(BF16).astype(F32)
    rest = x - high
    middle = rest.astype(BF16).astype(F32)
    return high, middle, rest - middle


def mix_bits(state):
    state = state ^ lax.shift_right_logical(state, jnp.int32(16))
    state = state * jnp.int32(-2048144789)
    state = state ^ lax.shift_right_logical(state, jnp.int32(13))
    state = state * jnp.int32(-1028477387)
    return state ^ lax.shift_right_logical(state, jnp.int32(16))


def gaussian(seeded):
    first = mix_bits(seeded)
    second = mix_bits(first + jnp.int32(1013904223))
    unit = (lax.shift_right_logical(first, jnp.int32(8)).astype(F32) + 0.5) * (1.0 / 16777216.0)
    square = -2.0 * jnp.log(unit)
    radius = square * lax.rsqrt(jnp.maximum(square, 1e-30))
    turn = (lax.shift_right_arithmetic(second, jnp.int32(8)).astype(F32) + 0.5) * (1.0 / 16777216.0)
    w = 0.25 - jnp.abs(turn)
    z = w * w
    sine = SINE[4]
    for c in SINE[3::-1]:
        sine = sine * z + c
    return radius * (sine * w)


TAIL = 64


def pick(core, offsets):
    return offsets[0] if offsets[0] == offsets[1] else jnp.where(core == 0, offsets[0], offsets[1])


def pack_kernel(tm_axis, sp_axis, offsets, coup, spec, basis, *rest):
    *outs, coup_out, spec_out, sems = rest
    me, sp = lax.axis_index(tm_axis), lax.axis_index(sp_axis)
    core = lax.rem(me, 2)
    copies = [
        pltpu.make_async_copy(coup, coup_out, sems.at[len(outs)]),
        pltpu.make_async_copy(spec, spec_out, sems.at[len(outs) + 1]),
    ]
    for i, (out, offset) in enumerate(zip(outs, offsets)):
        rows = out.shape[0] - TAIL
        block = sp ^ pick(core, offset)
        if offset[0] == offset[1]:
            block = block * 2 + core
        start = pl.multiple_of(block * rows, rows)
        copies.append(
            pltpu.make_async_copy(basis.at[pl.ds(start, rows), :], out.at[pl.ds(0, rows), :], sems.at[i])
        )
    for copy in copies:
        copy.start()
    for copy in copies:
        copy.wait()


def totals(ref):
    product = square = total = None
    for t in range(ref.shape[0]):
        c = ref[pl.ds(t, 1), :]
        product = c if t == 0 else product * c
        square = c * c if t == 0 else square * (c * c)
        total = square if t == 0 else total + square
    return product, total


def joined(early, late):
    return early[0] * late[0], early[1] + (early[0] * early[0]) * late[1]


def table_rows(shape, rows):
    row = lax.broadcasted_iota(jnp.int32, shape, 0)
    table = jnp.zeros(shape, F32)
    for j, value in enumerate(rows):
        table = jnp.where(row == j, value, table)
    return table


def ordered(first, mine, theirs):
    early = tuple(jnp.where(first, x, y) for x, y in zip(mine, theirs))
    late = tuple(jnp.where(first, y, x) for x, y in zip(mine, theirs))
    return early, late


def table_kernel(tm_axis, count, coup, other, spec, *rest):
    out, *messages, tail, sems = rest[count:]
    first = lax.rem(lax.axis_index(tm_axis), 2) == 0
    (x,), (y,) = ordered(first, (coup[...],), (other[...],))
    parts = split3(x) + split3(y)
    parts = parts + (table_rows(x.shape, split3(spec[...])), jnp.zeros_like(x))
    for j in range(4):
        tail[pl.ds(16 * j, 16), :] = jnp.concatenate(parts[2 * j : 2 * j + 2], 0).astype(BF16)
    copies = []
    for i, message in enumerate(messages):
        rows = message.shape[0] - TAIL
        copies.append(pltpu.make_async_copy(tail, message.at[pl.ds(rows, TAIL), :], sems.at[i]))
        copies[-1].start()
    early, late = ordered(first, totals(coup), totals(other))
    out[...] = table_rows(out.shape, (*joined(early, late), *early, *late))
    for copy in copies:
        copy.wait()


def noise_kernel(tm_axis, sp_axis, blocks, extras, keys, counters, *rest):
    *outs, base = rest[extras:]
    outs = outs[: len(blocks)]
    steps, vecs, modes = outs[0].shape
    me, sp = lax.axis_index(tm_axis), lax.axis_index(sp_axis)
    diagonal = lax.broadcasted_iota(jnp.int32, (vecs, vecs), 0) == lax.broadcasted_iota(
        jnp.int32, (vecs, vecs), 1
    )

    def column(ref):
        row = jnp.broadcast_to(ref[...].astype(F32), (vecs, vecs))
        return jnp.sum(jnp.where(diagonal, row, 0.0), axis=1, keepdims=True).astype(jnp.int32)

    start = column(keys) * jnp.int32(668265261) + column(counters) * jnp.int32(374761393)
    base[...] = jnp.broadcast_to(start, base.shape)
    group = 8
    for out, (block, offset) in zip(outs, blocks):
        ids = (sp ^ pick(lax.rem(me, 2), offset)) * modes + lax.broadcasted_iota(jnp.int32, (1, modes), 1)
        lane = ids * jnp.int32(-1640531535)
        first_step = (me ^ block) * steps

        def step(t, _):
            shifted = lane + (first_step + t) * jnp.int32(374761393)
            for v in range(vecs // group):
                seeded = jnp.tile(base[pl.ds(v * group, group), :], (1, modes // 128)) + shifted
                out[t, pl.ds(v * group, group), :] = gaussian(seeded)
            return 0

        lax.fori_loop(0, steps, step, 0)


def chain(coup, spec, d_start, f_start):
    before, after = [], []
    square, total = None, None
    d_now = d_start
    for t in range(coup.shape[0]):
        c = coup[t : t + 1, :]
        square = c * c if t == 0 else square * (c * c)
        total = square if t == 0 else total + square
        before.append(d_now)
        d_now = d_start + f_start * total
        after.append(d_now)
    ratio = jnp.concatenate(before, 0) / jnp.concatenate(after, 0)
    return jnp.sqrt(ratio / spec), ratio


def after(start, total):
    return start[0] + start[1] * total[1], start[1] * (total[0] * total[0])


def select(flag, x, y):
    return tuple(jnp.where(flag, p, q) for p, q in zip(x, y))


def gain_of(start, total):
    return total[0] * start[0] / (start[0] + start[1] * total[1])


def offset_kernel(tm_axis, noise, coup, spec, table, *rest):
    received, rest = rest[:-7], rest[-7:]
    o_ref, sent, wts, df, tables, alpha, beta = rest
    steps, vecs, modes = noise.shape
    me = lax.axis_index(tm_axis)
    chip = me // 2
    first = lax.rem(me, 2) == 0
    one = jnp.ones((1, modes), F32)
    tables[chip] = table[...]
    for e, ref in enumerate(received):
        tables[chip ^ (e + 1)] = ref[...]
    now, start, weight = (one, one), (one, one), jnp.zeros((1, modes), F32)
    for b in range(tables.shape[0]):
        wts[b] = jnp.broadcast_to(weight, (8, modes))
        total = tables[b, pl.ds(0, 1), :], tables[b, pl.ds(1, 1), :]
        here = chip == b
        start = select(here, now, start)
        weight = jnp.where(here, 1.0, weight * gain_of(now, total))
        now = after(now, total)
    early = table[pl.ds(2, 1), :], table[pl.ds(3, 1), :]
    late = table[pl.ds(4, 1), :], table[pl.ds(5, 1), :]
    second = after(start, early)
    gain_early, gain_late = gain_of(start, early), gain_of(second, late)
    own = select(first, start, second)
    df[...] = table_rows((8, modes), (*own, gain_early, gain_late))
    c = coup[...]
    a, ratio = chain(c, spec[...], *own)
    alpha[...] = c * a
    beta[...] = c * ratio

    def tile(v, _):
        at = pl.ds(pl.multiple_of(v * 16, 16), 16)
        carry = jnp.zeros((16, modes), F32)
        for t in range(steps - 1, -1, -1):
            carry = alpha[pl.ds(t, 1), :] * noise[t, at, :] + beta[pl.ds(t, 1), :] * carry
        o_ref[at, :] = carry
        sent[at, :] = carry.astype(BF16)
        return 0

    lax.fori_loop(0, vecs // 16, tile, 0)


def combine_kernel(tm_axis, own, other, df, out, late):
    first = lax.rem(lax.axis_index(tm_axis), 2) == 0
    x, y = own[...], other[...].astype(F32)
    behind = jnp.where(first, y, x)
    out[...] = (jnp.where(first, x, y) + df[pl.ds(2, 1), :] * behind).astype(BF16)
    late[...] = behind


def carry_kernel(tm_axis, late, wts, df, *rest):
    *received, _, out = rest
    vecs, modes = late.shape
    me = lax.axis_index(tm_axis)
    first = lax.rem(me, 2) == 0
    carry = jnp.zeros(late.shape, F32)
    for e, ref in enumerate(received):
        carry = carry + wts[(me // 2) ^ (e + 1)][0:1, :] * ref[...].astype(F32)
    out[pl.ds(0, vecs), :] = jnp.where(first, late[...] + df[pl.ds(3, 1), :] * carry, carry).astype(BF16)
    out[pl.ds(vecs, 16), :] = table_rows((16, modes), split3(df[pl.ds(0, 1), :]) + split3(df[pl.ds(1, 1), :])).astype(BF16)


def sums_of(block):
    return block[0:1] + block[1:2] + block[2:3], block[3:4] + block[4:5] + block[5:6]


def set_coefs(coefs, c, lam, sums):
    a, ratio = chain(c, lam, *sums)
    coefs[0] = a
    coefs[1] = ratio
    coefs[2] = c


def values(noise, start, coefs, state, rhs, times):
    vecs = noise.shape[1]
    for v in range(0, vecs, 16):
        at = pl.ds(v, 16)
        carry = start(at)
        for n, t in enumerate(times):
            row = pl.ds(t, 1)
            value = coefs[0, row, :] * noise[t, at, :] + coefs[1, row, :] * carry
            if t:
                carry = coefs[2, row, :] * value
            rhs[pl.ds((len(times) - 1 - n) * vecs + v, 16), :] = value.astype(BF16)
        if times[-1]:
            state[at, :] = carry


def product(lhs, rhs):
    return lax.dot_general(lhs, rhs, (((1,), (1,)), ((), ())), preferred_element_type=F32)


def halves_of(steps):
    times = list(range(steps - 1, -1, -1))
    return times[: steps // 2], times[steps // 2 :]


def own_kernel(sp_axis, coup, spec, basis, noise, message, out, lhs, rhs, state, coefs, sem):
    rows = lhs.shape[0]
    steps, vecs, _ = noise.shape
    start = pl.multiple_of(lax.axis_index(sp_axis) * rows, rows)
    copy = pltpu.make_async_copy(basis.at[pl.ds(start, rows), :], lhs, sem)
    copy.start()
    set_coefs(coefs, coup[...], spec[...], sums_of(message[pl.ds(vecs, 16), :].astype(F32)))
    late, early = halves_of(steps)
    width = vecs * len(late)
    values(noise, lambda at: message[at, :].astype(F32), coefs, state, rhs.at[0], late)
    copy.wait()
    values(noise, lambda at: state[at, :], coefs, state, rhs.at[1], early)
    out[:, pl.ds(width, width)] = product(lhs[...], rhs[0])
    out[:, pl.ds(0, width)] = product(lhs[...], rhs[1])


def final_kernel(tm_axis, pairs, single, partial, *rest):
    fetched = len(pairs) + len(single)
    count = 2 * len(pairs) + len(single)
    direct, rest = rest[:fetched], rest[fetched:]
    swapped, rest = rest[:fetched], rest[fetched:]
    noise, rest = rest[:count], rest[count:]
    messages, rest = rest[:count], rest[count:]
    out, lhs, rhs, state, coefs, result, sems = rest
    steps, vecs, _ = noise[0].shape
    core = lax.rem(lax.axis_index(tm_axis), 2)
    first = core == 0
    copies = []
    for i in range(len(single)):
        rows = lhs.shape[1] // 2
        for j, source in enumerate((direct[i], swapped[i])):
            at = pl.multiple_of((core if j == 0 else 1 - core) * rows, rows)
            copies.append(
                pltpu.make_async_copy(
                    source.at[pl.ds(0, rows), :], lhs.at[i, pl.ds(at, rows), :], sems.at[2 * i + j]
                )
            )
            copies[-1].start()

    def chosen(x, y):
        return lambda at: jnp.where(first, messages[x][at, :].astype(F32), messages[y][at, :].astype(F32))

    items = []
    for j, (x, y) in enumerate(pairs):
        i = len(single) + j
        rows = direct[i].shape[0] - TAIL
        near = lambda i=i, rows=rows: direct[i][pl.ds(0, rows), :]
        far = lambda i=i, rows=rows: swapped[i][pl.ds(0, rows), :]
        items.append((near, direct[i], noise[len(single) + j], chosen(x - 1, y - 1)))
        items.append((far, swapped[i], noise[len(single) + len(pairs) + j], chosen(y - 1, x - 1)))
    for i, d in enumerate(single):
        items.append((lambda i=i: lhs[i], direct[i], noise[i], chosen(d - 1, d - 1)))
    for n, (_, source, _, message) in enumerate(items):
        rows = source.shape[0] - TAIL
        x = [source[pl.ds(rows + 16 * j, 16), :].astype(F32) for j in range(4)]
        before = x[0][0:8] + x[0][8:16] + x[1][0:8]
        behind = x[1][8:16] + x[2][0:8] + x[2][8:16]
        lam = x[3][0:1] + x[3][1:2] + x[3][2:3]
        set_coefs(coefs.at[n], jnp.where(first, before, behind), lam, sums_of(message(pl.ds(vecs, 16))))
    late, early = halves_of(steps)
    width = vecs * len(late)
    work = [(h, n) for h in range(2) for n in range(count)]

    def fill(h, n):
        start = items[n][3] if h == 0 else lambda at: state[n, at, :]
        values(items[n][2], start, coefs.at[n], state.at[n], rhs.at[h, n], late if h == 0 else early)

    fill(*work[0])
    outs = []
    for k, (h, n) in enumerate(work):
        if k + 1 < len(work):
            fill(*work[k + 1])
        if h == 0 and n == count - len(single):
            for copy in copies:
                copy.wait()
        term = product(items[n][0](), rhs[h, n])
        at = pl.ds((1 - h) * width, width)
        result[h] = (partial[:, at] if n == 0 else result[h]) + term
        if n == count - 1:
            outs.append(pltpu.make_async_copy(result.at[h], out.at[:, at], sems.at[2 * len(single) + h]))
            outs[-1].start()
    for copy in outs:
        copy.wait()


def kernel_call(body, **options):
    return pl.pallas_call(body, **options)


def local(spectrum, coupling, spatial_basis, noise_keys, noise_counters):
    steps, modes = coupling.shape
    vecs = noise_keys.shape[0]
    tm, space = lax.axis_size("tm"), lax.axis_size("space")
    chips = tm // 2
    nodes_here = spatial_basis.shape[0] // space
    half = nodes_here // 2
    keys, counters = noise_keys.reshape(1, vecs), noise_counters.reshape(1, vecs)
    f32 = lambda *shape: jax.ShapeDtypeStruct(shape, F32)
    bf16 = lambda *shape: jax.ShapeDtypeStruct(shape, BF16)
    fast = dict(compiler_params=LIMIT)
    in_hbm = [
        pltpu.with_memory_space_constraint(x, pltpu.HBM)
        for x in (coupling, spectrum.reshape(1, modes), spatial_basis)
    ]

    pairs, single = partners(space)
    routes = [(d, d) for d in single] + pairs
    sizes = [half + TAIL] * len(single) + [nodes_here + TAIL] * len(pairs)
    other = swap(coupling, "tm", 1)
    *messages, coup, spec = kernel_call(
        functools.partial(pack_kernel, "tm", "space", routes),
        out_shape=[bf16(n, modes) for n in sizes] + [f32(steps, modes), f32(1, modes)],
        in_specs=[HBM] * 3,
        out_specs=[VMEM] * (len(sizes) + 2),
        scratch_shapes=[pltpu.SemaphoreType.DMA((len(sizes) + 2,))],
        **fast,
    )(*in_hbm)
    table, *messages = kernel_call(
        functools.partial(table_kernel, "tm", len(sizes)),
        out_shape=[f32(8, modes)] + [bf16(n, modes) for n in sizes],
        in_specs=[VMEM] * 3 + [ANY] * len(sizes),
        out_specs=[VMEM] + [ANY] * len(sizes),
        scratch_shapes=[pltpu.VMEM((TAIL, modes), BF16), pltpu.SemaphoreType.DMA((len(sizes),))],
        input_output_aliases={3 + i: 1 + i for i in range(len(sizes))},
        **fast,
    )(coup, other, spec, *messages)
    tables = [swap(table, "tm", 2 * e) for e in range(1, chips)]
    direct = [exchange(m, lambda t, s, r=r: (t, s ^ r[t % 2])) for m, r in zip(messages, routes)]

    def noise_of(blocks, after, through=()):
        count = len(blocks) * steps * vecs * modes
        extras = len(after) + len(through)
        return kernel_call(
            functools.partial(noise_kernel, "tm", "space", blocks, extras),
            out_shape=[f32(steps, vecs, modes)] * len(blocks)
            + [jax.ShapeDtypeStruct(x.shape, x.dtype) for x in through],
            in_specs=[VMEM] * 2 + [ANY] * extras,
            out_specs=[VMEM] * len(blocks) + [ANY] * len(through),
            scratch_shapes=[pltpu.VMEM((vecs, 128), jnp.int32)],
            input_output_aliases={2 + len(after) + i: len(blocks) + i for i in range(len(through))},
            cost_estimate=pl.CostEstimate(flops=count * 60, transcendentals=count * 2, bytes_accessed=count * 4),
            **fast,
        )(keys, counters, *after, *through)

    (own,) = noise_of([(0, (0, 0))], (table,))
    state, sent, weights, sums = kernel_call(
        functools.partial(offset_kernel, "tm"),
        out_shape=[f32(vecs, modes), bf16(vecs, modes), f32(chips, 8, modes), f32(8, modes)],
        in_specs=[VMEM] * (4 + len(tables)),
        out_specs=[VMEM] * 4,
        scratch_shapes=[pltpu.VMEM((chips, 8, modes), F32)] + [pltpu.VMEM((steps, modes), F32)] * 2,
        **fast,
    )(own, coup, spec, table, *tables)
    total, late = kernel_call(
        functools.partial(combine_kernel, "tm"),
        out_shape=[bf16(vecs, modes), f32(vecs, modes)],
        in_specs=[VMEM] * 3,
        out_specs=[VMEM] * 2,
        **fast,
    )(state, swap(sent, "tm", 1), sums)
    later = [swap(total, "tm", 2 * e) for e in range(1, chips)]
    noise = list(noise_of([(0, (d, d)) for d in single], (total,)))
    noise += noise_of([(0, r) for r in pairs], (noise[-1],))
    carry = kernel_call(
        functools.partial(carry_kernel, "tm"),
        out_shape=bf16(vecs + 16, modes),
        in_specs=[VMEM] * (3 + len(later)) + [ANY],
        out_specs=VMEM,
        **fast,
    )(late, weights, sums, *later, noise[-1])
    carries = [swap(carry, "space", d) for d in range(1, space)]
    swapped = [swap(m, "tm", 1) for m in direct]
    noise += noise_of([(0, r[::-1]) for r in pairs], (carry,))

    flops = 2 * nodes_here * modes * steps * vecs
    half_cols = steps // 2 * vecs
    result = f32(nodes_here, steps * vecs)
    out = kernel_call(
        functools.partial(own_kernel, "space"),
        out_shape=result,
        in_specs=[VMEM, VMEM, HBM, VMEM, VMEM],
        out_specs=VMEM,
        scratch_shapes=[
            pltpu.VMEM((nodes_here, modes), BF16),
            pltpu.VMEM((2, half_cols, modes), BF16),
            pltpu.VMEM((vecs, modes), F32),
            pltpu.VMEM((3, steps, modes), F32),
            pltpu.SemaphoreType.DMA,
        ],
        cost_estimate=pl.CostEstimate(flops=flops, transcendentals=0, bytes_accessed=4 * steps * vecs * modes),
        **fast,
    )(coup, spec, spatial_basis, own, carry)
    count = space - 1
    return kernel_call(
        functools.partial(final_kernel, "tm", pairs, single),
        out_shape=result,
        in_specs=[VMEM] * (1 + len(direct) + len(swapped) + len(noise) + len(carries)),
        out_specs=HBM,
        scratch_shapes=[
            pltpu.VMEM((len(single), nodes_here, modes), BF16),
            pltpu.VMEM((2, count, half_cols, modes), BF16),
            pltpu.VMEM((count, vecs, modes), F32),
            pltpu.VMEM((count, 3, steps, modes), F32),
            pltpu.VMEM((2, nodes_here, half_cols), F32),
            pltpu.SemaphoreType.DMA((2 * len(single) + 2,)),
        ],
        cost_estimate=pl.CostEstimate(
            flops=flops * count, transcendentals=0, bytes_accessed=4 * steps * vecs * modes * count
        ),
        **fast,
    )(out, *direct, *swapped, *noise, *carries)


def solution(mesh):
    in_specs = (P("space"), P("tm", "space"), P(None, "space"), P(), P())
    out_specs = P("space", "tm")
    return jax.shard_map(local, mesh=mesh, in_specs=in_specs, out_specs=out_specs, check_vma=False)
```

```python
import functools

import jax
import jax.numpy as jnp
from jax import lax
from jax.experimental import pallas as pl
from jax.experimental.pallas import tpu as pltpu
from jax.sharding import PartitionSpec as P


F32 = jnp.float32
BF16 = jnp.bfloat16
VMEM = pl.BlockSpec(memory_space=pltpu.VMEM)
ANY = pl.BlockSpec(memory_space=pl.ANY)
HBM = pl.BlockSpec(memory_space=pltpu.HBM)
LIMIT = pltpu.CompilerParams(vmem_limit_bytes=24 << 20)
SINE = (6.28318516, -41.34165503, 81.60100406, -76.54978208, 39.53670436)


def partners(count):
    pairs = [(i, i + 1) for i in range(1, count - 2, 2)]
    return pairs, ([count - 1] if count > 1 else [])


def exchange(x, move):
    tm, space = lax.axis_size("tm"), lax.axis_size("space")
    moves = []
    for t in range(tm):
        for s in range(space):
            to = move(t, s)
            if to is not None:
                moves.append((t * space + s, to[0] * space + to[1]))
    return lax.ppermute(x, ("tm", "space"), moves)


def swap(x, axis, offset):
    count = lax.axis_size(axis)
    return lax.ppermute(x, axis, [(i, i ^ offset) for i in range(count)])


def split3(x):
    high = x.astype(BF16).astype(F32)
    rest = x - high
    middle = rest.astype(BF16).astype(F32)
    return high, middle, rest - middle


def mix_bits(state):
    state = state ^ lax.shift_right_logical(state, jnp.int32(16))
    state = state * jnp.int32(-2048144789)
    state = state ^ lax.shift_right_logical(state, jnp.int32(13))
    state = state * jnp.int32(-1028477387)
    return state ^ lax.shift_right_logical(state, jnp.int32(16))


def gaussian(seeded):
    first = mix_bits(seeded)
    second = mix_bits(first + jnp.int32(1013904223))
    unit = (lax.shift_right_logical(first, jnp.int32(8)).astype(F32) + 0.5) * (1.0 / 16777216.0)
    square = -2.0 * jnp.log(unit)
    radius = square * lax.rsqrt(jnp.maximum(square, 1e-30))
    turn = (lax.shift_right_arithmetic(second, jnp.int32(8)).astype(F32) + 0.5) * (1.0 / 16777216.0)
    w = 0.25 - jnp.abs(turn)
    z = w * w
    sine = SINE[4]
    for c in SINE[3::-1]:
        sine = sine * z + c
    return radius * (sine * w)


TAIL = 64


def pick(core, offsets):
    return offsets[0] if offsets[0] == offsets[1] else jnp.where(core == 0, offsets[0], offsets[1])


def pack_kernel(tm_axis, sp_axis, offsets, coup, spec, basis, keys, counters, *rest):
    *outs, coup_out, spec_out, base, key_row, counter_row, sems = rest
    me, sp = lax.axis_index(tm_axis), lax.axis_index(sp_axis)
    core = lax.rem(me, 2)
    copies = [
        pltpu.make_async_copy(coup, coup_out, sems.at[len(outs)]),
        pltpu.make_async_copy(spec, spec_out, sems.at[len(outs) + 1]),
    ]
    rows_in = [
        pltpu.make_async_copy(keys, key_row, sems.at[len(outs) + 2]),
        pltpu.make_async_copy(counters, counter_row, sems.at[len(outs) + 3]),
    ]
    for i, (out, offset) in enumerate(zip(outs, offsets)):
        rows = out.shape[0] - TAIL
        block = sp ^ pick(core, offset)
        if offset[0] == offset[1]:
            block = block * 2 + core
        start = pl.multiple_of(block * rows, rows)
        copies.append(
            pltpu.make_async_copy(basis.at[pl.ds(start, rows), :], out.at[pl.ds(0, rows), :], sems.at[i])
        )
    for copy in rows_in + copies:
        copy.start()
    for copy in rows_in:
        copy.wait()
    base_columns(key_row, counter_row, base)
    for copy in copies:
        copy.wait()


def totals(ref):
    product = square = total = None
    for t in range(ref.shape[0]):
        c = ref[pl.ds(t, 1), :]
        product = c if t == 0 else product * c
        square = c * c if t == 0 else square * (c * c)
        total = square if t == 0 else total + square
    return product, total


def joined(early, late):
    return early[0] * late[0], early[1] + (early[0] * early[0]) * late[1]


def table_rows(shape, rows):
    row = lax.broadcasted_iota(jnp.int32, shape, 0)
    table = jnp.zeros(shape, F32)
    for j, value in enumerate(rows):
        table = jnp.where(row == j, value, table)
    return table


def ordered(first, mine, theirs):
    early = tuple(jnp.where(first, x, y) for x, y in zip(mine, theirs))
    late = tuple(jnp.where(first, y, x) for x, y in zip(mine, theirs))
    return early, late


def table_kernel(tm_axis, count, coup, other, spec, *rest):
    out, *messages, tail, sems = rest[count:]
    first = lax.rem(lax.axis_index(tm_axis), 2) == 0
    (x,), (y,) = ordered(first, (coup[...],), (other[...],))
    parts = split3(x) + split3(y)
    parts = parts + (table_rows(x.shape, split3(spec[...])), jnp.zeros_like(x))
    for j in range(4):
        tail[pl.ds(16 * j, 16), :] = jnp.concatenate(parts[2 * j : 2 * j + 2], 0).astype(BF16)
    copies = []
    for i, message in enumerate(messages):
        rows = message.shape[0] - TAIL
        copies.append(pltpu.make_async_copy(tail, message.at[pl.ds(rows, TAIL), :], sems.at[i]))
        copies[-1].start()
    early, late = ordered(first, totals(coup), totals(other))
    out[...] = table_rows(out.shape, (*joined(early, late), *early, *late))
    for copy in copies:
        copy.wait()


def base_columns(keys, counters, base):
    vecs = base.shape[0]
    diagonal = lax.broadcasted_iota(jnp.int32, (vecs, vecs), 0) == lax.broadcasted_iota(
        jnp.int32, (vecs, vecs), 1
    )

    def column(ref):
        row = jnp.broadcast_to(ref[...].astype(F32), (vecs, vecs))
        return jnp.sum(jnp.where(diagonal, row, 0.0), axis=1, keepdims=True).astype(jnp.int32)

    start = column(keys) * jnp.int32(668265261) + column(counters) * jnp.int32(374761393)
    base[...] = jnp.broadcast_to(start, base.shape)


def noise_kernel(tm_axis, sp_axis, offsets, extras, base, *rest):
    outs = rest[extras:]
    steps, vecs, modes = outs[0].shape
    me, sp = lax.axis_index(tm_axis), lax.axis_index(sp_axis)
    group = 8
    for out, offset in zip(outs, offsets):
        ids = (sp ^ pick(lax.rem(me, 2), offset)) * modes + lax.broadcasted_iota(jnp.int32, (1, modes), 1)
        lane = ids * jnp.int32(-1640531535)
        first_step = me * steps

        def step(t, _):
            shifted = lane + (first_step + t) * jnp.int32(374761393)
            for v in range(vecs // group):
                seeded = jnp.tile(base[pl.ds(v * group, group), :], (1, modes // 128)) + shifted
                out[t, pl.ds(v * group, group), :] = gaussian(seeded)
            return 0

        lax.fori_loop(0, steps, step, 0)


def running(x, combine, identity):
    row = lax.broadcasted_iota(jnp.int32, x.shape, 0)
    shift = 1
    while shift < x.shape[0]:
        x = combine(x, jnp.where(row < shift, identity, pltpu.roll(x, shift, 0)))
        shift *= 2
    return x


def chain(c, spec, d_start, f_start):
    total = running(running(c * c, jnp.multiply, 1.0), jnp.add, 0.0)
    behind = d_start + f_start * total
    row = lax.broadcasted_iota(jnp.int32, c.shape, 0)
    ratio = jnp.where(row == 0, d_start, pltpu.roll(behind, 1, 0)) / behind
    return jnp.sqrt(ratio / spec), ratio


def after(start, total):
    return start[0] + start[1] * total[1], start[1] * (total[0] * total[0])


def select(flag, x, y):
    return tuple(jnp.where(flag, p, q) for p, q in zip(x, y))


def gain_of(start, total):
    return total[0] * start[0] / (start[0] + start[1] * total[1])


def offset_kernel(tm_axis, noise, coup, spec, table, *rest):
    received, rest = rest[:-7], rest[-7:]
    o_ref, sent, wts, df, tables, alpha, beta = rest
    steps, vecs, modes = noise.shape
    me = lax.axis_index(tm_axis)
    chip = me // 2
    first = lax.rem(me, 2) == 0
    one = jnp.ones((1, modes), F32)
    tables[chip] = table[...]
    for e, ref in enumerate(received):
        tables[chip ^ (e + 1)] = ref[...]
    now, start, weight = (one, one), (one, one), jnp.zeros((1, modes), F32)
    for b in range(tables.shape[0]):
        wts[b] = jnp.broadcast_to(weight, (8, modes))
        total = tables[b, pl.ds(0, 1), :], tables[b, pl.ds(1, 1), :]
        here = chip == b
        start = select(here, now, start)
        weight = jnp.where(here, 1.0, weight * gain_of(now, total))
        now = after(now, total)
    early = table[pl.ds(2, 1), :], table[pl.ds(3, 1), :]
    late = table[pl.ds(4, 1), :], table[pl.ds(5, 1), :]
    second = after(start, early)
    gain_early, gain_late = gain_of(start, early), gain_of(second, late)
    own = select(first, start, second)
    df[...] = table_rows((8, modes), (*own, gain_early, gain_late))
    c = coup[...]
    a, ratio = chain(c, spec[...], *own)
    alpha[...] = c * a
    beta[...] = c * ratio

    def tile(v, _):
        at = pl.ds(pl.multiple_of(v * 16, 16), 16)
        carry = jnp.zeros((16, modes), F32)
        for t in range(steps - 1, -1, -1):
            carry = alpha[pl.ds(t, 1), :] * noise[t, at, :] + beta[pl.ds(t, 1), :] * carry
        o_ref[at, :] = carry
        sent[at, :] = carry.astype(BF16)
        return 0

    lax.fori_loop(0, vecs // 16, tile, 0)


def combine_kernel(tm_axis, own, other, df, out, late):
    first = lax.rem(lax.axis_index(tm_axis), 2) == 0
    x, y = own[...], other[...].astype(F32)
    behind = jnp.where(first, y, x)
    out[...] = (jnp.where(first, x, y) + df[pl.ds(2, 1), :] * behind).astype(BF16)
    late[...] = behind


def carry_kernel(tm_axis, late, wts, df, *rest):
    *received, _, out = rest
    vecs, modes = late.shape
    me = lax.axis_index(tm_axis)
    first = lax.rem(me, 2) == 0
    carry = jnp.zeros(late.shape, F32)
    for e, ref in enumerate(received):
        carry = carry + wts[(me // 2) ^ (e + 1)][0:1, :] * ref[...].astype(F32)
    out[pl.ds(0, vecs), :] = jnp.where(first, late[...] + df[pl.ds(3, 1), :] * carry, carry).astype(BF16)
    out[pl.ds(vecs, 16), :] = table_rows((16, modes), split3(df[pl.ds(0, 1), :]) + split3(df[pl.ds(1, 1), :])).astype(BF16)


def sums_of(block):
    return block[0:1] + block[1:2] + block[2:3], block[3:4] + block[4:5] + block[5:6]


def set_coefs(coefs, c, lam, sums):
    a, ratio = chain(c, lam, *sums)
    row = lax.broadcasted_iota(jnp.int32, c.shape, 0)
    steps = c.shape[0]
    coefs[0] = a
    coefs[1] = ratio * jnp.where(row == steps - 1, 1.0, pltpu.roll(c, steps - 1, 0))


def values(noise, start, coefs, state, rhs, times, part=(0, 1)):
    vecs = noise.shape[1]
    share = vecs // part[1]
    for v in range(part[0] * share, (part[0] + 1) * share, 16):
        at = pl.ds(v, 16)
        value = start(at)
        for n, t in enumerate(times):
            row = pl.ds(t, 1)
            value = coefs[0, row, :] * noise[t, at, :] + coefs[1, row, :] * value
            rhs[pl.ds((len(times) - 1 - n) * vecs + v, 16), :] = value.astype(BF16)
        if times[-1]:
            state[at, :] = value


def product(lhs, rhs):
    return lax.dot_general(lhs, rhs, (((1,), (1,)), ((), ())), preferred_element_type=F32)


def halves_of(steps):
    times = list(range(steps - 1, -1, -1))
    return times[: steps // 2], times[steps // 2 :]


def region(position, n):
    return pl.when(position >= -n)


def own_kernel(sp_axis, coup, spec, basis, noise, message, out, lhs, rhs, state, coefs, sem):
    rows = lhs.shape[0]
    steps, vecs, _ = noise.shape
    start = pl.multiple_of(lax.axis_index(sp_axis) * rows, rows)
    copy = pltpu.make_async_copy(basis.at[pl.ds(start, rows), :], lhs, sem)
    copy.start()
    set_coefs(coefs, coup[...], spec[...], sums_of(message[pl.ds(vecs, 16), :].astype(F32)))
    late, early = halves_of(steps)
    width = vecs * len(late)
    values(noise, lambda at: message[at, :].astype(F32), coefs, state, rhs.at[0], late)
    copy.wait()

    @region(start, 0)
    def _():
        out[:, pl.ds(width, width)] = product(lhs[...], rhs[0])
        values(noise, lambda at: state[at, :], coefs, state, rhs.at[1], early)

    @region(start, 1)
    def _():
        out[:, pl.ds(0, width)] = product(lhs[...], rhs[1])


def final_kernel(tm_axis, pairs, single, partial, *rest):
    fetched = len(pairs) + len(single)
    count = 2 * len(pairs) + len(single)
    direct, rest = rest[:fetched], rest[fetched:]
    swapped, rest = rest[:fetched], rest[fetched:]
    noise, rest = rest[:count], rest[count:]
    messages, rest = rest[:count], rest[count:]
    out, lhs, rhs, state, coefs, result, sems = rest
    steps, vecs, _ = noise[0].shape
    core = lax.rem(lax.axis_index(tm_axis), 2)
    first = core == 0
    copies = []
    for i in range(len(single)):
        rows = lhs.shape[1] // 2
        for j, source in enumerate((direct[i], swapped[i])):
            at = pl.multiple_of((core if j == 0 else 1 - core) * rows, rows)
            copies.append(
                pltpu.make_async_copy(
                    source.at[pl.ds(0, rows), :], lhs.at[i, pl.ds(at, rows), :], sems.at[2 * i + j]
                )
            )
            copies[-1].start()

    def chosen(x, y):
        return lambda at: jnp.where(first, messages[x][at, :].astype(F32), messages[y][at, :].astype(F32))

    items = []
    for j, (x, y) in enumerate(pairs):
        i = len(single) + j
        rows = direct[i].shape[0] - TAIL
        near = lambda at=pl.ds(0, rows), i=i: direct[i][at, :]
        far = lambda at=pl.ds(0, rows), i=i: swapped[i][at, :]
        items.append((near, direct[i], noise[len(single) + j], chosen(x - 1, y - 1)))
        items.append((far, swapped[i], noise[len(single) + len(pairs) + j], chosen(y - 1, x - 1)))
    for i, d in enumerate(single):
        items.append((lambda at=slice(None), i=i: lhs[i, at, :], direct[i], noise[i], chosen(d - 1, d - 1)))

    def prepare(n):
        _, source, _, message = items[n]
        rows = source.shape[0] - TAIL
        x = [source[pl.ds(rows + 16 * j, 16), :].astype(F32) for j in range(4)]
        before = x[0][0:8] + x[0][8:16] + x[1][0:8]
        behind = x[1][8:16] + x[2][0:8] + x[2][8:16]
        lam = x[3][0:1] + x[3][1:2] + x[3][2:3]
        set_coefs(coefs.at[n], jnp.where(first, before, behind), lam, sums_of(message(pl.ds(vecs, 16))))

    late, early = halves_of(steps)
    width = vecs * len(late)
    work = [(h, n) for h in range(2) for n in range(count)]

    def fill(h, n, part=(0, 1)):
        start = items[n][3] if h == 0 else lambda at: state[n, at, :]
        values(items[n][2], start, coefs.at[n], state.at[n], rhs.at[h, n], late if h == 0 else early, part)

    def output(h, part=None):
        rows = result.shape[1]
        take = pl.ds(0, rows) if part is None else pl.ds(part * (rows // 2), rows // 2)
        at = pl.ds((1 - h) * width, width)
        slot = 2 * len(single) + h + (part or 0)
        return pltpu.make_async_copy(result.at[h, take, :], out.at[take, at], sems.at[slot])

    prepare(0)
    fill(*work[0])
    for k, (h, n) in enumerate(work):
        if h == 0 and n == 2 * len(pairs):
            for copy in copies:
                copy.wait()
        at = pl.ds((1 - h) * width, width)
        last = k + 1 == len(work)

        @region(core, k)
        def _():
            rows = result.shape[1] // 2
            if not last and work[k + 1][0] == 0:
                prepare(work[k + 1][1])
            for part in range(2):
                take = pl.ds(part * rows, rows)
                term = product(items[n][0](take), rhs[h, n])
                result[h, take, :] = (partial[take, at] if n == 0 else result[h, take, :]) + term
                if last:
                    output(h, part).start()
                else:
                    fill(*work[k + 1], (part, 2))

        if h == 0 and n == count - 1:
            output(0).start()
    output(0).wait()
    output(1, 0).wait()
    output(1, 1).wait()


def kernel_call(body, **options):
    return pl.pallas_call(body, **options)


def local(spectrum, coupling, spatial_basis, noise_keys, noise_counters):
    steps, modes = coupling.shape
    vecs = noise_keys.shape[0]
    tm, space = lax.axis_size("tm"), lax.axis_size("space")
    chips = tm // 2
    nodes_here = spatial_basis.shape[0] // space
    half = nodes_here // 2
    keys, counters = noise_keys.reshape(1, vecs), noise_counters.reshape(1, vecs)
    f32 = lambda *shape: jax.ShapeDtypeStruct(shape, F32)
    bf16 = lambda *shape: jax.ShapeDtypeStruct(shape, BF16)
    fast = dict(compiler_params=LIMIT)
    in_hbm = [
        pltpu.with_memory_space_constraint(x, pltpu.HBM)
        for x in (coupling, spectrum.reshape(1, modes), spatial_basis, keys, counters)
    ]

    pairs, single = partners(space)
    routes = [(d, d) for d in single] + pairs
    sizes = [half + TAIL] * len(single) + [nodes_here + TAIL] * len(pairs)
    other = swap(coupling, "tm", 1)
    *messages, coup, spec, base = kernel_call(
        functools.partial(pack_kernel, "tm", "space", routes),
        out_shape=[bf16(n, modes) for n in sizes]
        + [f32(steps, modes), f32(1, modes), jax.ShapeDtypeStruct((vecs, 128), jnp.int32)],
        in_specs=[HBM] * 5,
        out_specs=[VMEM] * (len(sizes) + 3),
        scratch_shapes=[pltpu.VMEM((1, vecs), jnp.int32)] * 2 + [pltpu.SemaphoreType.DMA((len(sizes) + 4,))],
        **fast,
    )(*in_hbm)
    table, *messages = kernel_call(
        functools.partial(table_kernel, "tm", len(sizes)),
        out_shape=[f32(8, modes)] + [bf16(n, modes) for n in sizes],
        in_specs=[VMEM] * 3 + [ANY] * len(sizes),
        out_specs=[VMEM] + [ANY] * len(sizes),
        scratch_shapes=[pltpu.VMEM((TAIL, modes), BF16), pltpu.SemaphoreType.DMA((len(sizes),))],
        input_output_aliases={3 + i: 1 + i for i in range(len(sizes))},
        **fast,
    )(coup, other, spec, *messages)
    tables = [swap(table, "tm", 2 * e) for e in range(1, chips)]
    direct = [exchange(m, lambda t, s, r=r: (t, s ^ r[t % 2])) for m, r in zip(messages, routes)]

    def noise_of(offsets, after):
        count = len(offsets) * steps * vecs * modes
        return kernel_call(
            functools.partial(noise_kernel, "tm", "space", offsets, len(after)),
            out_shape=[f32(steps, vecs, modes)] * len(offsets),
            in_specs=[VMEM] + [ANY] * len(after),
            out_specs=[VMEM] * len(offsets),
            cost_estimate=pl.CostEstimate(flops=count * 60, transcendentals=count * 2, bytes_accessed=count * 4),
            **fast,
        )(base, *after)

    (own,) = noise_of([(0, 0)], (table,))
    state, sent, weights, sums = kernel_call(
        functools.partial(offset_kernel, "tm"),
        out_shape=[f32(vecs, modes), bf16(vecs, modes), f32(chips, 8, modes), f32(8, modes)],
        in_specs=[VMEM] * (4 + len(tables)),
        out_specs=[VMEM] * 4,
        scratch_shapes=[pltpu.VMEM((chips, 8, modes), F32)] + [pltpu.VMEM((steps, modes), F32)] * 2,
        **fast,
    )(own, coup, spec, table, *tables)
    total, late = kernel_call(
        functools.partial(combine_kernel, "tm"),
        out_shape=[bf16(vecs, modes), f32(vecs, modes)],
        in_specs=[VMEM] * 3,
        out_specs=[VMEM] * 2,
        **fast,
    )(state, swap(sent, "tm", 1), sums)
    later = [swap(total, "tm", 2 * e) for e in range(1, chips)]
    noise = list(noise_of([(d, d) for d in single], (total,)))
    noise += noise_of(pairs, (noise[-1],))
    carry = kernel_call(
        functools.partial(carry_kernel, "tm"),
        out_shape=bf16(vecs + 16, modes),
        in_specs=[VMEM] * (3 + len(later)) + [ANY],
        out_specs=VMEM,
        **fast,
    )(late, weights, sums, *later, noise[-1])
    carries = [swap(carry, "space", d) for d in range(1, space)]
    swapped = [swap(m, "tm", 1) for m in direct]
    noise += noise_of([r[::-1] for r in pairs], (carry,))

    flops = 2 * nodes_here * modes * steps * vecs
    half_cols = steps // 2 * vecs
    result = f32(nodes_here, steps * vecs)
    out = kernel_call(
        functools.partial(own_kernel, "space"),
        out_shape=result,
        in_specs=[VMEM, VMEM, HBM, VMEM, VMEM],
        out_specs=VMEM,
        scratch_shapes=[
            pltpu.VMEM((nodes_here, modes), BF16),
            pltpu.VMEM((2, half_cols, modes), BF16),
            pltpu.VMEM((vecs, modes), F32),
            pltpu.VMEM((2, steps, modes), F32),
            pltpu.SemaphoreType.DMA,
        ],
        cost_estimate=pl.CostEstimate(flops=flops, transcendentals=0, bytes_accessed=4 * steps * vecs * modes),
        **fast,
    )(coup, spec, spatial_basis, own, carry)
    count = space - 1
    return kernel_call(
        functools.partial(final_kernel, "tm", pairs, single),
        out_shape=result,
        in_specs=[VMEM] * (1 + len(direct) + len(swapped) + len(noise) + len(carries)),
        out_specs=HBM,
        scratch_shapes=[
            pltpu.VMEM((len(single), nodes_here, modes), BF16),
            pltpu.VMEM((2, count, half_cols, modes), BF16),
            pltpu.VMEM((count, vecs, modes), F32),
            pltpu.VMEM((count, 2, steps, modes), F32),
            pltpu.VMEM((2, nodes_here, half_cols), F32),
            pltpu.SemaphoreType.DMA((2 * len(single) + 3,)),
        ],
        cost_estimate=pl.CostEstimate(
            flops=flops * count, transcendentals=0, bytes_accessed=4 * steps * vecs * modes * count
        ),
        **fast,
    )(out, *direct, *swapped, *noise, *carries)


def solution(mesh):
    in_specs = (P("space"), P("tm", "space"), P(None, "space"), P(), P())
    out_specs = P("space", "tm")
    return jax.shard_map(local, mesh=mesh, in_specs=in_specs, out_specs=out_specs, check_vma=False)
```

```python
import functools

import jax
import jax.numpy as jnp
from jax import lax
from jax.experimental import pallas as pl
from jax.experimental.pallas import tpu as pltpu
from jax.sharding import PartitionSpec as P


F32 = jnp.float32
BF16 = jnp.bfloat16
VMEM = pl.BlockSpec(memory_space=pltpu.VMEM)
ANY = pl.BlockSpec(memory_space=pl.ANY)
HBM = pl.BlockSpec(memory_space=pltpu.HBM)
LIMIT = pltpu.CompilerParams(vmem_limit_bytes=24 << 20)
SINE = (6.28318516, -41.34165503, 81.60100406, -76.54978208, 39.53670436)


def partners(count):
    pairs = [(i, i + 1) for i in range(1, count - 2, 2)]
    return pairs, ([count - 1] if count > 1 else [])


def exchange(x, move):
    tm, space = lax.axis_size("tm"), lax.axis_size("space")
    moves = []
    for t in range(tm):
        for s in range(space):
            to = move(t, s)
            if to is not None:
                moves.append((t * space + s, to[0] * space + to[1]))
    return lax.ppermute(x, ("tm", "space"), moves)


def swap(x, axis, offset):
    count = lax.axis_size(axis)
    return lax.ppermute(x, axis, [(i, i ^ offset) for i in range(count)])


def split3(x):
    high = x.astype(BF16).astype(F32)
    rest = x - high
    middle = rest.astype(BF16).astype(F32)
    return high, middle, rest - middle


def mix_bits(state):
    state = state ^ lax.shift_right_logical(state, jnp.int32(16))
    state = state * jnp.int32(-2048144789)
    state = state ^ lax.shift_right_logical(state, jnp.int32(13))
    state = state * jnp.int32(-1028477387)
    return state ^ lax.shift_right_logical(state, jnp.int32(16))


def gaussian(seeded):
    first = mix_bits(seeded)
    second = mix_bits(first + jnp.int32(1013904223))
    unit = (lax.shift_right_logical(first, jnp.int32(8)).astype(F32) + 0.5) * (1.0 / 16777216.0)
    square = -2.0 * jnp.log(unit)
    radius = square * lax.rsqrt(jnp.maximum(square, 1e-30))
    turn = (lax.shift_right_arithmetic(second, jnp.int32(8)).astype(F32) + 0.5) * (1.0 / 16777216.0)
    w = 0.25 - jnp.abs(turn)
    z = w * w
    sine = SINE[4]
    for c in SINE[3::-1]:
        sine = sine * z + c
    return radius * (sine * w)


TAIL = 64


def pick(core, offsets):
    return offsets[0] if offsets[0] == offsets[1] else jnp.where(core == 0, offsets[0], offsets[1])


def pack_kernel(tm_axis, sp_axis, offsets, coup, spec, basis, keys, counters, *rest):
    *outs, coup_out, spec_out, base, key_row, counter_row, sems = rest
    me, sp = lax.axis_index(tm_axis), lax.axis_index(sp_axis)
    core = lax.rem(me, 2)
    copies = [
        pltpu.make_async_copy(coup, coup_out, sems.at[len(outs)]),
        pltpu.make_async_copy(spec, spec_out, sems.at[len(outs) + 1]),
    ]
    rows_in = [
        pltpu.make_async_copy(keys, key_row, sems.at[len(outs) + 2]),
        pltpu.make_async_copy(counters, counter_row, sems.at[len(outs) + 3]),
    ]
    for i, (out, offset) in enumerate(zip(outs, offsets)):
        rows = out.shape[0] - TAIL
        block = sp ^ pick(core, offset)
        if offset[0] == offset[1]:
            block = block * 2 + core
        start = pl.multiple_of(block * rows, rows)
        copies.append(
            pltpu.make_async_copy(basis.at[pl.ds(start, rows), :], out.at[pl.ds(0, rows), :], sems.at[i])
        )
    for copy in rows_in + copies:
        copy.start()
    for copy in rows_in:
        copy.wait()
    base_columns(key_row, counter_row, base)
    for copy in copies:
        copy.wait()


def totals(ref):
    product = square = total = None
    for t in range(ref.shape[0]):
        c = ref[pl.ds(t, 1), :]
        product = c if t == 0 else product * c
        square = c * c if t == 0 else square * (c * c)
        total = square if t == 0 else total + square
    return product, total


def joined(early, late):
    return early[0] * late[0], early[1] + (early[0] * early[0]) * late[1]


def table_rows(shape, rows):
    row = lax.broadcasted_iota(jnp.int32, shape, 0)
    table = jnp.zeros(shape, F32)
    for j, value in enumerate(rows):
        table = jnp.where(row == j, value, table)
    return table


def ordered(first, mine, theirs):
    early = tuple(jnp.where(first, x, y) for x, y in zip(mine, theirs))
    late = tuple(jnp.where(first, y, x) for x, y in zip(mine, theirs))
    return early, late


def table_kernel(tm_axis, count, coup, other, spec, *rest):
    out, *messages, tail, sems = rest[count:]
    first = lax.rem(lax.axis_index(tm_axis), 2) == 0
    (x,), (y,) = ordered(first, (coup[...],), (other[...],))
    parts = split3(x) + split3(y)
    parts = parts + (table_rows(x.shape, split3(spec[...])), jnp.zeros_like(x))
    for j in range(4):
        tail[pl.ds(16 * j, 16), :] = jnp.concatenate(parts[2 * j : 2 * j + 2], 0).astype(BF16)
    copies = []
    for i, message in enumerate(messages):
        rows = message.shape[0] - TAIL
        copies.append(pltpu.make_async_copy(tail, message.at[pl.ds(rows, TAIL), :], sems.at[i]))
        copies[-1].start()
    early, late = ordered(first, totals(coup), totals(other))
    out[...] = table_rows(out.shape, (*joined(early, late), *early, *late))
    for copy in copies:
        copy.wait()


def base_columns(keys, counters, base):
    vecs = base.shape[0]
    diagonal = lax.broadcasted_iota(jnp.int32, (vecs, vecs), 0) == lax.broadcasted_iota(
        jnp.int32, (vecs, vecs), 1
    )

    def column(ref):
        row = jnp.broadcast_to(ref[...].astype(F32), (vecs, vecs))
        return jnp.sum(jnp.where(diagonal, row, 0.0), axis=1, keepdims=True).astype(jnp.int32)

    start = column(keys) * jnp.int32(668265261) + column(counters) * jnp.int32(374761393)
    base[...] = jnp.broadcast_to(start, base.shape)


def noise_kernel(tm_axis, sp_axis, offsets, extras, base, *rest):
    outs = rest[extras:]
    steps, vecs, modes = outs[0].shape
    me, sp = lax.axis_index(tm_axis), lax.axis_index(sp_axis)
    group = 8
    for out, offset in zip(outs, offsets):
        ids = (sp ^ pick(lax.rem(me, 2), offset)) * modes + lax.broadcasted_iota(jnp.int32, (1, modes), 1)
        lane = ids * jnp.int32(-1640531535)
        first_step = me * steps

        def step(t, _):
            shifted = lane + (first_step + t) * jnp.int32(374761393)
            for v in range(vecs // group):
                seeded = jnp.tile(base[pl.ds(v * group, group), :], (1, modes // 128)) + shifted
                out[t, pl.ds(v * group, group), :] = gaussian(seeded)
            return 0

        lax.fori_loop(0, steps, step, 0)


def running(x, combine, identity):
    row = lax.broadcasted_iota(jnp.int32, x.shape, 0)
    shift = 1
    while shift < x.shape[0]:
        x = combine(x, jnp.where(row < shift, identity, pltpu.roll(x, shift, 0)))
        shift *= 2
    return x


def chain(c, spec, d_start, f_start):
    total = running(running(c * c, jnp.multiply, 1.0), jnp.add, 0.0)
    behind = d_start + f_start * total
    row = lax.broadcasted_iota(jnp.int32, c.shape, 0)
    ratio = jnp.where(row == 0, d_start, pltpu.roll(behind, 1, 0)) / behind
    return jnp.sqrt(ratio / spec), ratio


def after(start, total):
    return start[0] + start[1] * total[1], start[1] * (total[0] * total[0])


def select(flag, x, y):
    return tuple(jnp.where(flag, p, q) for p, q in zip(x, y))


def gain_of(start, total):
    return total[0] * start[0] / (start[0] + start[1] * total[1])


def offset_kernel(tm_axis, noise, coup, spec, table, *rest):
    received, rest = rest[:-7], rest[-7:]
    o_ref, sent, wts, df, tables, alpha, beta = rest
    steps, vecs, modes = noise.shape
    me = lax.axis_index(tm_axis)
    chip = me // 2
    first = lax.rem(me, 2) == 0
    one = jnp.ones((1, modes), F32)
    tables[chip] = table[...]
    for e, ref in enumerate(received):
        tables[chip ^ (e + 1)] = ref[...]
    now, start, weight = (one, one), (one, one), jnp.zeros((1, modes), F32)
    for b in range(tables.shape[0]):
        wts[b] = jnp.broadcast_to(weight, (8, modes))
        total = tables[b, pl.ds(0, 1), :], tables[b, pl.ds(1, 1), :]
        here = chip == b
        start = select(here, now, start)
        weight = jnp.where(here, 1.0, weight * gain_of(now, total))
        now = after(now, total)
    early = table[pl.ds(2, 1), :], table[pl.ds(3, 1), :]
    late = table[pl.ds(4, 1), :], table[pl.ds(5, 1), :]
    second = after(start, early)
    gain_early, gain_late = gain_of(start, early), gain_of(second, late)
    own = select(first, start, second)
    df[...] = table_rows((8, modes), (*own, gain_early, gain_late))
    c = coup[...]
    a, ratio = chain(c, spec[...], *own)
    alpha[...] = c * a
    beta[...] = c * ratio

    def tile(v, _):
        at = pl.ds(pl.multiple_of(v * 16, 16), 16)
        carry = jnp.zeros((16, modes), F32)
        for t in range(steps - 1, -1, -1):
            carry = alpha[pl.ds(t, 1), :] * noise[t, at, :] + beta[pl.ds(t, 1), :] * carry
        o_ref[at, :] = carry
        sent[at, :] = carry.astype(BF16)
        return 0

    lax.fori_loop(0, vecs // 16, tile, 0)


def combine_kernel(tm_axis, own, other, df, out, late):
    core = lax.rem(lax.axis_index(tm_axis), 2)
    first = core == 0
    half = out.shape[0]
    late[...] = jnp.where(first, other[...].astype(F32), own[...])
    at = pl.ds(pl.multiple_of(core * half, half), half)
    x, y = own[at, :], other[at, :].astype(F32)
    out[...] = (jnp.where(first, x, y) + df[pl.ds(2, 1), :] * jnp.where(first, y, x)).astype(BF16)


def half_kernel(tm_axis, wts, *rest):
    *received, _, out, sent = rest
    chip = lax.axis_index(tm_axis) // 2
    carry = jnp.zeros(out.shape, F32)
    for e, ref in enumerate(received):
        carry = carry + wts[chip ^ (e + 1)][0:1, :] * ref[...].astype(F32)
    out[...] = carry
    sent[...] = carry.astype(BF16)


def carry_kernel(tm_axis, mine, theirs, late, df, _, out):
    half, modes = mine.shape
    core = lax.rem(lax.axis_index(tm_axis), 2)
    gain = df[pl.ds(3, 1), :]
    for j in range(2):
        at = pl.ds(j * half, half)
        carry = jnp.where(core == j, mine[...], theirs[...].astype(F32))
        out[at, :] = jnp.where(core == 0, late[at, :] + gain * carry, carry).astype(BF16)
    parts = split3(df[pl.ds(0, 1), :]) + split3(df[pl.ds(1, 1), :])
    out[pl.ds(2 * half, 16), :] = table_rows((16, modes), parts).astype(BF16)


def sums_of(block):
    return block[0:1] + block[1:2] + block[2:3], block[3:4] + block[4:5] + block[5:6]


def set_coefs(coefs, c, lam, sums):
    a, ratio = chain(c, lam, *sums)
    row = lax.broadcasted_iota(jnp.int32, c.shape, 0)
    steps = c.shape[0]
    coefs[0] = a
    coefs[1] = ratio * jnp.where(row == steps - 1, 1.0, pltpu.roll(c, steps - 1, 0))


def values(noise, start, coefs, state, rhs, times, part=(0, 1)):
    vecs = noise.shape[1]
    share = vecs // part[1]
    for v in range(part[0] * share, (part[0] + 1) * share, 16):
        at = pl.ds(v, 16)
        value = start(at)
        for n, t in enumerate(times):
            row = pl.ds(t, 1)
            value = coefs[0, row, :] * noise[t, at, :] + coefs[1, row, :] * value
            rhs[pl.ds((len(times) - 1 - n) * vecs + v, 16), :] = value.astype(BF16)
        if times[-1]:
            state[at, :] = value


def product(lhs, rhs):
    return lax.dot_general(lhs, rhs, (((1,), (1,)), ((), ())), preferred_element_type=F32)


def halves_of(steps):
    times = list(range(steps - 1, -1, -1))
    return times[: steps // 2], times[steps // 2 :]


def own_kernel(sp_axis, coup, spec, basis, noise, message, out, lhs, rhs, state, coefs, sem):
    rows = lhs.shape[0]
    steps, vecs, _ = noise.shape
    start = pl.multiple_of(lax.axis_index(sp_axis) * rows, rows)
    copy = pltpu.make_async_copy(basis.at[pl.ds(start, rows), :], lhs, sem)
    copy.start()
    set_coefs(coefs, coup[...], spec[...], sums_of(message[pl.ds(vecs, 16), :].astype(F32)))
    late, early = halves_of(steps)
    width = vecs * len(late)
    values(noise, lambda at: message[at, :].astype(F32), coefs, state, rhs.at[0], late)
    copy.wait()
    values(noise, lambda at: state[at, :], coefs, state, rhs.at[1], early)
    out[:, pl.ds(width, width)] = product(lhs[...], rhs[0])
    out[:, pl.ds(0, width)] = product(lhs[...], rhs[1])


def final_kernel(tm_axis, pairs, single, partial, *rest):
    fetched = len(pairs) + len(single)
    count = 2 * len(pairs) + len(single)
    direct, rest = rest[:fetched], rest[fetched:]
    swapped, rest = rest[:fetched], rest[fetched:]
    noise, rest = rest[:count], rest[count:]
    messages, rest = rest[:count], rest[count:]
    out, lhs, rhs, state, coefs, result, sems = rest
    steps, vecs, _ = noise[0].shape
    core = lax.rem(lax.axis_index(tm_axis), 2)
    first = core == 0
    copies = []
    for i in range(len(single)):
        rows = lhs.shape[1] // 2
        for j, source in enumerate((direct[i], swapped[i])):
            at = pl.multiple_of((core if j == 0 else 1 - core) * rows, rows)
            copies.append(
                pltpu.make_async_copy(
                    source.at[pl.ds(0, rows), :], lhs.at[i, pl.ds(at, rows), :], sems.at[2 * i + j]
                )
            )
            copies[-1].start()

    def chosen(x, y):
        return lambda at: jnp.where(first, messages[x][at, :].astype(F32), messages[y][at, :].astype(F32))

    items = []
    for j, (x, y) in enumerate(pairs):
        i = len(single) + j
        rows = direct[i].shape[0] - TAIL
        near = lambda i=i, rows=rows: direct[i][pl.ds(0, rows), :]
        far = lambda i=i, rows=rows: swapped[i][pl.ds(0, rows), :]
        items.append((near, direct[i], noise[len(single) + j], chosen(x - 1, y - 1)))
        items.append((far, swapped[i], noise[len(single) + len(pairs) + j], chosen(y - 1, x - 1)))
    for i, d in enumerate(single):
        items.append((lambda i=i: lhs[i], direct[i], noise[i], chosen(d - 1, d - 1)))
    for n, (_, source, _, message) in enumerate(items):
        rows = source.shape[0] - TAIL
        x = [source[pl.ds(rows + 16 * j, 16), :].astype(F32) for j in range(4)]
        before = x[0][0:8] + x[0][8:16] + x[1][0:8]
        behind = x[1][8:16] + x[2][0:8] + x[2][8:16]
        lam = x[3][0:1] + x[3][1:2] + x[3][2:3]
        set_coefs(coefs.at[n], jnp.where(first, before, behind), lam, sums_of(message(pl.ds(vecs, 16))))
    late, early = halves_of(steps)
    width = vecs * len(late)
    work = [(h, n) for h in range(2) for n in range(count)]

    def fill(h, n):
        start = items[n][3] if h == 0 else lambda at: state[n, at, :]
        values(items[n][2], start, coefs.at[n], state.at[n], rhs.at[h, n], late if h == 0 else early)

    fill(*work[0])
    outs = []
    for k, (h, n) in enumerate(work):
        if k + 1 < len(work):
            fill(*work[k + 1])
        if h == 0 and n == count - len(single):
            for copy in copies:
                copy.wait()
        term = product(items[n][0](), rhs[h, n])
        at = pl.ds((1 - h) * width, width)
        result[h] = (partial[:, at] if n == 0 else result[h]) + term
        if n == count - 1:
            outs.append(pltpu.make_async_copy(result.at[h], out.at[:, at], sems.at[2 * len(single) + h]))
            outs[-1].start()
    for copy in outs:
        copy.wait()


def kernel_call(body, **options):
    return pl.pallas_call(body, **options)


def local(spectrum, coupling, spatial_basis, noise_keys, noise_counters):
    steps, modes = coupling.shape
    vecs = noise_keys.shape[0]
    tm, space = lax.axis_size("tm"), lax.axis_size("space")
    chips = tm // 2
    nodes_here = spatial_basis.shape[0] // space
    half = nodes_here // 2
    keys, counters = noise_keys.reshape(1, vecs), noise_counters.reshape(1, vecs)
    f32 = lambda *shape: jax.ShapeDtypeStruct(shape, F32)
    bf16 = lambda *shape: jax.ShapeDtypeStruct(shape, BF16)
    fast = dict(compiler_params=LIMIT)
    in_hbm = [
        pltpu.with_memory_space_constraint(x, pltpu.HBM)
        for x in (coupling, spectrum.reshape(1, modes), spatial_basis, keys, counters)
    ]

    pairs, single = partners(space)
    routes = [(d, d) for d in single] + pairs
    sizes = [half + TAIL] * len(single) + [nodes_here + TAIL] * len(pairs)
    other = swap(coupling, "tm", 1)
    *messages, coup, spec, base = kernel_call(
        functools.partial(pack_kernel, "tm", "space", routes),
        out_shape=[bf16(n, modes) for n in sizes]
        + [f32(steps, modes), f32(1, modes), jax.ShapeDtypeStruct((vecs, 128), jnp.int32)],
        in_specs=[HBM] * 5,
        out_specs=[VMEM] * (len(sizes) + 3),
        scratch_shapes=[pltpu.VMEM((1, vecs), jnp.int32)] * 2 + [pltpu.SemaphoreType.DMA((len(sizes) + 4,))],
        **fast,
    )(*in_hbm)
    table, *messages = kernel_call(
        functools.partial(table_kernel, "tm", len(sizes)),
        out_shape=[f32(8, modes)] + [bf16(n, modes) for n in sizes],
        in_specs=[VMEM] * 3 + [ANY] * len(sizes),
        out_specs=[VMEM] + [ANY] * len(sizes),
        scratch_shapes=[pltpu.VMEM((TAIL, modes), BF16), pltpu.SemaphoreType.DMA((len(sizes),))],
        input_output_aliases={3 + i: 1 + i for i in range(len(sizes))},
        **fast,
    )(coup, other, spec, *messages)
    tables = [swap(table, "tm", 2 * e) for e in range(1, chips)]
    direct = [exchange(m, lambda t, s, r=r: (t, s ^ r[t % 2])) for m, r in zip(messages, routes)]

    def noise_of(offsets, after):
        count = len(offsets) * steps * vecs * modes
        return kernel_call(
            functools.partial(noise_kernel, "tm", "space", offsets, len(after)),
            out_shape=[f32(steps, vecs, modes)] * len(offsets),
            in_specs=[VMEM] + [ANY] * len(after),
            out_specs=[VMEM] * len(offsets),
            cost_estimate=pl.CostEstimate(flops=count * 60, transcendentals=count * 2, bytes_accessed=count * 4),
            **fast,
        )(base, *after)

    (own,) = noise_of([(0, 0)], (table,))
    state, sent, weights, sums = kernel_call(
        functools.partial(offset_kernel, "tm"),
        out_shape=[f32(vecs, modes), bf16(vecs, modes), f32(chips, 8, modes), f32(8, modes)],
        in_specs=[VMEM] * (4 + len(tables)),
        out_specs=[VMEM] * 4,
        scratch_shapes=[pltpu.VMEM((chips, 8, modes), F32)] + [pltpu.VMEM((steps, modes), F32)] * 2,
        **fast,
    )(own, coup, spec, table, *tables)
    total, late = kernel_call(
        functools.partial(combine_kernel, "tm"),
        out_shape=[bf16(vecs // 2, modes), f32(vecs, modes)],
        in_specs=[VMEM] * 3,
        out_specs=[VMEM] * 2,
        **fast,
    )(state, swap(sent, "tm", 1), sums)
    later = [swap(total, "tm", 2 * e) for e in range(1, chips)]
    noise = list(noise_of([(d, d) for d in single], (total,)))
    mine, sent = kernel_call(
        functools.partial(half_kernel, "tm"),
        out_shape=[f32(vecs // 2, modes), bf16(vecs // 2, modes)],
        in_specs=[VMEM] * (1 + len(later)) + [ANY],
        out_specs=[VMEM] * 2,
        **fast,
    )(weights, *later, noise[-1])
    theirs = swap(sent, "tm", 1)
    noise += noise_of(pairs, (sent,))
    carry = kernel_call(
        functools.partial(carry_kernel, "tm"),
        out_shape=bf16(vecs + 16, modes),
        in_specs=[VMEM] * 4 + [ANY],
        out_specs=VMEM,
        **fast,
    )(mine, theirs, late, sums, noise[-1])
    carries = [swap(carry, "space", d) for d in range(1, space)]
    swapped = [swap(m, "tm", 1) for m in direct]
    noise += noise_of([r[::-1] for r in pairs], (carry,))

    flops = 2 * nodes_here * modes * steps * vecs
    half_cols = steps // 2 * vecs
    result = f32(nodes_here, steps * vecs)
    out = kernel_call(
        functools.partial(own_kernel, "space"),
        out_shape=result,
        in_specs=[VMEM, VMEM, HBM, VMEM, VMEM],
        out_specs=VMEM,
        scratch_shapes=[
            pltpu.VMEM((nodes_here, modes), BF16),
            pltpu.VMEM((2, half_cols, modes), BF16),
            pltpu.VMEM((vecs, modes), F32),
            pltpu.VMEM((2, steps, modes), F32),
            pltpu.SemaphoreType.DMA,
        ],
        cost_estimate=pl.CostEstimate(flops=flops, transcendentals=0, bytes_accessed=4 * steps * vecs * modes),
        **fast,
    )(coup, spec, spatial_basis, own, carry)
    count = space - 1
    return kernel_call(
        functools.partial(final_kernel, "tm", pairs, single),
        out_shape=result,
        in_specs=[VMEM] * (1 + len(direct) + len(swapped) + len(noise) + len(carries)),
        out_specs=HBM,
        scratch_shapes=[
            pltpu.VMEM((len(single), nodes_here, modes), BF16),
            pltpu.VMEM((2, count, half_cols, modes), BF16),
            pltpu.VMEM((count, vecs, modes), F32),
            pltpu.VMEM((count, 2, steps, modes), F32),
            pltpu.VMEM((2, nodes_here, half_cols), F32),
            pltpu.SemaphoreType.DMA((2 * len(single) + 2,)),
        ],
        cost_estimate=pl.CostEstimate(
            flops=flops * count, transcendentals=0, bytes_accessed=4 * steps * vecs * modes * count
        ),
        **fast,
    )(out, *direct, *swapped, *noise, *carries)


def solution(mesh):
    in_specs = (P("space"), P("tm", "space"), P(None, "space"), P(), P())
    out_specs = P("space", "tm")
    return jax.shard_map(local, mesh=mesh, in_specs=in_specs, out_specs=out_specs, check_vma=False)
```

```python
import functools

import jax
import jax.numpy as jnp
from jax import lax
from jax.experimental import pallas as pl
from jax.experimental.pallas import tpu as pltpu
from jax.sharding import PartitionSpec as P


F32 = jnp.float32
BF16 = jnp.bfloat16
VMEM = pl.BlockSpec(memory_space=pltpu.VMEM)
ANY = pl.BlockSpec(memory_space=pl.ANY)
HBM = pl.BlockSpec(memory_space=pltpu.HBM)
LIMIT = pltpu.CompilerParams(vmem_limit_bytes=24 << 20)
SINE = (6.28318516, -41.34165503, 81.60100406, -76.54978208, 39.53670436)


def partners(count):
    pairs = [(i, i + 1) for i in range(1, count - 2, 2)]
    return pairs, ([count - 1] if count > 1 else [])


def exchange(x, move):
    tm, space = lax.axis_size("tm"), lax.axis_size("space")
    moves = []
    for t in range(tm):
        for s in range(space):
            to = move(t, s)
            if to is not None:
                moves.append((t * space + s, to[0] * space + to[1]))
    return lax.ppermute(x, ("tm", "space"), moves)


def swap(x, axis, offset):
    count = lax.axis_size(axis)
    return lax.ppermute(x, axis, [(i, i ^ offset) for i in range(count)])


def split3(x):
    high = x.astype(BF16).astype(F32)
    rest = x - high
    middle = rest.astype(BF16).astype(F32)
    return high, middle, rest - middle


def mix_bits(state):
    state = state ^ lax.shift_right_logical(state, jnp.int32(16))
    state = state * jnp.int32(-2048144789)
    state = state ^ lax.shift_right_logical(state, jnp.int32(13))
    state = state * jnp.int32(-1028477387)
    return state ^ lax.shift_right_logical(state, jnp.int32(16))


def gaussian(seeded):
    first = mix_bits(seeded)
    second = mix_bits(first + jnp.int32(1013904223))
    unit = (lax.shift_right_logical(first, jnp.int32(8)).astype(F32) + 0.5) * (1.0 / 16777216.0)
    square = -2.0 * jnp.log(unit)
    radius = square * lax.rsqrt(jnp.maximum(square, 1e-30))
    turn = (lax.shift_right_arithmetic(second, jnp.int32(8)).astype(F32) + 0.5) * (1.0 / 16777216.0)
    w = 0.25 - jnp.abs(turn)
    z = w * w
    sine = SINE[4]
    for c in SINE[3::-1]:
        sine = sine * z + c
    return radius * (sine * w)


TAIL = 64


def pick(core, offsets):
    return offsets[0] if offsets[0] == offsets[1] else jnp.where(core == 0, offsets[0], offsets[1])


def pack_kernel(tm_axis, sp_axis, offsets, coup, spec, basis, keys, counters, *rest):
    *outs, coup_out, spec_out, base, key_row, counter_row, sems = rest
    me, sp = lax.axis_index(tm_axis), lax.axis_index(sp_axis)
    core = lax.rem(me, 2)
    copies = [
        pltpu.make_async_copy(coup, coup_out, sems.at[len(outs)]),
        pltpu.make_async_copy(spec, spec_out, sems.at[len(outs) + 1]),
    ]
    rows_in = [
        pltpu.make_async_copy(keys, key_row, sems.at[len(outs) + 2]),
        pltpu.make_async_copy(counters, counter_row, sems.at[len(outs) + 3]),
    ]
    for i, (out, offset) in enumerate(zip(outs, offsets)):
        rows = out.shape[0] - TAIL
        block = sp ^ pick(core, offset)
        if offset[0] == offset[1]:
            block = block * 2 + core
        start = pl.multiple_of(block * rows, rows)
        copies.append(
            pltpu.make_async_copy(basis.at[pl.ds(start, rows), :], out.at[pl.ds(0, rows), :], sems.at[i])
        )
    for copy in rows_in + copies:
        copy.start()
    for copy in rows_in:
        copy.wait()
    base_columns(key_row, counter_row, base)
    for copy in copies:
        copy.wait()


def totals(ref):
    product = square = total = None
    for t in range(ref.shape[0]):
        c = ref[pl.ds(t, 1), :]
        product = c if t == 0 else product * c
        square = c * c if t == 0 else square * (c * c)
        total = square if t == 0 else total + square
    return product, total


def joined(early, late):
    return early[0] * late[0], early[1] + (early[0] * early[0]) * late[1]


def table_rows(shape, rows):
    row = lax.broadcasted_iota(jnp.int32, shape, 0)
    table = jnp.zeros(shape, F32)
    for j, value in enumerate(rows):
        table = jnp.where(row == j, value, table)
    return table


def ordered(first, mine, theirs):
    early = tuple(jnp.where(first, x, y) for x, y in zip(mine, theirs))
    late = tuple(jnp.where(first, y, x) for x, y in zip(mine, theirs))
    return early, late


def table_kernel(tm_axis, count, coup, other, spec, *rest):
    out, *messages, tail, sems = rest[count:]
    first = lax.rem(lax.axis_index(tm_axis), 2) == 0
    (x,), (y,) = ordered(first, (coup[...],), (other[...],))
    parts = split3(x) + split3(y)
    parts = parts + (table_rows(x.shape, split3(spec[...])), jnp.zeros_like(x))
    for j in range(4):
        tail[pl.ds(16 * j, 16), :] = jnp.concatenate(parts[2 * j : 2 * j + 2], 0).astype(BF16)
    copies = []
    for i, message in enumerate(messages):
        rows = message.shape[0] - TAIL
        copies.append(pltpu.make_async_copy(tail, message.at[pl.ds(rows, TAIL), :], sems.at[i]))
        copies[-1].start()
    early, late = ordered(first, totals(coup), totals(other))
    out[...] = table_rows(out.shape, (*joined(early, late), *early, *late))
    for copy in copies:
        copy.wait()


def base_columns(keys, counters, base):
    vecs = base.shape[0]
    diagonal = lax.broadcasted_iota(jnp.int32, (vecs, vecs), 0) == lax.broadcasted_iota(
        jnp.int32, (vecs, vecs), 1
    )

    def column(ref):
        row = jnp.broadcast_to(ref[...].astype(F32), (vecs, vecs))
        return jnp.sum(jnp.where(diagonal, row, 0.0), axis=1, keepdims=True).astype(jnp.int32)

    start = column(keys) * jnp.int32(668265261) + column(counters) * jnp.int32(374761393)
    base[...] = jnp.broadcast_to(start, base.shape)


def noise_kernel(tm_axis, sp_axis, offsets, extras, base, *rest):
    outs = rest[extras:]
    steps, vecs, modes = outs[0].shape
    me, sp = lax.axis_index(tm_axis), lax.axis_index(sp_axis)
    group = 8
    for out, offset in zip(outs, offsets):
        ids = (sp ^ pick(lax.rem(me, 2), offset)) * modes + lax.broadcasted_iota(jnp.int32, (1, modes), 1)
        lane = ids * jnp.int32(-1640531535)
        first_step = me * steps

        def step(t, _):
            shifted = lane + (first_step + t) * jnp.int32(374761393)
            for v in range(vecs // group):
                seeded = jnp.tile(base[pl.ds(v * group, group), :], (1, modes // 128)) + shifted
                out[t, pl.ds(v * group, group), :] = gaussian(seeded)
            return 0

        lax.fori_loop(0, steps, step, 0)


def running(x, combine, identity):
    row = lax.broadcasted_iota(jnp.int32, x.shape, 0)
    shift = 1
    while shift < x.shape[0]:
        x = combine(x, jnp.where(row < shift, identity, pltpu.roll(x, shift, 0)))
        shift *= 2
    return x


def chain(c, spec, d_start, f_start):
    total = running(running(c * c, jnp.multiply, 1.0), jnp.add, 0.0)
    behind = d_start + f_start * total
    row = lax.broadcasted_iota(jnp.int32, c.shape, 0)
    ratio = jnp.where(row == 0, d_start, pltpu.roll(behind, 1, 0)) / behind
    return jnp.sqrt(ratio / spec), ratio


def after(start, total):
    return start[0] + start[1] * total[1], start[1] * (total[0] * total[0])


def select(flag, x, y):
    return tuple(jnp.where(flag, p, q) for p, q in zip(x, y))


def gain_of(start, total):
    return total[0] * start[0] / (start[0] + start[1] * total[1])


def offset_kernel(tm_axis, noise, coup, spec, table, *rest):
    received, rest = rest[:-7], rest[-7:]
    o_ref, sent, wts, df, tables, alpha, beta = rest
    steps, vecs, modes = noise.shape
    me = lax.axis_index(tm_axis)
    chip = me // 2
    first = lax.rem(me, 2) == 0
    one = jnp.ones((1, modes), F32)
    tables[chip] = table[...]
    for e, ref in enumerate(received):
        tables[chip ^ (e + 1)] = ref[...]
    now, start, weight = (one, one), (one, one), jnp.zeros((1, modes), F32)
    for b in range(tables.shape[0]):
        wts[b] = jnp.broadcast_to(weight, (8, modes))
        total = tables[b, pl.ds(0, 1), :], tables[b, pl.ds(1, 1), :]
        here = chip == b
        start = select(here, now, start)
        weight = jnp.where(here, 1.0, weight * gain_of(now, total))
        now = after(now, total)
    early = table[pl.ds(2, 1), :], table[pl.ds(3, 1), :]
    late = table[pl.ds(4, 1), :], table[pl.ds(5, 1), :]
    second = after(start, early)
    gain_early, gain_late = gain_of(start, early), gain_of(second, late)
    own = select(first, start, second)
    df[...] = table_rows((8, modes), (*own, gain_early, gain_late))
    c = coup[...]
    a, ratio = chain(c, spec[...], *own)
    alpha[...] = c * a
    beta[...] = c * ratio

    def tile(v, _):
        at = pl.ds(pl.multiple_of(v * 16, 16), 16)
        carry = jnp.zeros((16, modes), F32)
        for t in range(steps - 1, -1, -1):
            carry = alpha[pl.ds(t, 1), :] * noise[t, at, :] + beta[pl.ds(t, 1), :] * carry
        o_ref[at, :] = carry
        sent[at, :] = carry.astype(BF16)
        return 0

    lax.fori_loop(0, vecs // 16, tile, 0)


def combine_kernel(tm_axis, own, other, df, out, late):
    core = lax.rem(lax.axis_index(tm_axis), 2)
    first = core == 0
    half = out.shape[0]
    late[...] = jnp.where(first, other[...].astype(F32), own[...])
    at = pl.ds(pl.multiple_of(core * half, half), half)
    x, y = own[at, :], other[at, :].astype(F32)
    out[...] = (jnp.where(first, x, y) + df[pl.ds(2, 1), :] * jnp.where(first, y, x)).astype(BF16)


def half_kernel(tm_axis, wts, *rest):
    *received, _, out, sent = rest
    chip = lax.axis_index(tm_axis) // 2
    carry = jnp.zeros(out.shape, F32)
    for e, ref in enumerate(received):
        carry = carry + wts[chip ^ (e + 1)][0:1, :] * ref[...].astype(F32)
    out[...] = carry
    sent[...] = carry.astype(BF16)


def carry_kernel(tm_axis, mine, theirs, late, df, out):
    half, modes = mine.shape
    core = lax.rem(lax.axis_index(tm_axis), 2)
    gain = df[pl.ds(3, 1), :]
    for j in range(2):
        at = pl.ds(j * half, half)
        carry = jnp.where(core == j, mine[...], theirs[...].astype(F32))
        out[at, :] = jnp.where(core == 0, late[at, :] + gain * carry, carry).astype(BF16)
    parts = split3(df[pl.ds(0, 1), :]) + split3(df[pl.ds(1, 1), :])
    out[pl.ds(2 * half, 16), :] = table_rows((16, modes), parts).astype(BF16)


def sums_of(block):
    return block[0:1] + block[1:2] + block[2:3], block[3:4] + block[4:5] + block[5:6]


def set_coefs(coefs, c, lam, sums):
    a, ratio = chain(c, lam, *sums)
    row = lax.broadcasted_iota(jnp.int32, c.shape, 0)
    steps = c.shape[0]
    coefs[0] = a
    coefs[1] = ratio * jnp.where(row == steps - 1, 1.0, pltpu.roll(c, steps - 1, 0))


def values(noise, start, coefs, state, rhs, times, part=(0, 1)):
    vecs = noise.shape[1]
    share = vecs // part[1]
    for v in range(part[0] * share, (part[0] + 1) * share, 16):
        at = pl.ds(v, 16)
        value = start(at)
        for n, t in enumerate(times):
            row = pl.ds(t, 1)
            value = coefs[0, row, :] * noise[t, at, :] + coefs[1, row, :] * value
            rhs[pl.ds((len(times) - 1 - n) * vecs + v, 16), :] = value.astype(BF16)
        if times[-1]:
            state[at, :] = value


def product(lhs, rhs):
    return lax.dot_general(lhs, rhs, (((1,), (1,)), ((), ())), preferred_element_type=F32)


def halves_of(steps):
    times = list(range(steps - 1, -1, -1))
    return times[: steps // 2], times[steps // 2 :]


def own_kernel(sp_axis, coup, spec, basis, noise, message, out, lhs, rhs, state, coefs, sem):
    rows = lhs.shape[0]
    steps, vecs, _ = noise.shape
    start = pl.multiple_of(lax.axis_index(sp_axis) * rows, rows)
    copy = pltpu.make_async_copy(basis.at[pl.ds(start, rows), :], lhs, sem)
    copy.start()
    set_coefs(coefs, coup[...], spec[...], sums_of(message[pl.ds(vecs, 16), :].astype(F32)))
    late, early = halves_of(steps)
    width = vecs * len(late)
    values(noise, lambda at: message[at, :].astype(F32), coefs, state, rhs.at[0], late)
    copy.wait()
    values(noise, lambda at: state[at, :], coefs, state, rhs.at[1], early)
    out[:, pl.ds(width, width)] = product(lhs[...], rhs[0])
    out[:, pl.ds(0, width)] = product(lhs[...], rhs[1])


def final_kernel(tm_axis, pairs, single, partial, *rest):
    fetched = len(pairs) + len(single)
    count = 2 * len(pairs) + len(single)
    direct, rest = rest[:fetched], rest[fetched:]
    swapped, rest = rest[:fetched], rest[fetched:]
    noise, rest = rest[:count], rest[count:]
    messages, rest = rest[:count], rest[count:]
    out, lhs, rhs, state, coefs, result, sems = rest
    steps, vecs, _ = noise[0].shape
    core = lax.rem(lax.axis_index(tm_axis), 2)
    first = core == 0
    copies = []
    for i in range(len(single)):
        rows = lhs.shape[1] // 2
        for j, source in enumerate((direct[i], swapped[i])):
            at = pl.multiple_of((core if j == 0 else 1 - core) * rows, rows)
            copies.append(
                pltpu.make_async_copy(
                    source.at[pl.ds(0, rows), :], lhs.at[i, pl.ds(at, rows), :], sems.at[2 * i + j]
                )
            )
            copies[-1].start()

    def chosen(x, y):
        return lambda at: jnp.where(first, messages[x][at, :].astype(F32), messages[y][at, :].astype(F32))

    items = []
    for j, (x, y) in enumerate(pairs):
        i = len(single) + j
        rows = direct[i].shape[0] - TAIL
        near = lambda i=i, rows=rows: direct[i][pl.ds(0, rows), :]
        far = lambda i=i, rows=rows: swapped[i][pl.ds(0, rows), :]
        items.append((near, direct[i], noise[len(single) + j], chosen(x - 1, y - 1)))
        items.append((far, swapped[i], noise[len(single) + len(pairs) + j], chosen(y - 1, x - 1)))
    for i, d in enumerate(single):
        items.append((lambda i=i: lhs[i], direct[i], noise[i], chosen(d - 1, d - 1)))
    for n, (_, source, _, message) in enumerate(items):
        rows = source.shape[0] - TAIL
        x = [source[pl.ds(rows + 16 * j, 16), :].astype(F32) for j in range(4)]
        before = x[0][0:8] + x[0][8:16] + x[1][0:8]
        behind = x[1][8:16] + x[2][0:8] + x[2][8:16]
        lam = x[3][0:1] + x[3][1:2] + x[3][2:3]
        set_coefs(coefs.at[n], jnp.where(first, before, behind), lam, sums_of(message(pl.ds(vecs, 16))))
    late, early = halves_of(steps)
    width = vecs * len(late)
    work = [(h, n) for h in range(2) for n in range(count)]

    def fill(h, n):
        start = items[n][3] if h == 0 else lambda at: state[n, at, :]
        values(items[n][2], start, coefs.at[n], state.at[n], rhs.at[h, n], late if h == 0 else early)

    fill(*work[0])
    outs = []
    for k, (h, n) in enumerate(work):
        if k + 1 < len(work):
            fill(*work[k + 1])
        if h == 0 and n == count - len(single):
            for copy in copies:
                copy.wait()
        term = product(items[n][0](), rhs[h, n])
        at = pl.ds((1 - h) * width, width)
        result[h] = (partial[:, at] if n == 0 else result[h]) + term
        if n == count - 1:
            outs.append(pltpu.make_async_copy(result.at[h], out.at[:, at], sems.at[2 * len(single) + h]))
            outs[-1].start()
    for copy in outs:
        copy.wait()


def kernel_call(body, **options):
    return pl.pallas_call(body, **options)


def local(spectrum, coupling, spatial_basis, noise_keys, noise_counters):
    steps, modes = coupling.shape
    vecs = noise_keys.shape[0]
    tm, space = lax.axis_size("tm"), lax.axis_size("space")
    chips = tm // 2
    nodes_here = spatial_basis.shape[0] // space
    half = nodes_here // 2
    keys, counters = noise_keys.reshape(1, vecs), noise_counters.reshape(1, vecs)
    f32 = lambda *shape: jax.ShapeDtypeStruct(shape, F32)
    bf16 = lambda *shape: jax.ShapeDtypeStruct(shape, BF16)
    fast = dict(compiler_params=LIMIT)
    in_hbm = [
        pltpu.with_memory_space_constraint(x, pltpu.HBM)
        for x in (coupling, spectrum.reshape(1, modes), spatial_basis, keys, counters)
    ]

    pairs, single = partners(space)
    routes = [(d, d) for d in single] + pairs
    sizes = [half + TAIL] * len(single) + [nodes_here + TAIL] * len(pairs)
    other = swap(coupling, "tm", 1)
    *messages, coup, spec, base = kernel_call(
        functools.partial(pack_kernel, "tm", "space", routes),
        out_shape=[bf16(n, modes) for n in sizes]
        + [f32(steps, modes), f32(1, modes), jax.ShapeDtypeStruct((vecs, 128), jnp.int32)],
        in_specs=[HBM] * 5,
        out_specs=[VMEM] * (len(sizes) + 3),
        scratch_shapes=[pltpu.VMEM((1, vecs), jnp.int32)] * 2 + [pltpu.SemaphoreType.DMA((len(sizes) + 4,))],
        **fast,
    )(*in_hbm)
    table, *messages = kernel_call(
        functools.partial(table_kernel, "tm", len(sizes)),
        out_shape=[f32(8, modes)] + [bf16(n, modes) for n in sizes],
        in_specs=[VMEM] * 3 + [ANY] * len(sizes),
        out_specs=[VMEM] + [ANY] * len(sizes),
        scratch_shapes=[pltpu.VMEM((TAIL, modes), BF16), pltpu.SemaphoreType.DMA((len(sizes),))],
        input_output_aliases={3 + i: 1 + i for i in range(len(sizes))},
        **fast,
    )(coup, other, spec, *messages)
    tables = [swap(table, "tm", 2 * e) for e in range(1, chips)]
    direct = [exchange(m, lambda t, s, r=r: (t, s ^ r[t % 2])) for m, r in zip(messages, routes)]

    def noise_of(offsets, after):
        count = len(offsets) * steps * vecs * modes
        return kernel_call(
            functools.partial(noise_kernel, "tm", "space", offsets, len(after)),
            out_shape=[f32(steps, vecs, modes)] * len(offsets),
            in_specs=[VMEM] + [ANY] * len(after),
            out_specs=[VMEM] * len(offsets),
            cost_estimate=pl.CostEstimate(flops=count * 60, transcendentals=count * 2, bytes_accessed=count * 4),
            **fast,
        )(base, *after)

    (own,) = noise_of([(0, 0)], (table,))
    state, sent, weights, sums = kernel_call(
        functools.partial(offset_kernel, "tm"),
        out_shape=[f32(vecs, modes), bf16(vecs, modes), f32(chips, 8, modes), f32(8, modes)],
        in_specs=[VMEM] * (4 + len(tables)),
        out_specs=[VMEM] * 4,
        scratch_shapes=[pltpu.VMEM((chips, 8, modes), F32)] + [pltpu.VMEM((steps, modes), F32)] * 2,
        **fast,
    )(own, coup, spec, table, *tables)
    total, late = kernel_call(
        functools.partial(combine_kernel, "tm"),
        out_shape=[bf16(vecs // 2, modes), f32(vecs, modes)],
        in_specs=[VMEM] * 3,
        out_specs=[VMEM] * 2,
        **fast,
    )(state, swap(sent, "tm", 1), sums)
    later = [swap(total, "tm", 2 * e) for e in range(1, chips)]
    noise = list(noise_of([(d, d) for d in single], (total,)))
    mine, sent = kernel_call(
        functools.partial(half_kernel, "tm"),
        out_shape=[f32(vecs // 2, modes), bf16(vecs // 2, modes)],
        in_specs=[VMEM] * (1 + len(later)) + [ANY],
        out_specs=[VMEM] * 2,
        **fast,
    )(weights, *later, noise[-1])
    theirs = swap(sent, "tm", 1)
    carry = kernel_call(
        functools.partial(carry_kernel, "tm"),
        out_shape=bf16(vecs + 16, modes),
        in_specs=[VMEM] * 4,
        out_specs=VMEM,
        **fast,
    )(mine, theirs, late, sums)
    carries = [swap(carry, "space", d) for d in range(1, space)]
    swapped = [swap(m, "tm", 1) for m in direct]
    noise += noise_of(pairs, (carry,))
    noise += noise_of([r[::-1] for r in pairs], (noise[-1],))

    flops = 2 * nodes_here * modes * steps * vecs
    half_cols = steps // 2 * vecs
    result = f32(nodes_here, steps * vecs)
    out = kernel_call(
        functools.partial(own_kernel, "space"),
        out_shape=result,
        in_specs=[VMEM, VMEM, HBM, VMEM, VMEM],
        out_specs=VMEM,
        scratch_shapes=[
            pltpu.VMEM((nodes_here, modes), BF16),
            pltpu.VMEM((2, half_cols, modes), BF16),
            pltpu.VMEM((vecs, modes), F32),
            pltpu.VMEM((2, steps, modes), F32),
            pltpu.SemaphoreType.DMA,
        ],
        cost_estimate=pl.CostEstimate(flops=flops, transcendentals=0, bytes_accessed=4 * steps * vecs * modes),
        **fast,
    )(coup, spec, spatial_basis, own, carry)
    count = space - 1
    return kernel_call(
        functools.partial(final_kernel, "tm", pairs, single),
        out_shape=result,
        in_specs=[VMEM] * (1 + len(direct) + len(swapped) + len(noise) + len(carries)),
        out_specs=HBM,
        scratch_shapes=[
            pltpu.VMEM((len(single), nodes_here, modes), BF16),
            pltpu.VMEM((2, count, half_cols, modes), BF16),
            pltpu.VMEM((count, vecs, modes), F32),
            pltpu.VMEM((count, 2, steps, modes), F32),
            pltpu.VMEM((2, nodes_here, half_cols), F32),
            pltpu.SemaphoreType.DMA((2 * len(single) + 2,)),
        ],
        cost_estimate=pl.CostEstimate(
            flops=flops * count, transcendentals=0, bytes_accessed=4 * steps * vecs * modes * count
        ),
        **fast,
    )(out, *direct, *swapped, *noise, *carries)


def solution(mesh):
    in_specs = (P("space"), P("tm", "space"), P(None, "space"), P(), P())
    out_specs = P("space", "tm")
    return jax.shard_map(local, mesh=mesh, in_specs=in_specs, out_specs=out_specs, check_vma=False)
```

```python
import functools

import jax
import jax.numpy as jnp
from jax import lax
from jax.experimental import pallas as pl
from jax.experimental.pallas import tpu as pltpu
from jax.sharding import PartitionSpec as P


F32 = jnp.float32
BF16 = jnp.bfloat16
VMEM = pl.BlockSpec(memory_space=pltpu.VMEM)
ANY = pl.BlockSpec(memory_space=pl.ANY)
HBM = pl.BlockSpec(memory_space=pltpu.HBM)
LIMIT = pltpu.CompilerParams(vmem_limit_bytes=24 << 20)
SINE = (6.28318516, -41.34165503, 81.60100406, -76.54978208, 39.53670436)


def partners(count):
    pairs = [(i, i + 1) for i in range(1, count - 2, 2)]
    return pairs, ([count - 1] if count > 1 else [])


def exchange(x, move):
    tm, space = lax.axis_size("tm"), lax.axis_size("space")
    moves = []
    for t in range(tm):
        for s in range(space):
            to = move(t, s)
            if to is not None:
                moves.append((t * space + s, to[0] * space + to[1]))
    return lax.ppermute(x, ("tm", "space"), moves)


def swap(x, axis, offset):
    count = lax.axis_size(axis)
    return lax.ppermute(x, axis, [(i, i ^ offset) for i in range(count)])


def split3(x):
    high = x.astype(BF16).astype(F32)
    rest = x - high
    middle = rest.astype(BF16).astype(F32)
    return high, middle, rest - middle


def mix_bits(state):
    state = state ^ lax.shift_right_logical(state, jnp.int32(16))
    state = state * jnp.int32(-2048144789)
    state = state ^ lax.shift_right_logical(state, jnp.int32(13))
    state = state * jnp.int32(-1028477387)
    return state ^ lax.shift_right_logical(state, jnp.int32(16))


def gaussian(seeded):
    first = mix_bits(seeded)
    second = mix_bits(first + jnp.int32(1013904223))
    unit = (lax.shift_right_logical(first, jnp.int32(8)).astype(F32) + 0.5) * (1.0 / 16777216.0)
    square = -2.0 * jnp.log(unit)
    radius = square * lax.rsqrt(jnp.maximum(square, 1e-30))
    turn = (lax.shift_right_arithmetic(second, jnp.int32(8)).astype(F32) + 0.5) * (1.0 / 16777216.0)
    w = 0.25 - jnp.abs(turn)
    z = w * w
    sine = SINE[4]
    for c in SINE[3::-1]:
        sine = sine * z + c
    return radius * (sine * w)


TAIL = 64


def pick(core, offsets):
    return offsets[0] if offsets[0] == offsets[1] else jnp.where(core == 0, offsets[0], offsets[1])


def pack_kernel(tm_axis, sp_axis, offsets, coup, spec, basis, keys, counters, *rest):
    *outs, coup_out, spec_out, base, key_row, counter_row, sems = rest
    me, sp = lax.axis_index(tm_axis), lax.axis_index(sp_axis)
    core = lax.rem(me, 2)
    copies = [
        pltpu.make_async_copy(coup, coup_out, sems.at[len(outs)]),
        pltpu.make_async_copy(spec, spec_out, sems.at[len(outs) + 1]),
    ]
    rows_in = [
        pltpu.make_async_copy(keys, key_row, sems.at[len(outs) + 2]),
        pltpu.make_async_copy(counters, counter_row, sems.at[len(outs) + 3]),
    ]
    for i, (out, offset) in enumerate(zip(outs, offsets)):
        rows = out.shape[0] - TAIL
        block = sp ^ pick(core, offset)
        if offset[0] == offset[1]:
            block = block * 2 + core
        start = pl.multiple_of(block * rows, rows)
        copies.append(
            pltpu.make_async_copy(basis.at[pl.ds(start, rows), :], out.at[pl.ds(0, rows), :], sems.at[i])
        )
    for copy in rows_in + copies:
        copy.start()
    for copy in rows_in:
        copy.wait()
    base_columns(key_row, counter_row, base)
    for copy in copies:
        copy.wait()


def totals(ref):
    product = square = total = None
    for t in range(ref.shape[0]):
        c = ref[pl.ds(t, 1), :]
        product = c if t == 0 else product * c
        square = c * c if t == 0 else square * (c * c)
        total = square if t == 0 else total + square
    return product, total


def joined(early, late):
    return early[0] * late[0], early[1] + (early[0] * early[0]) * late[1]


def table_rows(shape, rows):
    row = lax.broadcasted_iota(jnp.int32, shape, 0)
    table = jnp.zeros(shape, F32)
    for j, value in enumerate(rows):
        table = jnp.where(row == j, value, table)
    return table


def ordered(first, mine, theirs):
    early = tuple(jnp.where(first, x, y) for x, y in zip(mine, theirs))
    late = tuple(jnp.where(first, y, x) for x, y in zip(mine, theirs))
    return early, late


def table_kernel(tm_axis, count, coup, other, spec, *rest):
    out, *messages, tail, sems = rest[count:]
    first = lax.rem(lax.axis_index(tm_axis), 2) == 0
    (x,), (y,) = ordered(first, (coup[...],), (other[...],))
    parts = split3(x) + split3(y)
    parts = parts + (table_rows(x.shape, split3(spec[...])), jnp.zeros_like(x))
    for j in range(4):
        tail[pl.ds(16 * j, 16), :] = jnp.concatenate(parts[2 * j : 2 * j + 2], 0).astype(BF16)
    copies = []
    for i, message in enumerate(messages):
        rows = message.shape[0] - TAIL
        copies.append(pltpu.make_async_copy(tail, message.at[pl.ds(rows, TAIL), :], sems.at[i]))
        copies[-1].start()
    early, late = ordered(first, totals(coup), totals(other))
    out[...] = table_rows(out.shape, (*joined(early, late), *early, *late))
    for copy in copies:
        copy.wait()


def base_columns(keys, counters, base):
    vecs = base.shape[0]
    diagonal = lax.broadcasted_iota(jnp.int32, (vecs, vecs), 0) == lax.broadcasted_iota(
        jnp.int32, (vecs, vecs), 1
    )

    def column(ref):
        row = jnp.broadcast_to(ref[...].astype(F32), (vecs, vecs))
        return jnp.sum(jnp.where(diagonal, row, 0.0), axis=1, keepdims=True).astype(jnp.int32)

    start = column(keys) * jnp.int32(668265261) + column(counters) * jnp.int32(374761393)
    base[...] = jnp.broadcast_to(start, base.shape)


def noise_kernel(tm_axis, sp_axis, parts, total_steps, extras, base, *rest):
    outs = rest[extras:]
    me, sp = lax.axis_index(tm_axis), lax.axis_index(sp_axis)
    group = 8
    for out, (offset, begin) in zip(outs, parts):
        steps, vecs, modes = out.shape
        ids = (sp ^ pick(lax.rem(me, 2), offset)) * modes + lax.broadcasted_iota(jnp.int32, (1, modes), 1)
        lane = ids * jnp.int32(-1640531535)
        first_step = me * total_steps + begin

        def step(t, _):
            shifted = lane + (first_step + t) * jnp.int32(374761393)
            for v in range(vecs // group):
                seeded = jnp.tile(base[pl.ds(v * group, group), :], (1, modes // 128)) + shifted
                out[t, pl.ds(v * group, group), :] = gaussian(seeded)
            return 0

        lax.fori_loop(0, steps, step, 0)


def running(x, combine, identity):
    row = lax.broadcasted_iota(jnp.int32, x.shape, 0)
    shift = 1
    while shift < x.shape[0]:
        x = combine(x, jnp.where(row < shift, identity, pltpu.roll(x, shift, 0)))
        shift *= 2
    return x


def chain(c, spec, d_start, f_start):
    total = running(running(c * c, jnp.multiply, 1.0), jnp.add, 0.0)
    behind = d_start + f_start * total
    row = lax.broadcasted_iota(jnp.int32, c.shape, 0)
    ratio = jnp.where(row == 0, d_start, pltpu.roll(behind, 1, 0)) / behind
    return jnp.sqrt(ratio / spec), ratio


def after(start, total):
    return start[0] + start[1] * total[1], start[1] * (total[0] * total[0])


def select(flag, x, y):
    return tuple(jnp.where(flag, p, q) for p, q in zip(x, y))


def gain_of(start, total):
    return total[0] * start[0] / (start[0] + start[1] * total[1])


def offset_kernel(tm_axis, noise, coup, spec, table, *rest):
    received, rest = rest[:-7], rest[-7:]
    o_ref, sent, wts, df, tables, alpha, beta = rest
    steps, vecs, modes = noise.shape
    me = lax.axis_index(tm_axis)
    chip = me // 2
    first = lax.rem(me, 2) == 0
    one = jnp.ones((1, modes), F32)
    tables[chip] = table[...]
    for e, ref in enumerate(received):
        tables[chip ^ (e + 1)] = ref[...]
    now, start, weight = (one, one), (one, one), jnp.zeros((1, modes), F32)
    for b in range(tables.shape[0]):
        wts[b] = jnp.broadcast_to(weight, (8, modes))
        total = tables[b, pl.ds(0, 1), :], tables[b, pl.ds(1, 1), :]
        here = chip == b
        start = select(here, now, start)
        weight = jnp.where(here, 1.0, weight * gain_of(now, total))
        now = after(now, total)
    early = table[pl.ds(2, 1), :], table[pl.ds(3, 1), :]
    late = table[pl.ds(4, 1), :], table[pl.ds(5, 1), :]
    second = after(start, early)
    gain_early, gain_late = gain_of(start, early), gain_of(second, late)
    own = select(first, start, second)
    df[...] = table_rows((8, modes), (*own, gain_early, gain_late))
    c = coup[...]
    a, ratio = chain(c, spec[...], *own)
    alpha[...] = c * a
    beta[...] = c * ratio

    def tile(v, _):
        at = pl.ds(pl.multiple_of(v * 16, 16), 16)
        carry = jnp.zeros((16, modes), F32)
        for t in range(steps - 1, -1, -1):
            carry = alpha[pl.ds(t, 1), :] * noise[t, at, :] + beta[pl.ds(t, 1), :] * carry
        o_ref[at, :] = carry
        sent[at, :] = carry.astype(BF16)
        return 0

    lax.fori_loop(0, vecs // 16, tile, 0)


def combine_kernel(tm_axis, own, other, df, _, out, late):
    core = lax.rem(lax.axis_index(tm_axis), 2)
    first = core == 0
    half = out.shape[0]
    late[...] = jnp.where(first, other[...].astype(F32), own[...])
    at = pl.ds(pl.multiple_of(core * half, half), half)
    x, y = own[at, :], other[at, :].astype(F32)
    out[...] = (jnp.where(first, x, y) + df[pl.ds(2, 1), :] * jnp.where(first, y, x)).astype(BF16)


def half_kernel(tm_axis, wts, *rest):
    *received, _, out, sent = rest
    chip = lax.axis_index(tm_axis) // 2
    carry = jnp.zeros(out.shape, F32)
    for e, ref in enumerate(received):
        carry = carry + wts[chip ^ (e + 1)][0:1, :] * ref[...].astype(F32)
    out[...] = carry
    sent[...] = carry.astype(BF16)


def carry_kernel(tm_axis, mine, theirs, late, df, _, out):
    half, modes = mine.shape
    core = lax.rem(lax.axis_index(tm_axis), 2)
    gain = df[pl.ds(3, 1), :]
    for j in range(2):
        at = pl.ds(j * half, half)
        carry = jnp.where(core == j, mine[...], theirs[...].astype(F32))
        out[at, :] = jnp.where(core == 0, late[at, :] + gain * carry, carry).astype(BF16)
    parts = split3(df[pl.ds(0, 1), :]) + split3(df[pl.ds(1, 1), :])
    out[pl.ds(2 * half, 16), :] = table_rows((16, modes), parts).astype(BF16)


def sums_of(block):
    return block[0:1] + block[1:2] + block[2:3], block[3:4] + block[4:5] + block[5:6]


def set_coefs(coefs, c, lam, sums):
    a, ratio = chain(c, lam, *sums)
    row = lax.broadcasted_iota(jnp.int32, c.shape, 0)
    steps = c.shape[0]
    coefs[0] = a
    coefs[1] = ratio * jnp.where(row == steps - 1, 1.0, pltpu.roll(c, steps - 1, 0))


def values(noise, start, coefs, state, rhs, times):
    span, vecs, _ = noise[0].shape
    for v in range(0, vecs, 16):
        at = pl.ds(v, 16)
        value = start(at)
        for n, t in enumerate(times):
            row = pl.ds(t, 1)
            value = coefs[0, row, :] * noise[t // span][t % span, at, :] + coefs[1, row, :] * value
            rhs[pl.ds((len(times) - 1 - n) * vecs + v, 16), :] = value.astype(BF16)
        if times[-1]:
            state[at, :] = value


def product(lhs, rhs):
    return lax.dot_general(lhs, rhs, (((1,), (1,)), ((), ())), preferred_element_type=F32)


def halves_of(steps):
    times = list(range(steps - 1, -1, -1))
    return times[: steps // 2], times[steps // 2 :]


def own_kernel(sp_axis, coup, spec, basis, noise, message, out, lhs, rhs, state, coefs, sem):
    rows = lhs.shape[0]
    steps, vecs, _ = noise.shape
    start = pl.multiple_of(lax.axis_index(sp_axis) * rows, rows)
    copy = pltpu.make_async_copy(basis.at[pl.ds(start, rows), :], lhs, sem)
    copy.start()
    set_coefs(coefs, coup[...], spec[...], sums_of(message[pl.ds(vecs, 16), :].astype(F32)))
    late, early = halves_of(steps)
    width = vecs * len(late)
    values((noise,), lambda at: message[at, :].astype(F32), coefs, state, rhs.at[0], late)
    copy.wait()
    values((noise,), lambda at: state[at, :], coefs, state, rhs.at[1], early)
    out[:, pl.ds(width, width)] = product(lhs[...], rhs[0])
    out[:, pl.ds(0, width)] = product(lhs[...], rhs[1])


def final_kernel(tm_axis, pairs, single, partial, *rest):
    fetched = len(pairs) + len(single)
    count = 2 * len(pairs) + len(single)
    direct, rest = rest[:fetched], rest[fetched:]
    swapped, rest = rest[:fetched], rest[fetched:]
    noise, rest = [rest[2 * n : 2 * n + 2] for n in range(count)], rest[2 * count :]
    messages, rest = rest[:count], rest[count:]
    out, lhs, rhs, state, coefs, result, sems = rest
    steps, vecs = 2 * noise[0][0].shape[0], noise[0][0].shape[1]
    core = lax.rem(lax.axis_index(tm_axis), 2)
    first = core == 0
    copies = []
    for i in range(len(single)):
        rows = lhs.shape[1] // 2
        for j, source in enumerate((direct[i], swapped[i])):
            at = pl.multiple_of((core if j == 0 else 1 - core) * rows, rows)
            copies.append(
                pltpu.make_async_copy(
                    source.at[pl.ds(0, rows), :], lhs.at[i, pl.ds(at, rows), :], sems.at[2 * i + j]
                )
            )
            copies[-1].start()

    def chosen(x, y):
        return lambda at: jnp.where(first, messages[x][at, :].astype(F32), messages[y][at, :].astype(F32))

    items = []
    for j, (x, y) in enumerate(pairs):
        i = len(single) + j
        rows = direct[i].shape[0] - TAIL
        near = lambda i=i, rows=rows: direct[i][pl.ds(0, rows), :]
        far = lambda i=i, rows=rows: swapped[i][pl.ds(0, rows), :]
        items.append((near, direct[i], noise[len(single) + j], chosen(x - 1, y - 1)))
        items.append((far, swapped[i], noise[len(single) + len(pairs) + j], chosen(y - 1, x - 1)))
    for i, d in enumerate(single):
        items.append((lambda i=i: lhs[i], direct[i], noise[i], chosen(d - 1, d - 1)))
    for n, (_, source, _, message) in enumerate(items):
        rows = source.shape[0] - TAIL
        x = [source[pl.ds(rows + 16 * j, 16), :].astype(F32) for j in range(4)]
        before = x[0][0:8] + x[0][8:16] + x[1][0:8]
        behind = x[1][8:16] + x[2][0:8] + x[2][8:16]
        lam = x[3][0:1] + x[3][1:2] + x[3][2:3]
        set_coefs(coefs.at[n], jnp.where(first, before, behind), lam, sums_of(message(pl.ds(vecs, 16))))
    late, early = halves_of(steps)
    width = vecs * len(late)
    work = [(h, n) for h in range(2) for n in range(count)]

    def fill(h, n):
        start = items[n][3] if h == 0 else lambda at: state[n, at, :]
        values(items[n][2], start, coefs.at[n], state.at[n], rhs.at[h, n], late if h == 0 else early)

    fill(*work[0])
    outs = []
    for k, (h, n) in enumerate(work):
        if k + 1 < len(work):
            fill(*work[k + 1])
        if h == 0 and n == count - len(single):
            for copy in copies:
                copy.wait()
        term = product(items[n][0](), rhs[h, n])
        at = pl.ds((1 - h) * width, width)
        result[h] = (partial[:, at] if n == 0 else result[h]) + term
        if n == count - 1:
            outs.append(pltpu.make_async_copy(result.at[h], out.at[:, at], sems.at[2 * len(single) + h]))
            outs[-1].start()
    for copy in outs:
        copy.wait()


def kernel_call(body, **options):
    return pl.pallas_call(body, **options)


def local(spectrum, coupling, spatial_basis, noise_keys, noise_counters):
    steps, modes = coupling.shape
    vecs = noise_keys.shape[0]
    tm, space = lax.axis_size("tm"), lax.axis_size("space")
    chips = tm // 2
    nodes_here = spatial_basis.shape[0] // space
    half = nodes_here // 2
    keys, counters = noise_keys.reshape(1, vecs), noise_counters.reshape(1, vecs)
    f32 = lambda *shape: jax.ShapeDtypeStruct(shape, F32)
    bf16 = lambda *shape: jax.ShapeDtypeStruct(shape, BF16)
    fast = dict(compiler_params=LIMIT)
    in_hbm = [
        pltpu.with_memory_space_constraint(x, pltpu.HBM)
        for x in (coupling, spectrum.reshape(1, modes), spatial_basis, keys, counters)
    ]

    pairs, single = partners(space)
    routes = [(d, d) for d in single] + pairs
    sizes = [half + TAIL] * len(single) + [nodes_here + TAIL] * len(pairs)
    other = swap(coupling, "tm", 1)
    *messages, coup, spec, base = kernel_call(
        functools.partial(pack_kernel, "tm", "space", routes),
        out_shape=[bf16(n, modes) for n in sizes]
        + [f32(steps, modes), f32(1, modes), jax.ShapeDtypeStruct((vecs, 128), jnp.int32)],
        in_specs=[HBM] * 5,
        out_specs=[VMEM] * (len(sizes) + 3),
        scratch_shapes=[pltpu.VMEM((1, vecs), jnp.int32)] * 2 + [pltpu.SemaphoreType.DMA((len(sizes) + 4,))],
        **fast,
    )(*in_hbm)
    table, *messages = kernel_call(
        functools.partial(table_kernel, "tm", len(sizes)),
        out_shape=[f32(8, modes)] + [bf16(n, modes) for n in sizes],
        in_specs=[VMEM] * 3 + [ANY] * len(sizes),
        out_specs=[VMEM] + [ANY] * len(sizes),
        scratch_shapes=[pltpu.VMEM((TAIL, modes), BF16), pltpu.SemaphoreType.DMA((len(sizes),))],
        input_output_aliases={3 + i: 1 + i for i in range(len(sizes))},
        **fast,
    )(coup, other, spec, *messages)
    tables = [swap(table, "tm", 2 * e) for e in range(1, chips)]
    direct = [exchange(m, lambda t, s, r=r: (t, s ^ r[t % 2])) for m, r in zip(messages, routes)]

    def noise_of(parts, span, after):
        count = len(parts) * span * vecs * modes
        return kernel_call(
            functools.partial(noise_kernel, "tm", "space", parts, steps, len(after)),
            out_shape=[f32(span, vecs, modes)] * len(parts),
            in_specs=[VMEM] + [ANY] * len(after),
            out_specs=[VMEM] * len(parts),
            cost_estimate=pl.CostEstimate(flops=count * 60, transcendentals=count * 2, bytes_accessed=count * 4),
            **fast,
        )(base, *after)

    span = steps // 2
    alone = [(d, d) for d in single]
    half_of = lambda routes, part, after: noise_of([(r, part * span) for r in routes], span, after)
    (own,) = noise_of([((0, 0), 0)], steps, (table,))
    state, sent, weights, sums = kernel_call(
        functools.partial(offset_kernel, "tm"),
        out_shape=[f32(vecs, modes), bf16(vecs, modes), f32(chips, 8, modes), f32(8, modes)],
        in_specs=[VMEM] * (4 + len(tables)),
        out_specs=[VMEM] * 4,
        scratch_shapes=[pltpu.VMEM((chips, 8, modes), F32)] + [pltpu.VMEM((steps, modes), F32)] * 2,
        **fast,
    )(own, coup, spec, table, *tables)
    alone_0 = half_of(alone, 0, (sent,))
    total, late = kernel_call(
        functools.partial(combine_kernel, "tm"),
        out_shape=[bf16(vecs // 2, modes), f32(vecs, modes)],
        in_specs=[VMEM] * 3 + [ANY],
        out_specs=[VMEM] * 2,
        **fast,
    )(state, swap(sent, "tm", 1), sums, alone_0[0])
    later = [swap(total, "tm", 2 * e) for e in range(1, chips)]
    alone_1 = half_of(alone, 1, (total,))
    mine, sent = kernel_call(
        functools.partial(half_kernel, "tm"),
        out_shape=[f32(vecs // 2, modes), bf16(vecs // 2, modes)],
        in_specs=[VMEM] * (1 + len(later)) + [ANY],
        out_specs=[VMEM] * 2,
        **fast,
    )(weights, *later, alone_1[0])
    theirs = swap(sent, "tm", 1)
    near_0 = half_of(pairs, 0, (sent,)) if pairs else [sent]
    carry = kernel_call(
        functools.partial(carry_kernel, "tm"),
        out_shape=bf16(vecs + 16, modes),
        in_specs=[VMEM] * 4 + [ANY],
        out_specs=VMEM,
        **fast,
    )(mine, theirs, late, sums, near_0[0])
    carries = [swap(carry, "space", d) for d in range(1, space)]
    swapped = [swap(m, "tm", 1) for m in direct]
    noise = [x for both in zip(alone_0, alone_1) for x in both]
    if pairs:
        near_1 = half_of(pairs, 1, (carry,))
        far = noise_of([(r[::-1], n * span) for r in pairs for n in range(2)], span, (near_1[-1],))
        noise += [x for both in zip(near_0, near_1) for x in both] + list(far)

    flops = 2 * nodes_here * modes * steps * vecs
    half_cols = steps // 2 * vecs
    result = f32(nodes_here, steps * vecs)
    out = kernel_call(
        functools.partial(own_kernel, "space"),
        out_shape=result,
        in_specs=[VMEM, VMEM, HBM, VMEM, VMEM],
        out_specs=VMEM,
        scratch_shapes=[
            pltpu.VMEM((nodes_here, modes), BF16),
            pltpu.VMEM((2, half_cols, modes), BF16),
            pltpu.VMEM((vecs, modes), F32),
            pltpu.VMEM((2, steps, modes), F32),
            pltpu.SemaphoreType.DMA,
        ],
        cost_estimate=pl.CostEstimate(flops=flops, transcendentals=0, bytes_accessed=4 * steps * vecs * modes),
        **fast,
    )(coup, spec, spatial_basis, own, carry)
    count = space - 1
    return kernel_call(
        functools.partial(final_kernel, "tm", pairs, single),
        out_shape=result,
        in_specs=[VMEM] * (1 + len(direct) + len(swapped) + len(noise) + len(carries)),
        out_specs=HBM,
        scratch_shapes=[
            pltpu.VMEM((len(single), nodes_here, modes), BF16),
            pltpu.VMEM((2, count, half_cols, modes), BF16),
            pltpu.VMEM((count, vecs, modes), F32),
            pltpu.VMEM((count, 2, steps, modes), F32),
            pltpu.VMEM((2, nodes_here, half_cols), F32),
            pltpu.SemaphoreType.DMA((2 * len(single) + 2,)),
        ],
        cost_estimate=pl.CostEstimate(
            flops=flops * count, transcendentals=0, bytes_accessed=4 * steps * vecs * modes * count
        ),
        **fast,
    )(out, *direct, *swapped, *noise, *carries)


def solution(mesh):
    in_specs = (P("space"), P("tm", "space"), P(None, "space"), P(), P())
    out_specs = P("space", "tm")
    return jax.shard_map(local, mesh=mesh, in_specs=in_specs, out_specs=out_specs, check_vma=False)
```

```python
import functools

import jax
import jax.numpy as jnp
from jax import lax
from jax.experimental import pallas as pl
from jax.experimental.pallas import tpu as pltpu
from jax.sharding import PartitionSpec as P


F32 = jnp.float32
BF16 = jnp.bfloat16
VMEM = pl.BlockSpec(memory_space=pltpu.VMEM)
ANY = pl.BlockSpec(memory_space=pl.ANY)
HBM = pl.BlockSpec(memory_space=pltpu.HBM)
LIMIT = pltpu.CompilerParams(vmem_limit_bytes=24 << 20)
SINE = (6.28318516, -41.34165503, 81.60100406, -76.54978208, 39.53670436)


def partners(count):
    pairs = [(i, i + 1) for i in range(1, count - 2, 2)]
    return pairs, ([count - 1] if count > 1 else [])


def exchange(x, move):
    tm, space = lax.axis_size("tm"), lax.axis_size("space")
    moves = []
    for t in range(tm):
        for s in range(space):
            to = move(t, s)
            if to is not None:
                moves.append((t * space + s, to[0] * space + to[1]))
    return lax.ppermute(x, ("tm", "space"), moves)


def swap(x, axis, offset):
    count = lax.axis_size(axis)
    return lax.ppermute(x, axis, [(i, i ^ offset) for i in range(count)])


def split3(x):
    high = x.astype(BF16).astype(F32)
    rest = x - high
    middle = rest.astype(BF16).astype(F32)
    return high, middle, rest - middle


def mix_bits(state):
    state = state ^ lax.shift_right_logical(state, jnp.int32(16))
    state = state * jnp.int32(-2048144789)
    state = state ^ lax.shift_right_logical(state, jnp.int32(13))
    state = state * jnp.int32(-1028477387)
    return state ^ lax.shift_right_logical(state, jnp.int32(16))


def gaussian(seeded):
    first = mix_bits(seeded)
    second = mix_bits(first + jnp.int32(1013904223))
    unit = (lax.shift_right_logical(first, jnp.int32(8)).astype(F32) + 0.5) * (1.0 / 16777216.0)
    square = -2.0 * jnp.log(unit)
    radius = square * lax.rsqrt(jnp.maximum(square, 1e-30))
    turn = (lax.shift_right_arithmetic(second, jnp.int32(8)).astype(F32) + 0.5) * (1.0 / 16777216.0)
    w = 0.25 - jnp.abs(turn)
    z = w * w
    sine = SINE[4]
    for c in SINE[3::-1]:
        sine = sine * z + c
    return radius * (sine * w)


TAIL = 64


def pick(core, offsets):
    return offsets[0] if offsets[0] == offsets[1] else jnp.where(core == 0, offsets[0], offsets[1])


def pack_kernel(tm_axis, sp_axis, offsets, coup, spec, basis, keys, counters, *rest):
    *outs, coup_out, spec_out, base, key_row, counter_row, sems = rest
    me, sp = lax.axis_index(tm_axis), lax.axis_index(sp_axis)
    core = lax.rem(me, 2)
    copies = [
        pltpu.make_async_copy(coup, coup_out, sems.at[len(outs)]),
        pltpu.make_async_copy(spec, spec_out, sems.at[len(outs) + 1]),
    ]
    rows_in = [
        pltpu.make_async_copy(keys, key_row, sems.at[len(outs) + 2]),
        pltpu.make_async_copy(counters, counter_row, sems.at[len(outs) + 3]),
    ]
    for i, (out, offset) in enumerate(zip(outs, offsets)):
        rows = out.shape[0] - TAIL
        block = sp ^ pick(core, offset)
        if offset[0] == offset[1]:
            block = block * 2 + core
        start = pl.multiple_of(block * rows, rows)
        copies.append(
            pltpu.make_async_copy(basis.at[pl.ds(start, rows), :], out.at[pl.ds(0, rows), :], sems.at[i])
        )
    for copy in rows_in + copies:
        copy.start()
    for copy in rows_in:
        copy.wait()
    base_columns(key_row, counter_row, base)
    for copy in copies:
        copy.wait()


def totals(ref):
    product = square = total = None
    for t in range(ref.shape[0]):
        c = ref[pl.ds(t, 1), :]
        product = c if t == 0 else product * c
        square = c * c if t == 0 else square * (c * c)
        total = square if t == 0 else total + square
    return product, total


def joined(early, late):
    return early[0] * late[0], early[1] + (early[0] * early[0]) * late[1]


def table_rows(shape, rows):
    row = lax.broadcasted_iota(jnp.int32, shape, 0)
    table = jnp.zeros(shape, F32)
    for j, value in enumerate(rows):
        table = jnp.where(row == j, value, table)
    return table


def ordered(first, mine, theirs):
    early = tuple(jnp.where(first, x, y) for x, y in zip(mine, theirs))
    late = tuple(jnp.where(first, y, x) for x, y in zip(mine, theirs))
    return early, late


def table_kernel(tm_axis, count, coup, other, spec, *rest):
    out, *messages, tail, sems = rest[count:]
    first = lax.rem(lax.axis_index(tm_axis), 2) == 0
    (x,), (y,) = ordered(first, (coup[...],), (other[...],))
    parts = split3(x) + split3(y)
    parts = parts + (table_rows(x.shape, split3(spec[...])), jnp.zeros_like(x))
    for j in range(4):
        tail[pl.ds(16 * j, 16), :] = jnp.concatenate(parts[2 * j : 2 * j + 2], 0).astype(BF16)
    copies = []
    for i, message in enumerate(messages):
        rows = message.shape[0] - TAIL
        copies.append(pltpu.make_async_copy(tail, message.at[pl.ds(rows, TAIL), :], sems.at[i]))
        copies[-1].start()
    early, late = ordered(first, totals(coup), totals(other))
    out[...] = table_rows(out.shape, (*joined(early, late), *early, *late))
    for copy in copies:
        copy.wait()


def base_columns(keys, counters, base):
    vecs = base.shape[0]
    diagonal = lax.broadcasted_iota(jnp.int32, (vecs, vecs), 0) == lax.broadcasted_iota(
        jnp.int32, (vecs, vecs), 1
    )

    def column(ref):
        row = jnp.broadcast_to(ref[...].astype(F32), (vecs, vecs))
        return jnp.sum(jnp.where(diagonal, row, 0.0), axis=1, keepdims=True).astype(jnp.int32)

    start = column(keys) * jnp.int32(668265261) + column(counters) * jnp.int32(374761393)
    base[...] = jnp.broadcast_to(start, base.shape)


def noise_kernel(tm_axis, sp_axis, parts, total_steps, extras, base, *rest):
    outs = rest[extras:]
    me, sp = lax.axis_index(tm_axis), lax.axis_index(sp_axis)
    group = 8
    for out, (offset, begin) in zip(outs, parts):
        steps, vecs, modes = out.shape
        ids = (sp ^ pick(lax.rem(me, 2), offset)) * modes + lax.broadcasted_iota(jnp.int32, (1, modes), 1)
        lane = ids * jnp.int32(-1640531535)
        first_step = me * total_steps + begin

        def step(t, _):
            shifted = lane + (first_step + t) * jnp.int32(374761393)
            for v in range(vecs // group):
                seeded = jnp.tile(base[pl.ds(v * group, group), :], (1, modes // 128)) + shifted
                out[t, pl.ds(v * group, group), :] = gaussian(seeded)
            return 0

        lax.fori_loop(0, steps, step, 0)


def running(x, combine, identity):
    row = lax.broadcasted_iota(jnp.int32, x.shape, 0)
    shift = 1
    while shift < x.shape[0]:
        x = combine(x, jnp.where(row < shift, identity, pltpu.roll(x, shift, 0)))
        shift *= 2
    return x


def chain(c, spec, d_start, f_start):
    total = running(running(c * c, jnp.multiply, 1.0), jnp.add, 0.0)
    behind = d_start + f_start * total
    row = lax.broadcasted_iota(jnp.int32, c.shape, 0)
    ratio = jnp.where(row == 0, d_start, pltpu.roll(behind, 1, 0)) / behind
    return jnp.sqrt(ratio / spec), ratio


def after(start, total):
    return start[0] + start[1] * total[1], start[1] * (total[0] * total[0])


def select(flag, x, y):
    return tuple(jnp.where(flag, p, q) for p, q in zip(x, y))


def gain_of(start, total):
    return total[0] * start[0] / (start[0] + start[1] * total[1])


def offset_kernel(tm_axis, noise, coup, spec, table, *rest):
    received, rest = rest[:-7], rest[-7:]
    o_ref, sent, wts, df, tables, alpha, beta = rest
    steps, vecs, modes = noise.shape
    me = lax.axis_index(tm_axis)
    chip = me // 2
    first = lax.rem(me, 2) == 0
    one = jnp.ones((1, modes), F32)
    tables[chip] = table[...]
    for e, ref in enumerate(received):
        tables[chip ^ (e + 1)] = ref[...]
    now, start, weight = (one, one), (one, one), jnp.zeros((1, modes), F32)
    for b in range(tables.shape[0]):
        wts[b] = jnp.broadcast_to(weight, (8, modes))
        total = tables[b, pl.ds(0, 1), :], tables[b, pl.ds(1, 1), :]
        here = chip == b
        start = select(here, now, start)
        weight = jnp.where(here, 1.0, weight * gain_of(now, total))
        now = after(now, total)
    early = table[pl.ds(2, 1), :], table[pl.ds(3, 1), :]
    late = table[pl.ds(4, 1), :], table[pl.ds(5, 1), :]
    second = after(start, early)
    gain_early, gain_late = gain_of(start, early), gain_of(second, late)
    own = select(first, start, second)
    df[...] = table_rows((8, modes), (*own, gain_early, gain_late))
    c = coup[...]
    a, ratio = chain(c, spec[...], *own)
    alpha[...] = c * a
    beta[...] = c * ratio

    def tile(v, _):
        at = pl.ds(pl.multiple_of(v * 16, 16), 16)
        carry = jnp.zeros((16, modes), F32)
        for t in range(steps - 1, -1, -1):
            carry = alpha[pl.ds(t, 1), :] * noise[t, at, :] + beta[pl.ds(t, 1), :] * carry
        o_ref[at, :] = carry
        sent[at, :] = carry.astype(BF16)
        return 0

    lax.fori_loop(0, vecs // 16, tile, 0)


def combine_kernel(tm_axis, own, other, df, out, late):
    core = lax.rem(lax.axis_index(tm_axis), 2)
    first = core == 0
    half = out.shape[0]
    late[...] = jnp.where(first, other[...].astype(F32), own[...])
    at = pl.ds(pl.multiple_of(core * half, half), half)
    x, y = own[at, :], other[at, :].astype(F32)
    out[...] = (jnp.where(first, x, y) + df[pl.ds(2, 1), :] * jnp.where(first, y, x)).astype(BF16)


def half_kernel(tm_axis, wts, *rest):
    *received, _, out, sent = rest
    chip = lax.axis_index(tm_axis) // 2
    carry = jnp.zeros(out.shape, F32)
    for e, ref in enumerate(received):
        carry = carry + wts[chip ^ (e + 1)][0:1, :] * ref[...].astype(F32)
    out[...] = carry
    sent[...] = carry.astype(BF16)


def carry_kernel(tm_axis, mine, theirs, late, df, _, out):
    half, modes = mine.shape
    core = lax.rem(lax.axis_index(tm_axis), 2)
    gain = df[pl.ds(3, 1), :]
    for j in range(2):
        at = pl.ds(j * half, half)
        carry = jnp.where(core == j, mine[...], theirs[...].astype(F32))
        out[at, :] = jnp.where(core == 0, late[at, :] + gain * carry, carry).astype(BF16)
    parts = split3(df[pl.ds(0, 1), :]) + split3(df[pl.ds(1, 1), :])
    out[pl.ds(2 * half, 8), :] = table_rows((8, modes), parts).astype(BF16)


def sums_of(block):
    return block[0:1] + block[1:2] + block[2:3], block[3:4] + block[4:5] + block[5:6]


def set_coefs(coefs, c, lam, sums):
    a, ratio = chain(c, lam, *sums)
    row = lax.broadcasted_iota(jnp.int32, c.shape, 0)
    steps = c.shape[0]
    coefs[0] = a
    coefs[1] = ratio * jnp.where(row == steps - 1, 1.0, pltpu.roll(c, steps - 1, 0))


def values(noise, start, coefs, state, rhs, times):
    span, vecs, _ = noise[0].shape
    for v in range(0, vecs, 16):
        at = pl.ds(v, 16)
        value = start(at)
        for n, t in enumerate(times):
            row = pl.ds(t, 1)
            value = coefs[0, row, :] * noise[t // span][t % span, at, :] + coefs[1, row, :] * value
            rhs[pl.ds((len(times) - 1 - n) * vecs + v, 16), :] = value.astype(BF16)
        if times[-1]:
            state[at, :] = value


def product(lhs, rhs):
    return lax.dot_general(lhs, rhs, (((1,), (1,)), ((), ())), preferred_element_type=F32)


def halves_of(steps):
    times = list(range(steps - 1, -1, -1))
    return times[: steps // 2], times[steps // 2 :]


def own_kernel(sp_axis, coup, spec, basis, noise, message, out, lhs, rhs, state, coefs, sem):
    rows = lhs.shape[0]
    steps, vecs, _ = noise.shape
    start = pl.multiple_of(lax.axis_index(sp_axis) * rows, rows)
    copy = pltpu.make_async_copy(basis.at[pl.ds(start, rows), :], lhs, sem)
    copy.start()
    set_coefs(coefs, coup[...], spec[...], sums_of(message[pl.ds(vecs, 8), :].astype(F32)))
    late, early = halves_of(steps)
    width = vecs * len(late)
    values((noise,), lambda at: message[at, :].astype(F32), coefs, state, rhs.at[0], late)
    copy.wait()
    values((noise,), lambda at: state[at, :], coefs, state, rhs.at[1], early)
    out[:, pl.ds(width, width)] = product(lhs[...], rhs[0])
    out[:, pl.ds(0, width)] = product(lhs[...], rhs[1])


def final_kernel(tm_axis, pairs, single, partial, *rest):
    fetched = len(pairs) + len(single)
    count = 2 * len(pairs) + len(single)
    direct, rest = rest[:fetched], rest[fetched:]
    swapped, rest = rest[:fetched], rest[fetched:]
    noise, rest = [rest[2 * n : 2 * n + 2] for n in range(count)], rest[2 * count :]
    messages, rest = rest[:count], rest[count:]
    out, lhs, rhs, state, coefs, result, sems = rest
    steps, vecs = 2 * noise[0][0].shape[0], noise[0][0].shape[1]
    core = lax.rem(lax.axis_index(tm_axis), 2)
    first = core == 0
    copies = []
    for i in range(len(single)):
        rows = lhs.shape[1] // 2
        for j, source in enumerate((direct[i], swapped[i])):
            at = pl.multiple_of((core if j == 0 else 1 - core) * rows, rows)
            copies.append(
                pltpu.make_async_copy(
                    source.at[pl.ds(0, rows), :], lhs.at[i, pl.ds(at, rows), :], sems.at[2 * i + j]
                )
            )
            copies[-1].start()

    def chosen(x, y):
        return lambda at: jnp.where(first, messages[x][at, :].astype(F32), messages[y][at, :].astype(F32))

    items = []
    for j, (x, y) in enumerate(pairs):
        i = len(single) + j
        rows = direct[i].shape[0] - TAIL
        near = lambda i=i, rows=rows: direct[i][pl.ds(0, rows), :]
        far = lambda i=i, rows=rows: swapped[i][pl.ds(0, rows), :]
        items.append((near, direct[i], noise[len(single) + j], chosen(x - 1, y - 1)))
        items.append((far, swapped[i], noise[len(single) + len(pairs) + j], chosen(y - 1, x - 1)))
    for i, d in enumerate(single):
        items.append((lambda i=i: lhs[i], direct[i], noise[i], chosen(d - 1, d - 1)))
    for n, (_, source, _, message) in enumerate(items):
        rows = source.shape[0] - TAIL
        x = [source[pl.ds(rows + 16 * j, 16), :].astype(F32) for j in range(4)]
        before = x[0][0:8] + x[0][8:16] + x[1][0:8]
        behind = x[1][8:16] + x[2][0:8] + x[2][8:16]
        lam = x[3][0:1] + x[3][1:2] + x[3][2:3]
        set_coefs(coefs.at[n], jnp.where(first, before, behind), lam, sums_of(message(pl.ds(vecs, 8))))
    late, early = halves_of(steps)
    width = vecs * len(late)
    work = [(h, n) for h in range(2) for n in range(count)]

    def fill(h, n):
        start = items[n][3] if h == 0 else lambda at: state[n, at, :]
        values(items[n][2], start, coefs.at[n], state.at[n], rhs.at[h, n], late if h == 0 else early)

    fill(*work[0])
    outs = []
    for k, (h, n) in enumerate(work):
        if k + 1 < len(work):
            fill(*work[k + 1])
        if h == 0 and n == count - len(single):
            for copy in copies:
                copy.wait()
        term = product(items[n][0](), rhs[h, n])
        at = pl.ds((1 - h) * width, width)
        result[h] = (partial[:, at] if n == 0 else result[h]) + term
        if n == count - 1:
            outs.append(pltpu.make_async_copy(result.at[h], out.at[:, at], sems.at[2 * len(single) + h]))
            outs[-1].start()
    for copy in outs:
        copy.wait()


def kernel_call(body, **options):
    return pl.pallas_call(body, **options)


def local(spectrum, coupling, spatial_basis, noise_keys, noise_counters):
    steps, modes = coupling.shape
    vecs = noise_keys.shape[0]
    tm, space = lax.axis_size("tm"), lax.axis_size("space")
    chips = tm // 2
    nodes_here = spatial_basis.shape[0] // space
    half = nodes_here // 2
    keys, counters = noise_keys.reshape(1, vecs), noise_counters.reshape(1, vecs)
    f32 = lambda *shape: jax.ShapeDtypeStruct(shape, F32)
    bf16 = lambda *shape: jax.ShapeDtypeStruct(shape, BF16)
    fast = dict(compiler_params=LIMIT)
    in_hbm = [
        pltpu.with_memory_space_constraint(x, pltpu.HBM)
        for x in (coupling, spectrum.reshape(1, modes), spatial_basis, keys, counters)
    ]

    pairs, single = partners(space)
    routes = [(d, d) for d in single] + pairs
    sizes = [half + TAIL] * len(single) + [nodes_here + TAIL] * len(pairs)
    other = swap(coupling, "tm", 1)
    *messages, coup, spec, base = kernel_call(
        functools.partial(pack_kernel, "tm", "space", routes),
        out_shape=[bf16(n, modes) for n in sizes]
        + [f32(steps, modes), f32(1, modes), jax.ShapeDtypeStruct((vecs, 128), jnp.int32)],
        in_specs=[HBM] * 5,
        out_specs=[VMEM] * (len(sizes) + 3),
        scratch_shapes=[pltpu.VMEM((1, vecs), jnp.int32)] * 2 + [pltpu.SemaphoreType.DMA((len(sizes) + 4,))],
        **fast,
    )(*in_hbm)
    table, *messages = kernel_call(
        functools.partial(table_kernel, "tm", len(sizes)),
        out_shape=[f32(8, modes)] + [bf16(n, modes) for n in sizes],
        in_specs=[VMEM] * 3 + [ANY] * len(sizes),
        out_specs=[VMEM] + [ANY] * len(sizes),
        scratch_shapes=[pltpu.VMEM((TAIL, modes), BF16), pltpu.SemaphoreType.DMA((len(sizes),))],
        input_output_aliases={3 + i: 1 + i for i in range(len(sizes))},
        **fast,
    )(coup, other, spec, *messages)
    tables = [swap(table, "tm", 2 * e) for e in range(1, chips)]
    direct = [exchange(m, lambda t, s, r=r: (t, s ^ r[t % 2])) for m, r in zip(messages, routes)]

    def noise_of(parts, span, after):
        count = len(parts) * span * vecs * modes
        return kernel_call(
            functools.partial(noise_kernel, "tm", "space", parts, steps, len(after)),
            out_shape=[f32(span, vecs, modes)] * len(parts),
            in_specs=[VMEM] + [ANY] * len(after),
            out_specs=[VMEM] * len(parts),
            cost_estimate=pl.CostEstimate(flops=count * 60, transcendentals=count * 2, bytes_accessed=count * 4),
            **fast,
        )(base, *after)

    span = steps // 2
    alone = [(d, d) for d in single]
    half_of = lambda routes, part, after: noise_of([(r, part * span) for r in routes], span, after)
    (own,) = noise_of([((0, 0), 0)], steps, (table,))
    state, sent, weights, sums = kernel_call(
        functools.partial(offset_kernel, "tm"),
        out_shape=[f32(vecs, modes), bf16(vecs, modes), f32(chips, 8, modes), f32(8, modes)],
        in_specs=[VMEM] * (4 + len(tables)),
        out_specs=[VMEM] * 4,
        scratch_shapes=[pltpu.VMEM((chips, 8, modes), F32)] + [pltpu.VMEM((steps, modes), F32)] * 2,
        **fast,
    )(own, coup, spec, table, *tables)
    total, late = kernel_call(
        functools.partial(combine_kernel, "tm"),
        out_shape=[bf16(vecs // 2, modes), f32(vecs, modes)],
        in_specs=[VMEM] * 3,
        out_specs=[VMEM] * 2,
        **fast,
    )(state, swap(sent, "tm", 1), sums)
    later = [swap(total, "tm", 2 * e) for e in range(1, chips)]
    whole = lambda routes: [(r, n * span) for r in routes for n in range(2)]
    noise = list(noise_of(whole(alone), span, (total,)))
    near_0 = half_of(pairs, 0, (noise[-1],)) if pairs else noise
    mine, sent = kernel_call(
        functools.partial(half_kernel, "tm"),
        out_shape=[f32(vecs // 2, modes), bf16(vecs // 2, modes)],
        in_specs=[VMEM] * (1 + len(later)) + [ANY],
        out_specs=[VMEM] * 2,
        **fast,
    )(weights, *later, near_0[-1])
    theirs = swap(sent, "tm", 1)
    near_1 = half_of(pairs, 1, (sent,)) if pairs else [sent]
    carry = kernel_call(
        functools.partial(carry_kernel, "tm"),
        out_shape=bf16(vecs + 8, modes),
        in_specs=[VMEM] * 4 + [ANY],
        out_specs=VMEM,
        **fast,
    )(mine, theirs, late, sums, near_1[0])
    carries = [swap(carry, "space", d) for d in range(1, space)]
    swapped = [swap(m, "tm", 1) for m in direct]
    if pairs:
        noise += [x for both in zip(near_0, near_1) for x in both]
        noise += noise_of(whole([r[::-1] for r in pairs]), span, (carry,))

    flops = 2 * nodes_here * modes * steps * vecs
    half_cols = steps // 2 * vecs
    result = f32(nodes_here, steps * vecs)
    out = kernel_call(
        functools.partial(own_kernel, "space"),
        out_shape=result,
        in_specs=[VMEM, VMEM, HBM, VMEM, VMEM],
        out_specs=VMEM,
        scratch_shapes=[
            pltpu.VMEM((nodes_here, modes), BF16),
            pltpu.VMEM((2, half_cols, modes), BF16),
            pltpu.VMEM((vecs, modes), F32),
            pltpu.VMEM((2, steps, modes), F32),
            pltpu.SemaphoreType.DMA,
        ],
        cost_estimate=pl.CostEstimate(flops=flops, transcendentals=0, bytes_accessed=4 * steps * vecs * modes),
        **fast,
    )(coup, spec, spatial_basis, own, carry)
    count = space - 1
    return kernel_call(
        functools.partial(final_kernel, "tm", pairs, single),
        out_shape=result,
        in_specs=[VMEM] * (1 + len(direct) + len(swapped) + len(noise) + len(carries)),
        out_specs=HBM,
        scratch_shapes=[
            pltpu.VMEM((len(single), nodes_here, modes), BF16),
            pltpu.VMEM((2, count, half_cols, modes), BF16),
            pltpu.VMEM((count, vecs, modes), F32),
            pltpu.VMEM((count, 2, steps, modes), F32),
            pltpu.VMEM((2, nodes_here, half_cols), F32),
            pltpu.SemaphoreType.DMA((2 * len(single) + 2,)),
        ],
        cost_estimate=pl.CostEstimate(
            flops=flops * count, transcendentals=0, bytes_accessed=4 * steps * vecs * modes * count
        ),
        **fast,
    )(out, *direct, *swapped, *noise, *carries)


def solution(mesh):
    in_specs = (P("space"), P("tm", "space"), P(None, "space"), P(), P())
    out_specs = P("space", "tm")
    return jax.shard_map(local, mesh=mesh, in_specs=in_specs, out_specs=out_specs, check_vma=False)
```

```python
import functools

import jax
import jax.numpy as jnp
from jax import lax
from jax.experimental import pallas as pl
from jax.experimental.pallas import tpu as pltpu
from jax.sharding import PartitionSpec as P


F32 = jnp.float32
BF16 = jnp.bfloat16
VMEM = pl.BlockSpec(memory_space=pltpu.VMEM)
ANY = pl.BlockSpec(memory_space=pl.ANY)
HBM = pl.BlockSpec(memory_space=pltpu.HBM)
LIMIT = pltpu.CompilerParams(vmem_limit_bytes=24 << 20)
SINE = (6.28318516, -41.34165503, 81.60100406, -76.54978208, 39.53670436)


def partners(count):
    pairs = [(i, i + 1) for i in range(1, count - 2, 2)]
    return pairs, ([count - 1] if count > 1 else [])


def exchange(x, move):
    tm, space = lax.axis_size("tm"), lax.axis_size("space")
    moves = []
    for t in range(tm):
        for s in range(space):
            to = move(t, s)
            if to is not None:
                moves.append((t * space + s, to[0] * space + to[1]))
    return lax.ppermute(x, ("tm", "space"), moves)


def swap(x, axis, offset):
    count = lax.axis_size(axis)
    return lax.ppermute(x, axis, [(i, i ^ offset) for i in range(count)])


def split3(x):
    high = x.astype(BF16).astype(F32)
    rest = x - high
    middle = rest.astype(BF16).astype(F32)
    return high, middle, rest - middle


def mix_bits(state):
    state = state ^ lax.shift_right_logical(state, jnp.int32(16))
    state = state * jnp.int32(-2048144789)
    state = state ^ lax.shift_right_logical(state, jnp.int32(13))
    state = state * jnp.int32(-1028477387)
    return state ^ lax.shift_right_logical(state, jnp.int32(16))


def gaussian(seeded):
    first = mix_bits(seeded)
    second = mix_bits(first + jnp.int32(1013904223))
    unit = (lax.shift_right_logical(first, jnp.int32(8)).astype(F32) + 0.5) * (1.0 / 16777216.0)
    square = -2.0 * jnp.log(unit)
    radius = square * lax.rsqrt(jnp.maximum(square, 1e-30))
    turn = (lax.shift_right_arithmetic(second, jnp.int32(8)).astype(F32) + 0.5) * (1.0 / 16777216.0)
    w = 0.25 - jnp.abs(turn)
    z = w * w
    sine = SINE[4]
    for c in SINE[3::-1]:
        sine = sine * z + c
    return radius * (sine * w)


TAIL = 64


def pick(core, offsets):
    return offsets[0] if offsets[0] == offsets[1] else jnp.where(core == 0, offsets[0], offsets[1])


def pack_kernel(tm_axis, sp_axis, offsets, coup, spec, basis, keys, counters, *rest):
    *outs, coup_out, spec_out, base, early, key_row, counter_row, sems = rest
    me, sp = lax.axis_index(tm_axis), lax.axis_index(sp_axis)
    core = lax.rem(me, 2)
    copies = [
        pltpu.make_async_copy(coup, coup_out, sems.at[len(outs)]),
        pltpu.make_async_copy(spec, spec_out, sems.at[len(outs) + 1]),
    ]
    rows_in = [
        pltpu.make_async_copy(keys, key_row, sems.at[len(outs) + 2]),
        pltpu.make_async_copy(counters, counter_row, sems.at[len(outs) + 3]),
    ]
    for i, (out, offset) in enumerate(zip(outs, offsets)):
        rows = out.shape[0] - TAIL
        block = sp ^ pick(core, offset)
        if offset[0] == offset[1]:
            block = block * 2 + core
        start = pl.multiple_of(block * rows, rows)
        copies.append(
            pltpu.make_async_copy(basis.at[pl.ds(start, rows), :], out.at[pl.ds(0, rows), :], sems.at[i])
        )
    for copy in rows_in + copies:
        copy.start()
    for copy in rows_in:
        copy.wait()
    base_columns(key_row, counter_row, base)
    fill_noise(early, base, mode_ids(sp, early.shape[2]), me * coup.shape[0], 0)
    for copy in copies:
        copy.wait()


def totals(ref):
    product = square = total = None
    for t in range(ref.shape[0]):
        c = ref[pl.ds(t, 1), :]
        product = c if t == 0 else product * c
        square = c * c if t == 0 else square * (c * c)
        total = square if t == 0 else total + square
    return product, total


def joined(early, late):
    return early[0] * late[0], early[1] + (early[0] * early[0]) * late[1]


def table_rows(shape, rows):
    row = lax.broadcasted_iota(jnp.int32, shape, 0)
    table = jnp.zeros(shape, F32)
    for j, value in enumerate(rows):
        table = jnp.where(row == j, value, table)
    return table


def ordered(first, mine, theirs):
    early = tuple(jnp.where(first, x, y) for x, y in zip(mine, theirs))
    late = tuple(jnp.where(first, y, x) for x, y in zip(mine, theirs))
    return early, late


def table_kernel(tm_axis, count, coup, other, spec, *rest):
    out, *messages, tail, sems = rest[count:]
    first = lax.rem(lax.axis_index(tm_axis), 2) == 0
    (x,), (y,) = ordered(first, (coup[...],), (other[...],))
    parts = split3(x) + split3(y)
    parts = parts + (table_rows(x.shape, split3(spec[...])), jnp.zeros_like(x))
    for j in range(4):
        tail[pl.ds(16 * j, 16), :] = jnp.concatenate(parts[2 * j : 2 * j + 2], 0).astype(BF16)
    copies = []
    for i, message in enumerate(messages):
        rows = message.shape[0] - TAIL
        copies.append(pltpu.make_async_copy(tail, message.at[pl.ds(rows, TAIL), :], sems.at[i]))
        copies[-1].start()
    early, late = ordered(first, totals(coup), totals(other))
    out[...] = table_rows(out.shape, (*joined(early, late), *early, *late))
    for copy in copies:
        copy.wait()


def base_columns(keys, counters, base):
    vecs = base.shape[0]
    diagonal = lax.broadcasted_iota(jnp.int32, (vecs, vecs), 0) == lax.broadcasted_iota(
        jnp.int32, (vecs, vecs), 1
    )

    def column(ref):
        row = jnp.broadcast_to(ref[...].astype(F32), (vecs, vecs))
        return jnp.sum(jnp.where(diagonal, row, 0.0), axis=1, keepdims=True).astype(jnp.int32)

    start = column(keys) * jnp.int32(668265261) + column(counters) * jnp.int32(374761393)
    base[...] = jnp.broadcast_to(start, base.shape)


def fill_noise(out, base, ids, first_step, begin):
    steps, vecs, modes = out.shape
    lane = ids * jnp.int32(-1640531535)
    group = 8

    def step(t, _):
        shifted = lane + (first_step + t) * jnp.int32(374761393)
        for v in range(vecs // group):
            seeded = jnp.tile(base[pl.ds(v * group, group), :], (1, modes // 128)) + shifted
            out[t, pl.ds(v * group, group), :] = gaussian(seeded)
        return 0

    lax.fori_loop(begin, steps, step, 0)


def mode_ids(block, modes):
    return block * modes + lax.broadcasted_iota(jnp.int32, (1, modes), 1)


def noise_kernel(tm_axis, sp_axis, parts, total_steps, extras, base, *rest):
    outs = rest[extras:]
    me, sp = lax.axis_index(tm_axis), lax.axis_index(sp_axis)
    for out, (offset, begin) in zip(outs, parts):
        ids = mode_ids(sp ^ pick(lax.rem(me, 2), offset), out.shape[2])
        fill_noise(out, base, ids, me * total_steps + begin, 0)


def chip_kernel(tm_axis, sp_axis, base, early, _, out):
    steps, _, modes = out.shape
    made = early.shape[0]
    for t in range(made):
        out[t] = early[t]
    me, sp = lax.axis_index(tm_axis), lax.axis_index(sp_axis)
    fill_noise(out, base, mode_ids(sp, modes), me * steps, made)


def running(x, combine, identity):
    row = lax.broadcasted_iota(jnp.int32, x.shape, 0)
    shift = 1
    while shift < x.shape[0]:
        x = combine(x, jnp.where(row < shift, identity, pltpu.roll(x, shift, 0)))
        shift *= 2
    return x


def chain(c, spec, d_start, f_start):
    total = running(running(c * c, jnp.multiply, 1.0), jnp.add, 0.0)
    behind = d_start + f_start * total
    row = lax.broadcasted_iota(jnp.int32, c.shape, 0)
    ratio = jnp.where(row == 0, d_start, pltpu.roll(behind, 1, 0)) / behind
    return jnp.sqrt(ratio / spec), ratio


def after(start, total):
    return start[0] + start[1] * total[1], start[1] * (total[0] * total[0])


def select(flag, x, y):
    return tuple(jnp.where(flag, p, q) for p, q in zip(x, y))


def gain_of(start, total):
    return total[0] * start[0] / (start[0] + start[1] * total[1])


def offset_kernel(tm_axis, noise, coup, spec, table, *rest):
    received, rest = rest[:-7], rest[-7:]
    o_ref, sent, wts, df, tables, alpha, beta = rest
    steps, vecs, modes = noise.shape
    me = lax.axis_index(tm_axis)
    chip = me // 2
    first = lax.rem(me, 2) == 0
    one = jnp.ones((1, modes), F32)
    tables[chip] = table[...]
    for e, ref in enumerate(received):
        tables[chip ^ (e + 1)] = ref[...]
    now, start, weight = (one, one), (one, one), jnp.zeros((1, modes), F32)
    for b in range(tables.shape[0]):
        wts[b] = jnp.broadcast_to(weight, (8, modes))
        total = tables[b, pl.ds(0, 1), :], tables[b, pl.ds(1, 1), :]
        here = chip == b
        start = select(here, now, start)
        weight = jnp.where(here, 1.0, weight * gain_of(now, total))
        now = after(now, total)
    early = table[pl.ds(2, 1), :], table[pl.ds(3, 1), :]
    late = table[pl.ds(4, 1), :], table[pl.ds(5, 1), :]
    second = after(start, early)
    gain_early, gain_late = gain_of(start, early), gain_of(second, late)
    own = select(first, start, second)
    df[...] = table_rows((8, modes), (*own, gain_early, gain_late))
    c = coup[...]
    a, ratio = chain(c, spec[...], *own)
    alpha[...] = c * a
    beta[...] = c * ratio

    def tile(v, _):
        at = pl.ds(pl.multiple_of(v * 16, 16), 16)
        carry = jnp.zeros((16, modes), F32)
        for t in range(steps - 1, -1, -1):
            carry = alpha[pl.ds(t, 1), :] * noise[t, at, :] + beta[pl.ds(t, 1), :] * carry
        o_ref[at, :] = carry
        sent[at, :] = carry.astype(BF16)
        return 0

    lax.fori_loop(0, vecs // 16, tile, 0)


def combine_kernel(tm_axis, own, other, df, out, late):
    core = lax.rem(lax.axis_index(tm_axis), 2)
    first = core == 0
    half = out.shape[0]
    late[...] = jnp.where(first, other[...].astype(F32), own[...])
    at = pl.ds(pl.multiple_of(core * half, half), half)
    x, y = own[at, :], other[at, :].astype(F32)
    out[...] = (jnp.where(first, x, y) + df[pl.ds(2, 1), :] * jnp.where(first, y, x)).astype(BF16)


def half_kernel(tm_axis, wts, *rest):
    *received, _, out, sent = rest
    chip = lax.axis_index(tm_axis) // 2
    carry = jnp.zeros(out.shape, F32)
    for e, ref in enumerate(received):
        carry = carry + wts[chip ^ (e + 1)][0:1, :] * ref[...].astype(F32)
    out[...] = carry
    sent[...] = carry.astype(BF16)


def carry_kernel(tm_axis, mine, theirs, late, df, _, out):
    half, modes = mine.shape
    core = lax.rem(lax.axis_index(tm_axis), 2)
    gain = df[pl.ds(3, 1), :]
    for j in range(2):
        at = pl.ds(j * half, half)
        carry = jnp.where(core == j, mine[...], theirs[...].astype(F32))
        out[at, :] = jnp.where(core == 0, late[at, :] + gain * carry, carry).astype(BF16)
    parts = split3(df[pl.ds(0, 1), :]) + split3(df[pl.ds(1, 1), :])
    out[pl.ds(2 * half, 8), :] = table_rows((8, modes), parts).astype(BF16)


def sums_of(block):
    return block[0:1] + block[1:2] + block[2:3], block[3:4] + block[4:5] + block[5:6]


def set_coefs(coefs, c, lam, sums):
    a, ratio = chain(c, lam, *sums)
    row = lax.broadcasted_iota(jnp.int32, c.shape, 0)
    steps = c.shape[0]
    coefs[0] = a
    coefs[1] = ratio * jnp.where(row == steps - 1, 1.0, pltpu.roll(c, steps - 1, 0))


def values(noise, start, coefs, state, rhs, times):
    span, vecs, _ = noise[0].shape
    for v in range(0, vecs, 16):
        at = pl.ds(v, 16)
        value = start(at)
        for n, t in enumerate(times):
            row = pl.ds(t, 1)
            value = coefs[0, row, :] * noise[t // span][t % span, at, :] + coefs[1, row, :] * value
            rhs[pl.ds((len(times) - 1 - n) * vecs + v, 16), :] = value.astype(BF16)
        if times[-1]:
            state[at, :] = value


def product(lhs, rhs):
    return lax.dot_general(lhs, rhs, (((1,), (1,)), ((), ())), preferred_element_type=F32)


def halves_of(steps):
    times = list(range(steps - 1, -1, -1))
    return times[: steps // 2], times[steps // 2 :]


def own_kernel(sp_axis, coup, spec, basis, noise, message, out, lhs, rhs, state, coefs, sem):
    rows = lhs.shape[0]
    steps, vecs, _ = noise.shape
    start = pl.multiple_of(lax.axis_index(sp_axis) * rows, rows)
    copy = pltpu.make_async_copy(basis.at[pl.ds(start, rows), :], lhs, sem)
    copy.start()
    set_coefs(coefs, coup[...], spec[...], sums_of(message[pl.ds(vecs, 8), :].astype(F32)))
    late, early = halves_of(steps)
    width = vecs * len(late)
    values((noise,), lambda at: message[at, :].astype(F32), coefs, state, rhs.at[0], late)
    copy.wait()
    values((noise,), lambda at: state[at, :], coefs, state, rhs.at[1], early)
    out[:, pl.ds(width, width)] = product(lhs[...], rhs[0])
    out[:, pl.ds(0, width)] = product(lhs[...], rhs[1])


def final_kernel(tm_axis, pairs, single, partial, *rest):
    fetched = len(pairs) + len(single)
    count = 2 * len(pairs) + len(single)
    direct, rest = rest[:fetched], rest[fetched:]
    swapped, rest = rest[:fetched], rest[fetched:]
    noise, rest = [rest[2 * n : 2 * n + 2] for n in range(count)], rest[2 * count :]
    messages, rest = rest[:count], rest[count:]
    out, lhs, rhs, state, coefs, result, sems = rest
    steps, vecs = 2 * noise[0][0].shape[0], noise[0][0].shape[1]
    core = lax.rem(lax.axis_index(tm_axis), 2)
    first = core == 0
    copies = []
    for i in range(len(single)):
        rows = lhs.shape[1] // 2
        for j, source in enumerate((direct[i], swapped[i])):
            at = pl.multiple_of((core if j == 0 else 1 - core) * rows, rows)
            copies.append(
                pltpu.make_async_copy(
                    source.at[pl.ds(0, rows), :], lhs.at[i, pl.ds(at, rows), :], sems.at[2 * i + j]
                )
            )
            copies[-1].start()

    def chosen(x, y):
        return lambda at: jnp.where(first, messages[x][at, :].astype(F32), messages[y][at, :].astype(F32))

    items = []
    for j, (x, y) in enumerate(pairs):
        i = len(single) + j
        rows = direct[i].shape[0] - TAIL
        near = lambda i=i, rows=rows: direct[i][pl.ds(0, rows), :]
        far = lambda i=i, rows=rows: swapped[i][pl.ds(0, rows), :]
        items.append((near, direct[i], noise[len(single) + j], chosen(x - 1, y - 1)))
        items.append((far, swapped[i], noise[len(single) + len(pairs) + j], chosen(y - 1, x - 1)))
    for i, d in enumerate(single):
        items.append((lambda i=i: lhs[i], direct[i], noise[i], chosen(d - 1, d - 1)))
    for n, (_, source, _, message) in enumerate(items):
        rows = source.shape[0] - TAIL
        x = [source[pl.ds(rows + 16 * j, 16), :].astype(F32) for j in range(4)]
        before = x[0][0:8] + x[0][8:16] + x[1][0:8]
        behind = x[1][8:16] + x[2][0:8] + x[2][8:16]
        lam = x[3][0:1] + x[3][1:2] + x[3][2:3]
        set_coefs(coefs.at[n], jnp.where(first, before, behind), lam, sums_of(message(pl.ds(vecs, 8))))
    late, early = halves_of(steps)
    width = vecs * len(late)
    work = [(h, n) for h in range(2) for n in range(count)]

    def fill(h, n):
        start = items[n][3] if h == 0 else lambda at: state[n, at, :]
        values(items[n][2], start, coefs.at[n], state.at[n], rhs.at[h, n], late if h == 0 else early)

    fill(*work[0])
    outs = []
    for k, (h, n) in enumerate(work):
        if k + 1 < len(work):
            fill(*work[k + 1])
        if h == 0 and n == count - len(single):
            for copy in copies:
                copy.wait()
        term = product(items[n][0](), rhs[h, n])
        at = pl.ds((1 - h) * width, width)
        result[h] = (partial[:, at] if n == 0 else result[h]) + term
        if n == count - 1:
            outs.append(pltpu.make_async_copy(result.at[h], out.at[:, at], sems.at[2 * len(single) + h]))
            outs[-1].start()
    for copy in outs:
        copy.wait()


def kernel_call(body, **options):
    return pl.pallas_call(body, **options)


def local(spectrum, coupling, spatial_basis, noise_keys, noise_counters):
    steps, modes = coupling.shape
    vecs = noise_keys.shape[0]
    tm, space = lax.axis_size("tm"), lax.axis_size("space")
    chips = tm // 2
    nodes_here = spatial_basis.shape[0] // space
    half = nodes_here // 2
    keys, counters = noise_keys.reshape(1, vecs), noise_counters.reshape(1, vecs)
    f32 = lambda *shape: jax.ShapeDtypeStruct(shape, F32)
    bf16 = lambda *shape: jax.ShapeDtypeStruct(shape, BF16)
    fast = dict(compiler_params=LIMIT)
    in_hbm = [
        pltpu.with_memory_space_constraint(x, pltpu.HBM)
        for x in (coupling, spectrum.reshape(1, modes), spatial_basis, keys, counters)
    ]

    pairs, single = partners(space)
    routes = [(d, d) for d in single] + pairs
    sizes = [half + TAIL] * len(single) + [nodes_here + TAIL] * len(pairs)
    other = swap(coupling, "tm", 1)
    *messages, coup, spec, base, early = kernel_call(
        functools.partial(pack_kernel, "tm", "space", routes),
        out_shape=[bf16(n, modes) for n in sizes]
        + [f32(steps, modes), f32(1, modes), jax.ShapeDtypeStruct((vecs, 128), jnp.int32)]
        + [f32(steps // 4, vecs, modes)],
        in_specs=[HBM] * 5,
        out_specs=[VMEM] * (len(sizes) + 4),
        scratch_shapes=[pltpu.VMEM((1, vecs), jnp.int32)] * 2 + [pltpu.SemaphoreType.DMA((len(sizes) + 4,))],
        **fast,
    )(*in_hbm)
    table, *messages = kernel_call(
        functools.partial(table_kernel, "tm", len(sizes)),
        out_shape=[f32(8, modes)] + [bf16(n, modes) for n in sizes],
        in_specs=[VMEM] * 3 + [ANY] * len(sizes),
        out_specs=[VMEM] + [ANY] * len(sizes),
        scratch_shapes=[pltpu.VMEM((TAIL, modes), BF16), pltpu.SemaphoreType.DMA((len(sizes),))],
        input_output_aliases={3 + i: 1 + i for i in range(len(sizes))},
        **fast,
    )(coup, other, spec, *messages)
    tables = [swap(table, "tm", 2 * e) for e in range(1, chips)]
    direct = [exchange(m, lambda t, s, r=r: (t, s ^ r[t % 2])) for m, r in zip(messages, routes)]

    def noise_of(parts, span, after):
        count = len(parts) * span * vecs * modes
        return kernel_call(
            functools.partial(noise_kernel, "tm", "space", parts, steps, len(after)),
            out_shape=[f32(span, vecs, modes)] * len(parts),
            in_specs=[VMEM] + [ANY] * len(after),
            out_specs=[VMEM] * len(parts),
            cost_estimate=pl.CostEstimate(flops=count * 60, transcendentals=count * 2, bytes_accessed=count * 4),
            **fast,
        )(base, *after)

    span = steps // 2
    alone = [(d, d) for d in single]
    half_of = lambda routes, part, after: noise_of([(r, part * span) for r in routes], span, after)
    own = kernel_call(
        functools.partial(chip_kernel, "tm", "space"),
        out_shape=f32(steps, vecs, modes),
        in_specs=[VMEM] * 2 + [ANY],
        out_specs=VMEM,
        **fast,
    )(base, early, table)
    state, sent, weights, sums = kernel_call(
        functools.partial(offset_kernel, "tm"),
        out_shape=[f32(vecs, modes), bf16(vecs, modes), f32(chips, 8, modes), f32(8, modes)],
        in_specs=[VMEM] * (4 + len(tables)),
        out_specs=[VMEM] * 4,
        scratch_shapes=[pltpu.VMEM((chips, 8, modes), F32)] + [pltpu.VMEM((steps, modes), F32)] * 2,
        **fast,
    )(own, coup, spec, table, *tables)
    total, late = kernel_call(
        functools.partial(combine_kernel, "tm"),
        out_shape=[bf16(vecs // 2, modes), f32(vecs, modes)],
        in_specs=[VMEM] * 3,
        out_specs=[VMEM] * 2,
        **fast,
    )(state, swap(sent, "tm", 1), sums)
    later = [swap(total, "tm", 2 * e) for e in range(1, chips)]
    whole = lambda routes: [(r, n * span) for r in routes for n in range(2)]
    noise = list(noise_of(whole(alone), span, (total,)))
    near_0 = half_of(pairs, 0, (noise[-1],)) if pairs else noise
    mine, sent = kernel_call(
        functools.partial(half_kernel, "tm"),
        out_shape=[f32(vecs // 2, modes), bf16(vecs // 2, modes)],
        in_specs=[VMEM] * (1 + len(later)) + [ANY],
        out_specs=[VMEM] * 2,
        **fast,
    )(weights, *later, near_0[-1])
    theirs = swap(sent, "tm", 1)
    near_1 = half_of(pairs, 1, (sent,)) if pairs else [sent]
    carry = kernel_call(
        functools.partial(carry_kernel, "tm"),
        out_shape=bf16(vecs + 8, modes),
        in_specs=[VMEM] * 4 + [ANY],
        out_specs=VMEM,
        **fast,
    )(mine, theirs, late, sums, near_1[0])
    carries = [swap(carry, "space", d) for d in range(1, space)]
    swapped = [swap(m, "tm", 1) for m in direct]
    if pairs:
        noise += [x for both in zip(near_0, near_1) for x in both]
        noise += noise_of(whole([r[::-1] for r in pairs]), span, (carry,))

    flops = 2 * nodes_here * modes * steps * vecs
    half_cols = steps // 2 * vecs
    result = f32(nodes_here, steps * vecs)
    out = kernel_call(
        functools.partial(own_kernel, "space"),
        out_shape=result,
        in_specs=[VMEM, VMEM, HBM, VMEM, VMEM],
        out_specs=VMEM,
        scratch_shapes=[
            pltpu.VMEM((nodes_here, modes), BF16),
            pltpu.VMEM((2, half_cols, modes), BF16),
            pltpu.VMEM((vecs, modes), F32),
            pltpu.VMEM((2, steps, modes), F32),
            pltpu.SemaphoreType.DMA,
        ],
        cost_estimate=pl.CostEstimate(flops=flops, transcendentals=0, bytes_accessed=4 * steps * vecs * modes),
        **fast,
    )(coup, spec, spatial_basis, own, carry)
    count = space - 1
    return kernel_call(
        functools.partial(final_kernel, "tm", pairs, single),
        out_shape=result,
        in_specs=[VMEM] * (1 + len(direct) + len(swapped) + len(noise) + len(carries)),
        out_specs=HBM,
        scratch_shapes=[
            pltpu.VMEM((len(single), nodes_here, modes), BF16),
            pltpu.VMEM((2, count, half_cols, modes), BF16),
            pltpu.VMEM((count, vecs, modes), F32),
            pltpu.VMEM((count, 2, steps, modes), F32),
            pltpu.VMEM((2, nodes_here, half_cols), F32),
            pltpu.SemaphoreType.DMA((2 * len(single) + 2,)),
        ],
        cost_estimate=pl.CostEstimate(
            flops=flops * count, transcendentals=0, bytes_accessed=4 * steps * vecs * modes * count
        ),
        **fast,
    )(out, *direct, *swapped, *noise, *carries)


def solution(mesh):
    in_specs = (P("space"), P("tm", "space"), P(None, "space"), P(), P())
    out_specs = P("space", "tm")
    return jax.shard_map(local, mesh=mesh, in_specs=in_specs, out_specs=out_specs, check_vma=False)
```

```python
import functools

import jax
import jax.numpy as jnp
from jax import lax
from jax.experimental import pallas as pl
from jax.experimental.pallas import tpu as pltpu
from jax.sharding import PartitionSpec as P


F32 = jnp.float32
BF16 = jnp.bfloat16
VMEM = pl.BlockSpec(memory_space=pltpu.VMEM)
ANY = pl.BlockSpec(memory_space=pl.ANY)
HBM = pl.BlockSpec(memory_space=pltpu.HBM)
LIMIT = pltpu.CompilerParams(vmem_limit_bytes=24 << 20)
SINE = (6.28318516, -41.34165503, 81.60100406, -76.54978208, 39.53670436)


def partners(count):
    pairs = [(i, i + 1) for i in range(1, count - 2, 2)]
    return pairs, ([count - 1] if count > 1 else [])


def exchange(x, move):
    tm, space = lax.axis_size("tm"), lax.axis_size("space")
    moves = []
    for t in range(tm):
        for s in range(space):
            to = move(t, s)
            if to is not None:
                moves.append((t * space + s, to[0] * space + to[1]))
    return lax.ppermute(x, ("tm", "space"), moves)


def swap(x, axis, offset):
    count = lax.axis_size(axis)
    return lax.ppermute(x, axis, [(i, i ^ offset) for i in range(count)])


def split3(x):
    high = x.astype(BF16).astype(F32)
    rest = x - high
    middle = rest.astype(BF16).astype(F32)
    return high, middle, rest - middle


def mix_bits(state):
    state = state ^ lax.shift_right_logical(state, jnp.int32(16))
    state = state * jnp.int32(-2048144789)
    state = state ^ lax.shift_right_logical(state, jnp.int32(13))
    state = state * jnp.int32(-1028477387)
    return state ^ lax.shift_right_logical(state, jnp.int32(16))


def gaussian(seeded):
    first = mix_bits(seeded)
    second = mix_bits(first + jnp.int32(1013904223))
    unit = (lax.shift_right_logical(first, jnp.int32(8)).astype(F32) + 0.5) * (1.0 / 16777216.0)
    square = -2.0 * jnp.log(unit)
    radius = square * lax.rsqrt(jnp.maximum(square, 1e-30))
    turn = (lax.shift_right_arithmetic(second, jnp.int32(8)).astype(F32) + 0.5) * (1.0 / 16777216.0)
    w = 0.25 - jnp.abs(turn)
    z = w * w
    sine = SINE[4]
    for c in SINE[3::-1]:
        sine = sine * z + c
    return radius * (sine * w)


TAIL = 64


def pick(core, offsets):
    return offsets[0] if offsets[0] == offsets[1] else jnp.where(core == 0, offsets[0], offsets[1])


def pack_kernel(tm_axis, sp_axis, offsets, coup, spec, basis, keys, counters, *rest):
    *outs, coup_out, spec_out, base, early, key_row, counter_row, sems = rest
    me, sp = lax.axis_index(tm_axis), lax.axis_index(sp_axis)
    core = lax.rem(me, 2)
    copies = [
        pltpu.make_async_copy(coup, coup_out, sems.at[len(outs)]),
        pltpu.make_async_copy(spec, spec_out, sems.at[len(outs) + 1]),
    ]
    rows_in = [
        pltpu.make_async_copy(keys, key_row, sems.at[len(outs) + 2]),
        pltpu.make_async_copy(counters, counter_row, sems.at[len(outs) + 3]),
    ]
    for i, (out, offset) in enumerate(zip(outs, offsets)):
        rows = out.shape[0] - TAIL
        block = sp ^ pick(core, offset)
        if offset[0] == offset[1]:
            block = block * 2 + core
        start = pl.multiple_of(block * rows, rows)
        copies.append(
            pltpu.make_async_copy(basis.at[pl.ds(start, rows), :], out.at[pl.ds(0, rows), :], sems.at[i])
        )
    for copy in rows_in + copies:
        copy.start()
    for copy in rows_in:
        copy.wait()
    base_columns(key_row, counter_row, base)
    fill_noise(early, base, mode_ids(sp, early.shape[2]), me * coup.shape[0], 0)
    for copy in copies:
        copy.wait()


def totals(ref):
    product = square = total = None
    for t in range(ref.shape[0]):
        c = ref[pl.ds(t, 1), :]
        product = c if t == 0 else product * c
        square = c * c if t == 0 else square * (c * c)
        total = square if t == 0 else total + square
    return product, total


def joined(early, late):
    return early[0] * late[0], early[1] + (early[0] * early[0]) * late[1]


def table_rows(shape, rows):
    row = lax.broadcasted_iota(jnp.int32, shape, 0)
    table = jnp.zeros(shape, F32)
    for j, value in enumerate(rows):
        table = jnp.where(row == j, value, table)
    return table


def ordered(first, mine, theirs):
    early = tuple(jnp.where(first, x, y) for x, y in zip(mine, theirs))
    late = tuple(jnp.where(first, y, x) for x, y in zip(mine, theirs))
    return early, late


def table_kernel(tm_axis, count, coup, other, spec, *rest):
    out, *messages, tail, sems = rest[count:]
    first = lax.rem(lax.axis_index(tm_axis), 2) == 0
    (x,), (y,) = ordered(first, (coup[...],), (other[...],))
    parts = split3(x) + split3(y)
    parts = parts + (table_rows(x.shape, split3(spec[...])), jnp.zeros_like(x))
    for j in range(4):
        tail[pl.ds(16 * j, 16), :] = jnp.concatenate(parts[2 * j : 2 * j + 2], 0).astype(BF16)
    copies = []
    for i, message in enumerate(messages):
        rows = message.shape[0] - TAIL
        copies.append(pltpu.make_async_copy(tail, message.at[pl.ds(rows, TAIL), :], sems.at[i]))
        copies[-1].start()
    early, late = ordered(first, totals(coup), totals(other))
    out[...] = table_rows(out.shape, (*joined(early, late), *early, *late))
    for copy in copies:
        copy.wait()


def base_columns(keys, counters, base):
    vecs = base.shape[0]
    diagonal = lax.broadcasted_iota(jnp.int32, (vecs, vecs), 0) == lax.broadcasted_iota(
        jnp.int32, (vecs, vecs), 1
    )

    def column(ref):
        row = jnp.broadcast_to(ref[...].astype(F32), (vecs, vecs))
        return jnp.sum(jnp.where(diagonal, row, 0.0), axis=1, keepdims=True).astype(jnp.int32)

    start = column(keys) * jnp.int32(668265261) + column(counters) * jnp.int32(374761393)
    base[...] = jnp.broadcast_to(start, base.shape)


def fill_noise(out, base, ids, first_step, begin):
    steps, vecs, modes = out.shape
    lane = ids * jnp.int32(-1640531535)
    group = 8

    def step(t, _):
        shifted = lane + (first_step + t) * jnp.int32(374761393)
        for v in range(vecs // group):
            seeded = jnp.tile(base[pl.ds(v * group, group), :], (1, modes // 128)) + shifted
            out[t, pl.ds(v * group, group), :] = gaussian(seeded)
        return 0

    lax.fori_loop(begin, steps, step, 0)


def mode_ids(block, modes):
    return block * modes + lax.broadcasted_iota(jnp.int32, (1, modes), 1)


def noise_kernel(tm_axis, sp_axis, parts, total_steps, extras, base, *rest):
    outs = rest[extras:]
    me, sp = lax.axis_index(tm_axis), lax.axis_index(sp_axis)
    for out, (offset, begin) in zip(outs, parts):
        ids = mode_ids(sp ^ pick(lax.rem(me, 2), offset), out.shape[2])
        fill_noise(out, base, ids, me * total_steps + begin, 0)


def chip_kernel(tm_axis, sp_axis, base, early, _, out):
    steps, _, modes = out.shape
    made = early.shape[0]
    for t in range(made):
        out[t] = early[t]
    me, sp = lax.axis_index(tm_axis), lax.axis_index(sp_axis)
    fill_noise(out, base, mode_ids(sp, modes), me * steps, made)


def running(x, combine, identity):
    row = lax.broadcasted_iota(jnp.int32, x.shape, 0)
    shift = 1
    while shift < x.shape[0]:
        x = combine(x, jnp.where(row < shift, identity, pltpu.roll(x, shift, 0)))
        shift *= 2
    return x


def chain(c, spec, d_start, f_start):
    total = running(running(c * c, jnp.multiply, 1.0), jnp.add, 0.0)
    behind = d_start + f_start * total
    row = lax.broadcasted_iota(jnp.int32, c.shape, 0)
    ratio = jnp.where(row == 0, d_start, pltpu.roll(behind, 1, 0)) / behind
    return jnp.sqrt(ratio / spec), ratio


def after(start, total):
    return start[0] + start[1] * total[1], start[1] * (total[0] * total[0])


def select(flag, x, y):
    return tuple(jnp.where(flag, p, q) for p, q in zip(x, y))


def gain_of(start, total):
    return total[0] * start[0] / (start[0] + start[1] * total[1])


def offset_kernel(tm_axis, noise, coup, spec, table, *rest):
    received, rest = rest[:-7], rest[-7:]
    o_ref, sent, wts, df, tables, alpha, beta = rest
    steps, vecs, modes = noise.shape
    me = lax.axis_index(tm_axis)
    chip = me // 2
    first = lax.rem(me, 2) == 0
    one = jnp.ones((1, modes), F32)
    tables[chip] = table[...]
    for e, ref in enumerate(received):
        tables[chip ^ (e + 1)] = ref[...]
    now, start, weight = (one, one), (one, one), jnp.zeros((1, modes), F32)
    for b in range(tables.shape[0]):
        wts[b] = jnp.broadcast_to(weight, (8, modes))
        total = tables[b, pl.ds(0, 1), :], tables[b, pl.ds(1, 1), :]
        here = chip == b
        start = select(here, now, start)
        weight = jnp.where(here, 1.0, weight * gain_of(now, total))
        now = after(now, total)
    early = table[pl.ds(2, 1), :], table[pl.ds(3, 1), :]
    late = table[pl.ds(4, 1), :], table[pl.ds(5, 1), :]
    second = after(start, early)
    gain_early, gain_late = gain_of(start, early), gain_of(second, late)
    own = select(first, start, second)
    df[...] = table_rows((8, modes), (*own, gain_early, gain_late))
    c = coup[...]
    a, ratio = chain(c, spec[...], *own)
    alpha[...] = c * a
    beta[...] = c * ratio

    def tile(v, _):
        at = pl.ds(pl.multiple_of(v * 16, 16), 16)
        carry = jnp.zeros((16, modes), F32)
        for t in range(steps - 1, -1, -1):
            carry = alpha[pl.ds(t, 1), :] * noise[t, at, :] + beta[pl.ds(t, 1), :] * carry
        o_ref[at, :] = carry
        sent[at, :] = carry.astype(BF16)
        return 0

    lax.fori_loop(0, vecs // 16, tile, 0)


def combine_kernel(tm_axis, own, other, df, out, late):
    core = lax.rem(lax.axis_index(tm_axis), 2)
    first = core == 0
    half = out.shape[0]
    late[...] = jnp.where(first, other[...].astype(F32), own[...])
    at = pl.ds(pl.multiple_of(core * half, half), half)
    x, y = own[at, :], other[at, :].astype(F32)
    out[...] = (jnp.where(first, x, y) + df[pl.ds(2, 1), :] * jnp.where(first, y, x)).astype(BF16)


def half_kernel(tm_axis, wts, *rest):
    *received, _, out, sent = rest
    chip = lax.axis_index(tm_axis) // 2
    carry = jnp.zeros(out.shape, F32)
    for e, ref in enumerate(received):
        carry = carry + wts[chip ^ (e + 1)][0:1, :] * ref[...].astype(F32)
    out[...] = carry
    sent[...] = carry.astype(BF16)


def carry_kernel(tm_axis, mine, theirs, late, df, _, out):
    half, modes = mine.shape
    core = lax.rem(lax.axis_index(tm_axis), 2)
    gain = df[pl.ds(3, 1), :]
    for j in range(2):
        at = pl.ds(j * half, half)
        carry = jnp.where(core == j, mine[...], theirs[...].astype(F32))
        out[at, :] = jnp.where(core == 0, late[at, :] + gain * carry, carry).astype(BF16)
    parts = split3(df[pl.ds(0, 1), :]) + split3(df[pl.ds(1, 1), :])
    out[pl.ds(2 * half, 8), :] = table_rows((8, modes), parts).astype(BF16)


def sums_of(block):
    return block[0:1] + block[1:2] + block[2:3], block[3:4] + block[4:5] + block[5:6]


def set_coefs(coefs, c, lam, sums):
    a, ratio = chain(c, lam, *sums)
    row = lax.broadcasted_iota(jnp.int32, c.shape, 0)
    steps = c.shape[0]
    coefs[0] = a
    coefs[1] = ratio * jnp.where(row == steps - 1, 1.0, pltpu.roll(c, steps - 1, 0))


def values(noise, start, coefs, state, rhs, times):
    span, vecs, _ = noise[0].shape
    for v in range(0, vecs, 16):
        at = pl.ds(v, 16)
        value = start(at)
        for n, t in enumerate(times):
            row = pl.ds(t, 1)
            value = coefs[0, row, :] * noise[t // span][t % span, at, :] + coefs[1, row, :] * value
            rhs[pl.ds((len(times) - 1 - n) * vecs + v, 16), :] = value.astype(BF16)
        if times[-1]:
            state[at, :] = value


def product(lhs, rhs):
    return lax.dot_general(lhs, rhs, (((1,), (1,)), ((), ())), preferred_element_type=F32)


def halves_of(steps):
    times = list(range(steps - 1, -1, -1))
    return times[: steps // 2], times[steps // 2 :]


def own_kernel(sp_axis, coup, spec, basis, noise, message, out, lhs, rhs, state, coefs, sem):
    rows = lhs.shape[0]
    steps, vecs, _ = noise.shape
    start = pl.multiple_of(lax.axis_index(sp_axis) * rows, rows)
    copy = pltpu.make_async_copy(basis.at[pl.ds(start, rows), :], lhs, sem)
    copy.start()
    set_coefs(coefs, coup[...], spec[...], sums_of(message[pl.ds(vecs, 8), :].astype(F32)))
    late, early = halves_of(steps)
    width = vecs * len(late)
    values((noise,), lambda at: message[at, :].astype(F32), coefs, state, rhs.at[0], late)
    copy.wait()
    values((noise,), lambda at: state[at, :], coefs, state, rhs.at[1], early)
    out[:, pl.ds(width, width)] = product(lhs[...], rhs[0])
    out[:, pl.ds(0, width)] = product(lhs[...], rhs[1])


def final_kernel(tm_axis, pairs, single, partial, *rest):
    fetched = len(pairs) + len(single)
    count = 2 * len(pairs) + len(single)
    direct, rest = rest[:fetched], rest[fetched:]
    swapped, rest = rest[:fetched], rest[fetched:]
    noise, rest = [rest[2 * n : 2 * n + 2] for n in range(count)], rest[2 * count :]
    messages, rest = rest[:count], rest[count:]
    out, lhs, rhs, state, coefs, result, sems = rest
    steps, vecs = 2 * noise[0][0].shape[0], noise[0][0].shape[1]
    core = lax.rem(lax.axis_index(tm_axis), 2)
    first = core == 0
    copies = []
    for i in range(len(single)):
        rows = lhs.shape[1] // 2
        for j, source in enumerate((direct[i], swapped[i])):
            at = pl.multiple_of((core if j == 0 else 1 - core) * rows, rows)
            copies.append(
                pltpu.make_async_copy(
                    source.at[pl.ds(0, rows), :], lhs.at[i, pl.ds(at, rows), :], sems.at[2 * i + j]
                )
            )
            copies[-1].start()

    def chosen(x, y):
        return lambda at: jnp.where(first, messages[x][at, :].astype(F32), messages[y][at, :].astype(F32))

    items = []
    for j, (x, y) in enumerate(pairs):
        i = len(single) + j
        rows = direct[i].shape[0] - TAIL
        near = lambda at=pl.ds(0, rows), i=i: direct[i][at, :]
        far = lambda at=pl.ds(0, rows), i=i: swapped[i][at, :]
        items.append((near, direct[i], noise[len(single) + j], chosen(x - 1, y - 1)))
        items.append((far, swapped[i], noise[len(single) + len(pairs) + j], chosen(y - 1, x - 1)))
    for i, d in enumerate(single):
        items.append((lambda at=slice(None), i=i: lhs[i, at, :], direct[i], noise[i], chosen(d - 1, d - 1)))
    for n, (_, source, _, message) in enumerate(items):
        rows = source.shape[0] - TAIL
        x = [source[pl.ds(rows + 16 * j, 16), :].astype(F32) for j in range(4)]
        before = x[0][0:8] + x[0][8:16] + x[1][0:8]
        behind = x[1][8:16] + x[2][0:8] + x[2][8:16]
        lam = x[3][0:1] + x[3][1:2] + x[3][2:3]
        set_coefs(coefs.at[n], jnp.where(first, before, behind), lam, sums_of(message(pl.ds(vecs, 8))))
    late, early = halves_of(steps)
    width = vecs * len(late)
    work = [(h, n) for h in range(2) for n in range(count)]

    def fill(h, n):
        start = items[n][3] if h == 0 else lambda at: state[n, at, :]
        values(items[n][2], start, coefs.at[n], state.at[n], rhs.at[h, n], late if h == 0 else early)

    fill(*work[0])
    outs = []
    for k, (h, n) in enumerate(work):
        if k + 1 < len(work):
            fill(*work[k + 1])
        if h == 0 and n == count - len(single):
            for copy in copies:
                copy.wait()
        at = pl.ds((1 - h) * width, width)
        rows = result.shape[1]
        ends = n == count - 1 and h == 1
        for part in range(2 if ends else 1):
            take = pl.ds(part * (rows // 2), rows // 2) if ends else pl.ds(0, rows)
            term = product(items[n][0](take), rhs[h, n])
            result[h, take, :] = (partial[take, at] if n == 0 else result[h, take, :]) + term
            if n == count - 1:
                slot = 2 * len(single) + h + part
                outs.append(pltpu.make_async_copy(result.at[h, take, :], out.at[take, at], sems.at[slot]))
                outs[-1].start()
    for copy in outs:
        copy.wait()


def kernel_call(body, **options):
    return pl.pallas_call(body, **options)


def local(spectrum, coupling, spatial_basis, noise_keys, noise_counters):
    steps, modes = coupling.shape
    vecs = noise_keys.shape[0]
    tm, space = lax.axis_size("tm"), lax.axis_size("space")
    chips = tm // 2
    nodes_here = spatial_basis.shape[0] // space
    half = nodes_here // 2
    keys, counters = noise_keys.reshape(1, vecs), noise_counters.reshape(1, vecs)
    f32 = lambda *shape: jax.ShapeDtypeStruct(shape, F32)
    bf16 = lambda *shape: jax.ShapeDtypeStruct(shape, BF16)
    fast = dict(compiler_params=LIMIT)
    in_hbm = [
        pltpu.with_memory_space_constraint(x, pltpu.HBM)
        for x in (coupling, spectrum.reshape(1, modes), spatial_basis, keys, counters)
    ]

    pairs, single = partners(space)
    routes = [(d, d) for d in single] + pairs
    sizes = [half + TAIL] * len(single) + [nodes_here + TAIL] * len(pairs)
    other = swap(coupling, "tm", 1)
    *messages, coup, spec, base, early = kernel_call(
        functools.partial(pack_kernel, "tm", "space", routes),
        out_shape=[bf16(n, modes) for n in sizes]
        + [f32(steps, modes), f32(1, modes), jax.ShapeDtypeStruct((vecs, 128), jnp.int32)]
        + [f32(steps // 4, vecs, modes)],
        in_specs=[HBM] * 5,
        out_specs=[VMEM] * (len(sizes) + 4),
        scratch_shapes=[pltpu.VMEM((1, vecs), jnp.int32)] * 2 + [pltpu.SemaphoreType.DMA((len(sizes) + 4,))],
        **fast,
    )(*in_hbm)
    table, *messages = kernel_call(
        functools.partial(table_kernel, "tm", len(sizes)),
        out_shape=[f32(8, modes)] + [bf16(n, modes) for n in sizes],
        in_specs=[VMEM] * 3 + [ANY] * len(sizes),
        out_specs=[VMEM] + [ANY] * len(sizes),
        scratch_shapes=[pltpu.VMEM((TAIL, modes), BF16), pltpu.SemaphoreType.DMA((len(sizes),))],
        input_output_aliases={3 + i: 1 + i for i in range(len(sizes))},
        **fast,
    )(coup, other, spec, *messages)
    tables = [swap(table, "tm", 2 * e) for e in range(1, chips)]
    direct = [exchange(m, lambda t, s, r=r: (t, s ^ r[t % 2])) for m, r in zip(messages, routes)]

    def noise_of(parts, span, after):
        count = len(parts) * span * vecs * modes
        return kernel_call(
            functools.partial(noise_kernel, "tm", "space", parts, steps, len(after)),
            out_shape=[f32(span, vecs, modes)] * len(parts),
            in_specs=[VMEM] + [ANY] * len(after),
            out_specs=[VMEM] * len(parts),
            cost_estimate=pl.CostEstimate(flops=count * 60, transcendentals=count * 2, bytes_accessed=count * 4),
            **fast,
        )(base, *after)

    span = steps // 2
    alone = [(d, d) for d in single]
    half_of = lambda routes, part, after: noise_of([(r, part * span) for r in routes], span, after)
    own = kernel_call(
        functools.partial(chip_kernel, "tm", "space"),
        out_shape=f32(steps, vecs, modes),
        in_specs=[VMEM] * 2 + [ANY],
        out_specs=VMEM,
        **fast,
    )(base, early, table)
    state, sent, weights, sums = kernel_call(
        functools.partial(offset_kernel, "tm"),
        out_shape=[f32(vecs, modes), bf16(vecs, modes), f32(chips, 8, modes), f32(8, modes)],
        in_specs=[VMEM] * (4 + len(tables)),
        out_specs=[VMEM] * 4,
        scratch_shapes=[pltpu.VMEM((chips, 8, modes), F32)] + [pltpu.VMEM((steps, modes), F32)] * 2,
        **fast,
    )(own, coup, spec, table, *tables)
    total, late = kernel_call(
        functools.partial(combine_kernel, "tm"),
        out_shape=[bf16(vecs // 2, modes), f32(vecs, modes)],
        in_specs=[VMEM] * 3,
        out_specs=[VMEM] * 2,
        **fast,
    )(state, swap(sent, "tm", 1), sums)
    later = [swap(total, "tm", 2 * e) for e in range(1, chips)]
    whole = lambda routes: [(r, n * span) for r in routes for n in range(2)]
    noise = list(noise_of(whole(alone), span, (total,)))
    near_0 = half_of(pairs, 0, (noise[-1],)) if pairs else noise
    mine, sent = kernel_call(
        functools.partial(half_kernel, "tm"),
        out_shape=[f32(vecs // 2, modes), bf16(vecs // 2, modes)],
        in_specs=[VMEM] * (1 + len(later)) + [ANY],
        out_specs=[VMEM] * 2,
        **fast,
    )(weights, *later, near_0[-1])
    theirs = swap(sent, "tm", 1)
    near_1 = half_of(pairs, 1, (sent,)) if pairs else [sent]
    carry = kernel_call(
        functools.partial(carry_kernel, "tm"),
        out_shape=bf16(vecs + 8, modes),
        in_specs=[VMEM] * 4 + [ANY],
        out_specs=VMEM,
        **fast,
    )(mine, theirs, late, sums, near_1[0])
    carries = [swap(carry, "space", d) for d in range(1, space)]
    swapped = [swap(m, "tm", 1) for m in direct]
    if pairs:
        noise += [x for both in zip(near_0, near_1) for x in both]
        noise += noise_of(whole([r[::-1] for r in pairs]), span, (carry,))

    flops = 2 * nodes_here * modes * steps * vecs
    half_cols = steps // 2 * vecs
    result = f32(nodes_here, steps * vecs)
    out = kernel_call(
        functools.partial(own_kernel, "space"),
        out_shape=result,
        in_specs=[VMEM, VMEM, HBM, VMEM, VMEM],
        out_specs=VMEM,
        scratch_shapes=[
            pltpu.VMEM((nodes_here, modes), BF16),
            pltpu.VMEM((2, half_cols, modes), BF16),
            pltpu.VMEM((vecs, modes), F32),
            pltpu.VMEM((2, steps, modes), F32),
            pltpu.SemaphoreType.DMA,
        ],
        cost_estimate=pl.CostEstimate(flops=flops, transcendentals=0, bytes_accessed=4 * steps * vecs * modes),
        **fast,
    )(coup, spec, spatial_basis, own, carry)
    count = space - 1
    return kernel_call(
        functools.partial(final_kernel, "tm", pairs, single),
        out_shape=result,
        in_specs=[VMEM] * (1 + len(direct) + len(swapped) + len(noise) + len(carries)),
        out_specs=HBM,
        scratch_shapes=[
            pltpu.VMEM((len(single), nodes_here, modes), BF16),
            pltpu.VMEM((2, count, half_cols, modes), BF16),
            pltpu.VMEM((count, vecs, modes), F32),
            pltpu.VMEM((count, 2, steps, modes), F32),
            pltpu.VMEM((2, nodes_here, half_cols), F32),
            pltpu.SemaphoreType.DMA((2 * len(single) + 3,)),
        ],
        cost_estimate=pl.CostEstimate(
            flops=flops * count, transcendentals=0, bytes_accessed=4 * steps * vecs * modes * count
        ),
        **fast,
    )(out, *direct, *swapped, *noise, *carries)


def solution(mesh):
    in_specs = (P("space"), P("tm", "space"), P(None, "space"), P(), P())
    out_specs = P("space", "tm")
    return jax.shard_map(local, mesh=mesh, in_specs=in_specs, out_specs=out_specs, check_vma=False)
```
